32 devices in a mesh: dp: 8 (over z, y), row: 4 (over x, core).
Axes of the slice: x: 2, y: 2, z: 4, core: 2. Of those that a mesh axis runs over, the one named last changes fastest.
Arguments:
- images: bfloat16 [16, 24, 24, 1024], P('dp', 'row'), may hold values from -6 to 6
- first_weight: bfloat16 [1024, 1024], P(('dp', 'row')), may hold values from -0.1875 to 0.1875
- conv_weight: bfloat16 [3, 3, 1024, 1024], P(None, None, ('dp', 'row')), may hold values from -0.0625 to 0.0625
- last_weight: bfloat16 [1024, 1024], P(('dp', 'row')), may hold values from -0.1875 to 0.1875
- norm_rows: bfloat16 [6, 1024], P(None, ('dp', 'row')), may hold values from -2 to 2, as said below
- read_weight: bfloat16 [1024, 4096], P(None, ('dp', 'row')), may hold values from -0.1875 to 0.1875
- read_bias: bfloat16 [4096], P(('dp', 'row')), may hold values from -3 to 3
- cotangent: bfloat16 [16, 12, 12, 4096], P('dp', 'row'), may hold values from -6 to 6
- live_count: int32 [8], P('dp'), may hold values from 1 to 2, as said below
Outputs:
- readout_out: bfloat16 [16, 12, 12, 4096], P('dp', 'row')
- image_grad: bfloat16 [16, 24, 24, 1024], P('dp', 'row')
- first_grad: float32 [1024, 1024], P(('dp', 'row'))
- conv_grad: float32 [3, 3, 1024, 1024], P(None, None, ('dp', 'row'))
- last_grad: float32 [1024, 1024], P(('dp', 'row'))
- norm_grad: float32 [6, 1024], P(None, ('dp', 'row'))
- read_grad: float32 [1024, 4096], P(None, ('dp', 'row'))
- bias_grad: float32 [4096], P(('dp', 'row'))
The draws below stay inside these ranges and needn't reach their ends.
Inputs may be any that keep to these rules, and one draw needn't show every extreme that they name: The first live_count[g] of the 2 slots of dp group g hold images; in every draw some group has all 2 live and some group one. `norm_rows`: rows 0, 2, 4 lie in 0.5 to 1.5.
All inputs are finite; a program needn't handle non-finite values.
Results may differ from the reference program's by a relative error of at most 0.012.
Values may be sent and summed in bfloat16 or wider, within the bound.
No kernel may reach another device: no remote copies, remote signals or barrier semaphores. Data moves between devices by JAX's collectives and lax.ppermute only.
A program may use at most 192 MiB of HBM per device.

```python
import jax
import jax.numpy as jnp
from jax import lax

C = 1024
OUT = 4096
H = 24
W = 24
SLOTS = 2
IMAGES = 16
N_DP = 8


def draw_norm_rows(key, part):
    gains = jax.random.uniform(key, (3, C), jnp.float32, 0.5, 1.5)
    shifts = 0.5 * jnp.clip(jax.random.normal(jax.random.fold_in(key, 7), (3, C), jnp.float32), -4.0, 4.0)
    return jnp.stack([gains, shifts], axis=1).reshape(6, C).astype(jnp.bfloat16)


def draw_live_count(key, part):
    counts = jax.random.randint(key, (N_DP,), 1, SLOTS + 1)
    order = jax.random.permutation(jax.random.fold_in(key, 11), N_DP)
    counts = counts.at[order[0]].set(SLOTS)
    counts = counts.at[order[1]].set(1)
    return counts.astype(jnp.int32)


def raised(values, own_key, source, target, parts, factor):
    owner, partner = [(jnp.arange(values.shape[dim]) // (values.shape[dim] // parts)).reshape([-1 if axis == dim else 1 for axis in range(values.ndim)]) for dim in (source, target)]
    chosen = jax.random.permutation(own_key, parts)[partner]
    strong = (owner == chosen) | (owner == (partner + parts // 2) % parts)
    return jnp.where(strong, factor * values, values)


def shard_levels(rng, dims, pieces, smallest, largest):
    level = 1.0
    for axis_at, blocks in pieces:
        heights = jax.random.uniform(jax.random.fold_in(jax.random.fold_in(rng, 6), axis_at), (blocks,), jnp.float32, smallest / len(pieces), largest / len(pieces))
        level = level * jnp.repeat(jnp.exp(heights), dims[axis_at] // blocks).reshape((-1,) + (1,) * (len(dims) - 1 - axis_at))
    return level


def bell_draw(rng, extent, deviation, reach, pieces=(), held_as=jnp.bfloat16):
    entries = jax.random.normal(rng, extent, jnp.float32) * deviation
    if len(pieces) > 0:
        entries = shard_levels(rng, extent, pieces, -0.22, 0.18) * entries
    return jnp.clip(entries, min=-reach, max=reach).astype(held_as)


def noise_with(rng, shape, scale, reach, cuts, heavy, kind=jnp.bfloat16):
    array = scale * jax.random.normal(rng, shape, jnp.float32)
    if cuts:
        array = array * shard_levels(rng, shape, cuts, -0.22, 0.18)
    return jnp.clip(raised(array, jax.random.fold_in(rng, 3), *heavy), -reach, reach).astype(kind)


def setup_inputs(seed: int = 0) -> dict:
    key_of = jax.random.split(jax.random.key(seed), 10)
    return {
        "images": noise_with(key_of[0], (IMAGES, H, W, C), 1.0, 6.0, ((0, 8), (1, 4)), (0, 3, 8, 2.0)),
        "first_weight": bell_draw(key_of[1], (C, C), C ** -0.5, 0.1875, ((0, 32),)),
        "conv_weight": bell_draw(key_of[2], (3, 3, C, C), (9 * C) ** -0.5, 0.0625, ((2, 32),)),
        "last_weight": bell_draw(key_of[3], (C, C), C ** -0.5, 0.1875, ((0, 32),)),
        "norm_rows": draw_norm_rows(jax.random.fold_in(key_of[9], 71), 0),
        "read_weight": bell_draw(key_of[5], (C, OUT), C ** -0.5, 0.1875, ((1, 32),)),
        "read_bias": bell_draw(key_of[6], (OUT,), 0.5, 3.0, ((0, 32),)),
        "cotangent": noise_with(key_of[7], (IMAGES, H // 2, W // 2, OUT), 1.0, 6.0, ((0, 8), (1, 4)), (0, 3, 8, 2.0)),
        "live_count": draw_live_count(jax.random.fold_in(key_of[9], 71), 0),
    }


@jax.custom_vjp
def low(v):
    return lax.optimization_barrier(v.astype(jnp.bfloat16)).astype(jnp.float32)

@jax.custom_vjp
def low_back(v):
    return v

def low_keep(v):
    return (low(v), None)

def low_pass(kept, grad):
    return (grad,)

def back_keep(v):
    return (v, None)

def back_low(kept, grad):
    return (low(grad),)
low.defvjp(low_keep, low_pass)
low_back.defvjp(back_keep, back_low)

def layer_norm(value, gain, shift):
    centred = value - lax.optimization_barrier(jnp.mean(value, axis=-1, keepdims=True))
    scale = lax.rsqrt(lax.optimization_barrier(jnp.mean(centred * centred, axis=-1, keepdims=True)) + 1e-06)
    return centred * scale * gain + shift

def project(value, weight):
    return jnp.einsum('sabc,cd->sabd', value, weight, precision=lax.Precision.HIGHEST)

def forward(inputs, first_weight, conv_weight, last_weight, norm_rows, read_weight, read_bias, mask):
    act_one = low_back(project(inputs, first_weight))
    low_one = low(jax.nn.silu(layer_norm(act_one, norm_rows[0], norm_rows[1])))
    rows = low_one.shape[1]
    cols = low_one.shape[2]
    padded = jnp.pad(low_one, ((0, 0), (1, 1), (1, 1), (0, 0)))
    act_two = jnp.zeros_like(low_one)
    for row_tap in range(3):
        for col_tap in range(3):
            act_two = act_two + project(padded[:, row_tap:row_tap + rows, col_tap:col_tap + cols], conv_weight[row_tap, col_tap])
    act_two = low_back(act_two)
    low_two = low(jax.nn.silu(layer_norm(act_two, norm_rows[2], norm_rows[3])))
    act_three = low_back(project(low_two, last_weight))
    summed = inputs + layer_norm(act_three, norm_rows[4], norm_rows[5])
    slots = summed.shape[0]
    width = summed.shape[3]
    pooled = low(lax.optimization_barrier(jnp.mean(summed.reshape(slots, rows // 2, 2, cols // 2, 2, width), axis=(2, 4))))
    logits = low_back(project(pooled, read_weight) + read_bias)
    return jax.nn.gelu(logits, approximate=False) * mask[:, None, None, None]

def reference(images, first_weight, conv_weight, last_weight, norm_rows, read_weight, read_bias, cotangent, live_count):
    weights = (first_weight.astype(jnp.float32), conv_weight.astype(jnp.float32), last_weight.astype(jnp.float32), norm_rows.astype(jnp.float32), read_weight.astype(jnp.float32), read_bias.astype(jnp.float32))
    groups = images.shape[0] // SLOTS
    blocks = images.astype(jnp.float32).reshape(groups, SLOTS, H, W, C)
    cot_blocks = cotangent.astype(jnp.float32).reshape(groups, SLOTS, H // 2, W // 2, OUT)
    slot_ids = jnp.arange(SLOTS, dtype=jnp.int32)

    def step(totals, item):
        block, cot_block, count = item
        mask = (slot_ids < count).astype(jnp.float32)

        def whole(inputs, first, conv, last, norms, read, bias):
            return forward(inputs, first, conv, last, norms, read, bias, mask)
        result, pull = jax.vjp(whole, block, *weights)
        grads = pull(cot_block)
        totals = tuple((total + grad for total, grad in zip(totals, grads[1:])))
        return (totals, (result, grads[0]))
    zeros = tuple((jnp.zeros_like(weight) for weight in weights))
    totals, (results, input_grads) = lax.scan(step, zeros, (blocks, cot_blocks, live_count))
    readout_out = results.reshape(groups * SLOTS, H // 2, W // 2, OUT).astype(jnp.bfloat16)
    image_grad = input_grads.reshape(groups * SLOTS, H, W, C).astype(jnp.bfloat16)
    return (readout_out, image_grad, totals[0], totals[1], totals[2], totals[3], totals[4], totals[5])
```

```python
import jax
import jax.numpy as jnp
from jax import lax
from jax.sharding import PartitionSpec as P

eps = 1e-06
F32 = jnp.float32
BF16 = jnp.bfloat16
RING = 8


def ring_order(n):
    return list(range(0, n, 2)) + list(range(n - 1, 0, -2))


def ring_pairs(n):
    order = ring_order(n)
    right = [(order[i], order[(i + 1) % n]) for i in range(n)]
    left = [(b, a) for a, b in right]
    return right, left


def ring_index(n, step):
    me = lax.axis_index("dp")
    place = jnp.where(me % 2 == 0, me // 2, n - 1 - me // 2)
    place = (place + step) % n
    return jnp.where(place < n // 2, 2 * place, 2 * (n - 1 - place) + 1)


def gather_dp(x, n):
    if n != RING:
        return lax.all_gather(x, "dp", axis=0, tiled=False)
    right, left = ring_pairs(n)
    rows = x.shape[0]
    half = rows // 2
    whole = jnp.zeros((n,) + x.shape, x.dtype)
    put = lambda whole, piece, step, at: lax.dynamic_update_slice(
        whole, piece[None], (ring_index(n, step), at, 0)
    )
    whole = put(whole, x, 0, 0)
    a, b = x, x
    for step in range(1, n // 2):
        a = lax.ppermute(a, "dp", right)
        b = lax.ppermute(b, "dp", left)
        whole = put(whole, a, -step, 0)
        whole = put(whole, b, step, 0)
    a = lax.ppermute(a[:half], "dp", right)
    b = lax.ppermute(b[half:], "dp", left)
    whole = put(whole, a, n // 2, 0)
    whole = put(whole, b, n // 2, half)
    return whole


def scatter_dp(parts, n):
    if n != RING:
        return lax.psum_scatter(parts.astype(F32), "dp", scatter_dimension=0, tiled=False)
    right, left = ring_pairs(n)
    rows = parts.shape[1]
    half = rows // 2
    own = lambda step: lax.dynamic_index_in_dim(parts, ring_index(n, step), 0, keepdims=False)
    far = own(n // 2)
    a = lax.ppermute(far[:half].astype(BF16), "dp", right)
    b = lax.ppermute(far[half:].astype(BF16), "dp", left)
    for step in range(n // 2 - 1, 0, -1):
        up, down = own(step).astype(F32), own(-step).astype(F32)
        if step == n // 2 - 1:
            up = jnp.concatenate([up[:half] + a.astype(F32), up[half:]], axis=0)
            down = jnp.concatenate([down[:half], down[half:] + b.astype(F32)], axis=0)
        else:
            up, down = up + a.astype(F32), down + b.astype(F32)
        a = lax.ppermute(up.astype(BF16), "dp", right)
        b = lax.ppermute(down.astype(BF16), "dp", left)
    return own(0).astype(F32) + a.astype(F32) + b.astype(F32)


def swap_row(x, q):
    return lax.ppermute(x, "row", [(i, i ^ q) for i in range(4)])


def gather_row(x):
    two = swap_row(x, 2)
    one = swap_row(x, 1)
    return [x, one, two, swap_row(two, 1)]


def exchange_row(pieces):
    return [pieces[0]] + [swap_row(pieces[q], q) for q in (1, 2, 3)]


def scatter_row(pieces):
    near = swap_row(jnp.stack([pieces[1], pieces[3]]).astype(BF16), 1).astype(F32)
    mine = pieces[0].astype(F32) + near[0]
    other = (pieces[2].astype(F32) + near[1]).astype(BF16)
    return mine + swap_row(other, 2).astype(F32)


def pick(choices, index):
    value = choices[0]
    for i in range(1, len(choices)):
        value = jnp.where(index == i, choices[i], value)
    return value


def dot(left, right):
    return jnp.dot(left, right, preferred_element_type=F32)


def dot_t(left, right):
    return lax.dot_general(left, right, (((1,), (1,)), ((), ())), preferred_element_type=F32)


def t_dot(left, right):
    return lax.dot_general(left, right, (((0,), (0,)), ((), ())), preferred_element_type=F32)


def normalize(value):
    centred = value - jnp.mean(value, axis=-1, keepdims=True)
    scale = lax.rsqrt(jnp.mean(centred * centred, axis=-1, keepdims=True) + eps)
    return centred * scale, scale


def norm_backward(grad_out, normed, scale, gain):
    weighted = grad_out * gain
    return scale * (
        weighted
        - jnp.mean(weighted, axis=-1, keepdims=True)
        - normed * jnp.mean(weighted * normed, axis=-1, keepdims=True)
    )


def silu_slope(value):
    gate = jax.nn.sigmoid(value)
    return gate * (1.0 + value * (1.0 - gate))


def gelu_slope(value):
    return (
        0.5 * (1.0 + lax.erf(value * 0.7071067811865476))
        + value * jnp.exp(-0.5 * value * value) * 0.3989422804014327
    )


def columns(value):
    cols = value.shape[2]
    wide = jnp.pad(value, ((0, 0), (1, 1), (1, 1), (0, 0)))
    return jnp.concatenate([wide[:, :, v : v + cols] for v in range(3)], axis=3)


def per_device(
    images,
    first_weight,
    conv_weight,
    last_weight,
    norm_rows,
    read_weight,
    read_bias,
    cotangent,
    live_count,
):
    n, ranks = lax.axis_size("dp"), lax.axis_size("row")
    row = lax.axis_index("row")
    slots, band, cols, width = images.shape
    patches = slots * band * cols
    high = ranks * band
    own = first_weight.shape[0]
    group = n * own
    outs = read_weight.shape[1]
    rows_at = [row ^ q for q in range(ranks)]

    first_mine = first_weight.reshape(own, n, ranks, own).transpose(0, 2, 1, 3).reshape(own, width)
    small = jnp.concatenate([norm_rows.reshape(-1), read_bias])
    small = jnp.pad(small, (0, 8 * width - small.shape[0])).reshape(8, width)
    first_ring = gather_dp(jnp.concatenate([first_mine, small], axis=0), n)
    first_parts = gather_row(first_ring)

    def interleave(parts):
        whole = jnp.zeros((n, ranks) + parts[0].shape[1:], parts[0].dtype)
        for q in range(ranks):
            whole = lax.dynamic_update_slice(whole, parts[q][:, None], (0, rows_at[q], 0, 0))
        return whole

    first_all = interleave(first_parts)
    first_full = first_all[:, :, :own].reshape(width, width)
    norms = first_all[:, :, own].reshape(n, ranks, width)[:, :, : 6 * own]
    norms = norms.reshape(n, ranks, 6, own).astype(F32)
    norm_vals = norms.transpose(2, 0, 1, 3).reshape(6, width)
    norm_swap = norms.transpose(2, 1, 0, 3).reshape(6, width)
    bias_mine = first_ring[:, own, 6 * own : 6 * own + outs].reshape(n * outs).astype(F32)

    conv_taps = [gather_dp(conv_weight[u].reshape(3 * own, width), n) for u in range(3)]
    conv_taps = [
        tap.reshape(n, 3, own, width).transpose(1, 0, 2, 3).reshape(3 * group, width) for tap in conv_taps
    ]
    last_full = interleave(gather_row(gather_dp(last_weight, n))).reshape(width, width)
    read_mine = gather_dp(read_weight.T, n).reshape(n * outs, width)

    cot = cotangent.reshape(-1, n, ranks, outs)
    cot = exchange_row([pick([cot[:, :, i] for i in range(ranks)], rows_at[q]) for q in range(ranks)])
    cot = jnp.concatenate(cot, axis=0).reshape(-1, n * outs)

    flat_in = images.reshape(patches, width)
    hat_one, scale_one = normalize(dot(flat_in, first_full))
    pre_one = hat_one * norm_swap[0] + norm_swap[1]
    low_one = jax.nn.silu(pre_one).astype(BF16)
    split = [low_one[:, i * group : (i + 1) * group] for i in range(ranks)]
    bands = exchange_row([pick(split, rows_at[q]) for q in range(ranks)])

    def stack_bands(pieces):
        whole = jnp.zeros((slots, ranks, band, cols, pieces[0].shape[-1]), pieces[0].dtype)
        for q in range(ranks):
            piece = pieces[q].reshape(slots, 1, band, cols, -1)
            whole = lax.dynamic_update_slice(whole, piece, (0, rows_at[q], 0, 0, 0))
        return whole.reshape(slots, high, cols, -1)

    def take_bands(value):
        value = value.reshape(slots, ranks, band * cols, -1)
        return [
            lax.dynamic_index_in_dim(value, rows_at[q], 1, keepdims=False).reshape(patches, -1)
            for q in range(ranks)
        ]

    wide_one = columns(stack_bands(bands))
    slabs = [wide_one[:, u : u + high].reshape(slots * high * cols, 3 * group) for u in range(3)]
    act_two = dot(slabs[0], conv_taps[0]) + dot(slabs[1], conv_taps[1]) + dot(slabs[2], conv_taps[2])
    hat_two, scale_two = normalize(scatter_row(take_bands(act_two)))
    pre_two = hat_two * norm_vals[2] + norm_vals[3]
    low_two = jax.nn.silu(pre_two).astype(BF16)
    hat_three, scale_three = normalize(dot(low_two, last_full))
    summed = flat_in.astype(F32) + (hat_three * norm_vals[4] + norm_vals[5])
    pooled = jnp.mean(summed.reshape(slots, band // 2, 2, cols // 2, 2, width), axis=(2, 4)).astype(BF16)
    pooled = pooled.reshape(-1, width)
    pools = jnp.concatenate(gather_row(pooled), axis=0)
    logits = dot_t(pools, read_mine) + bias_mine
    mask = (jnp.arange(slots, dtype=jnp.int32) < live_count[0]).astype(F32)
    mask = jnp.broadcast_to(mask[None, :, None], (ranks, slots, pooled.shape[0] // slots)).reshape(-1, 1)
    shown = (jax.nn.gelu(logits, approximate=False) * mask).astype(BF16)
    shown = exchange_row(jnp.split(shown, ranks, axis=0))
    readout = jnp.zeros((pooled.shape[0], n, ranks, outs), BF16)
    for q in range(ranks):
        readout = lax.dynamic_update_slice(
            readout, shown[q].reshape(-1, n, 1, outs), (0, 0, rows_at[q], 0)
        )
    readout_out = readout.reshape(slots, band // 2, cols // 2, n * ranks * outs)

    grad_low = (cot.astype(F32) * mask * gelu_slope(logits)).astype(BF16)
    read_terms = t_dot(grad_low, pools).reshape(n, outs, width)
    bias_terms = jnp.sum(grad_low.astype(F32), axis=0).reshape(n, 1, outs)
    bias_terms = jnp.pad(bias_terms, ((0, 0), (0, 7), (0, width - outs)))
    read_sum = scatter_dp(jnp.concatenate([read_terms, bias_terms], axis=1), n)
    read_grad, bias_grad = read_sum[:outs].T, read_sum[outs, :outs]
    grad_pool = scatter_row(jnp.split(dot(grad_low, read_mine), ranks, axis=0))
    grad_sum = (
        jnp.broadcast_to(
            grad_pool.reshape(slots, band // 2, 1, cols // 2, 1, width),
            (slots, band // 2, 2, cols // 2, 2, width),
        )
        * 0.25
    ).reshape(-1, width)
    gain_three = jnp.sum(grad_sum * hat_three, axis=0)
    shift_three = jnp.sum(grad_sum, axis=0)
    grad_three = norm_backward(grad_sum, hat_three, scale_three, norm_vals[4]).astype(BF16)
    grad_pre_two = dot_t(grad_three, last_full) * silu_slope(pre_two)
    gain_two = jnp.sum(grad_pre_two * hat_two, axis=0)
    shift_two = jnp.sum(grad_pre_two, axis=0)
    grad_two = norm_backward(grad_pre_two, hat_two, scale_two, norm_vals[2]).astype(BF16)
    grad_full = stack_bands(gather_row(grad_two))
    grad_flat = grad_full.reshape(-1, width)

    def row_sums(terms):
        terms = terms.reshape(n, ranks, -1, width)
        return scatter_row(
            [lax.dynamic_index_in_dim(terms, rows_at[q], 1, keepdims=False) for q in range(ranks)]
        )

    conv_grad = []
    for u in range(3):
        terms = t_dot(slabs[u], grad_flat).reshape(3, n, own, width).transpose(1, 0, 2, 3)
        conv_grad.append(scatter_dp(terms.reshape(n, 3 * own, width), n).reshape(3, own, width))
    conv_grad = jnp.stack(conv_grad)
    wide_grad = jnp.pad(grad_full, ((0, 0), (1, 1), (1, 1), (0, 0)))
    grad_mid = jnp.zeros((slots * high * cols, group), F32)
    for u in range(3):
        for v in range(3):
            slab = wide_grad[:, 2 - u : 2 - u + high, 2 - v : 2 - v + cols].reshape(-1, width)
            grad_mid = grad_mid + dot_t(slab, conv_taps[u][v * group : (v + 1) * group])
    pieces = exchange_row(take_bands(grad_mid.astype(BF16)))
    grad_low_one = jnp.concatenate(
        [pick([pieces[i ^ q] for i in range(ranks)], row) for q in range(ranks)], axis=1
    ).astype(F32)
    last_sum = scatter_dp(row_sums(t_dot(low_two, grad_three)), n)

    grad_pre_one = grad_low_one * silu_slope(pre_one)
    gain_one = jnp.sum(grad_pre_one * hat_one, axis=0)
    shift_one = jnp.sum(grad_pre_one, axis=0)
    grad_one = norm_backward(grad_pre_one, hat_one, scale_one, norm_swap[0]).astype(BF16)
    image_grad = (grad_sum + dot_t(grad_one, first_full)).astype(BF16)
    image_grad = image_grad.reshape(slots, band, cols, width)

    swapped = jnp.stack([gain_one, shift_one]).reshape(2, ranks, n, own).transpose(2, 1, 0, 3)
    plain = jnp.stack([gain_two, shift_two, gain_three, shift_three])
    plain = plain.reshape(4, n, ranks, own).transpose(1, 2, 0, 3)
    norm_terms = jnp.concatenate([swapped, plain], axis=2).reshape(n, ranks, 1, 6 * own)
    norm_terms = jnp.pad(norm_terms, ((0, 0), (0, 0), (0, 7), (0, width - 6 * own)))
    first_terms = t_dot(flat_in, grad_one).reshape(n, ranks, own, width)
    first_sum = scatter_dp(row_sums(jnp.concatenate([first_terms, norm_terms], axis=2)), n)
    norm_grad = first_sum[own, : 6 * own].reshape(6, own)
    first_grad = first_sum[:own].reshape(own, ranks, n, own).transpose(0, 2, 1, 3).reshape(own, width)
    return (
        readout_out,
        image_grad,
        first_grad,
        conv_grad,
        last_sum,
        norm_grad,
        read_grad,
        bias_grad,
    )


def solution(mesh):
    return jax.shard_map(
        per_device,
        mesh=mesh,
        in_specs=(
            P("dp", "row", None, None),
            P(("dp", "row"), None),
            P(None, None, ("dp", "row"), None),
            P(("dp", "row"), None),
            P(None, ("dp", "row")),
            P(None, ("dp", "row")),
            P(("dp", "row")),
            P("dp", "row", None, None),
            P("dp"),
        ),
        out_specs=(
            P("dp", "row", None, None),
            P("dp", "row", None, None),
            P(("dp", "row"), None),
            P(None, None, ("dp", "row"), None),
            P(("dp", "row"), None),
            P(None, ("dp", "row")),
            P(None, ("dp", "row")),
            P(("dp", "row")),
        ),
        check_vma=False,
    )
```

```python
import functools

import jax
import jax.numpy as jnp
from jax import lax
from jax.experimental import pallas as pl
from jax.experimental.pallas import tpu as pltpu
from jax.sharding import PartitionSpec as P

eps = 1e-06
F32 = jnp.float32
BF16 = jnp.bfloat16
RING = 8


def ring_order(n):
    return list(range(0, n, 2)) + list(range(n - 1, 0, -2))


def ring_pairs(n):
    order = ring_order(n)
    right = [(order[i], order[(i + 1) % n]) for i in range(n)]
    left = [(b, a) for a, b in right]
    return right, left


def ring_index(n, step):
    me = lax.axis_index("dp")
    place = jnp.where(me % 2 == 0, me // 2, n - 1 - me // 2)
    place = (place + step) % n
    return jnp.where(place < n // 2, 2 * place, 2 * (n - 1 - place) + 1)


def gather_dp(x, n):
    return lax.all_gather(x, "dp", axis=0, tiled=False)


def scatter_dp(parts, n):
    return lax.psum_scatter(parts.astype(F32), "dp", scatter_dimension=0, tiled=False)


def swap_row(x, q):
    return lax.ppermute(x, "row", [(i, i ^ q) for i in range(4)])


def gather_row(x):
    two = swap_row(x, 2)
    one = swap_row(x, 1)
    return [x, one, two, swap_row(two, 1)]


def exchange_row(pieces):
    return [pieces[0]] + [swap_row(pieces[q], q) for q in (1, 2, 3)]


def scatter_row(pieces):
    near = swap_row(jnp.stack([pieces[1], pieces[3]]).astype(BF16), 1).astype(F32)
    mine = pieces[0].astype(F32) + near[0]
    other = (pieces[2].astype(F32) + near[1]).astype(BF16)
    return mine + swap_row(other, 2).astype(F32)


def pick(choices, index):
    value = choices[0]
    for i in range(1, len(choices)):
        value = jnp.where(index == i, choices[i], value)
    return value


def dot(left, right):
    return jnp.dot(left, right, preferred_element_type=F32)


def dot_t(left, right):
    return lax.dot_general(left, right, (((1,), (1,)), ((), ())), preferred_element_type=F32)


def t_dot(left, right):
    return lax.dot_general(left, right, (((0,), (0,)), ((), ())), preferred_element_type=F32)


def normalize(value):
    centred = value - jnp.mean(value, axis=-1, keepdims=True)
    scale = lax.rsqrt(jnp.mean(centred * centred, axis=-1, keepdims=True) + eps)
    return centred * scale, scale


def norm_backward(grad_out, normed, scale, gain):
    weighted = grad_out * gain
    return scale * (
        weighted
        - jnp.mean(weighted, axis=-1, keepdims=True)
        - normed * jnp.mean(weighted * normed, axis=-1, keepdims=True)
    )


def silu_slope(value):
    gate = jax.nn.sigmoid(value)
    return gate * (1.0 + value * (1.0 - gate))


def gelu_slope(value):
    return (
        0.5 * (1.0 + lax.erf(value * 0.7071067811865476))
        + value * jnp.exp(-0.5 * value * value) * 0.3989422804014327
    )


def columns(value):
    cols = value.shape[2]
    wide = jnp.pad(value, ((0, 0), (1, 1), (1, 1), (0, 0)))
    return jnp.concatenate([wide[:, :, v : v + cols] for v in range(3)], axis=3)


def generic(
    images,
    first_weight,
    conv_weight,
    last_weight,
    norm_rows,
    read_weight,
    read_bias,
    cotangent,
    live_count,
):
    n, ranks = lax.axis_size("dp"), lax.axis_size("row")
    row = lax.axis_index("row")
    slots, band, cols, width = images.shape
    patches = slots * band * cols
    high = ranks * band
    own = first_weight.shape[0]
    group = n * own
    outs = read_weight.shape[1]
    rows_at = [row ^ q for q in range(ranks)]

    first_mine = first_weight.reshape(own, n, ranks, own).transpose(0, 2, 1, 3).reshape(own, width)
    small = jnp.concatenate([norm_rows.reshape(-1), read_bias])
    small = jnp.pad(small, (0, 8 * width - small.shape[0])).reshape(8, width)
    first_ring = gather_dp(jnp.concatenate([first_mine, small], axis=0), n)
    first_parts = gather_row(first_ring)

    def interleave(parts):
        whole = jnp.zeros((n, ranks) + parts[0].shape[1:], parts[0].dtype)
        for q in range(ranks):
            whole = lax.dynamic_update_slice(whole, parts[q][:, None], (0, rows_at[q], 0, 0))
        return whole

    first_all = interleave(first_parts)
    first_full = first_all[:, :, :own].reshape(width, width)
    norms = first_all[:, :, own].reshape(n, ranks, width)[:, :, : 6 * own]
    norms = norms.reshape(n, ranks, 6, own).astype(F32)
    norm_vals = norms.transpose(2, 0, 1, 3).reshape(6, width)
    norm_swap = norms.transpose(2, 1, 0, 3).reshape(6, width)
    bias_mine = first_ring[:, own, 6 * own : 6 * own + outs].reshape(n * outs).astype(F32)

    conv_taps = [gather_dp(conv_weight[u].reshape(3 * own, width), n) for u in range(3)]
    conv_taps = [
        tap.reshape(n, 3, own, width).transpose(1, 0, 2, 3).reshape(3 * group, width) for tap in conv_taps
    ]
    last_full = interleave(gather_row(gather_dp(last_weight, n))).reshape(width, width)
    read_mine = gather_dp(read_weight.T, n).reshape(n * outs, width)

    cot = cotangent.reshape(-1, n, ranks, outs)
    cot = exchange_row([pick([cot[:, :, i] for i in range(ranks)], rows_at[q]) for q in range(ranks)])
    cot = jnp.concatenate(cot, axis=0).reshape(-1, n * outs)

    flat_in = images.reshape(patches, width)
    hat_one, scale_one = normalize(dot(flat_in, first_full))
    pre_one = hat_one * norm_swap[0] + norm_swap[1]
    low_one = jax.nn.silu(pre_one).astype(BF16)
    split = [low_one[:, i * group : (i + 1) * group] for i in range(ranks)]
    bands = exchange_row([pick(split, rows_at[q]) for q in range(ranks)])

    def stack_bands(pieces):
        whole = jnp.zeros((slots, ranks, band, cols, pieces[0].shape[-1]), pieces[0].dtype)
        for q in range(ranks):
            piece = pieces[q].reshape(slots, 1, band, cols, -1)
            whole = lax.dynamic_update_slice(whole, piece, (0, rows_at[q], 0, 0, 0))
        return whole.reshape(slots, high, cols, -1)

    def take_bands(value):
        value = value.reshape(slots, ranks, band * cols, -1)
        return [
            lax.dynamic_index_in_dim(value, rows_at[q], 1, keepdims=False).reshape(patches, -1)
            for q in range(ranks)
        ]

    wide_one = columns(stack_bands(bands))
    slabs = [wide_one[:, u : u + high].reshape(slots * high * cols, 3 * group) for u in range(3)]
    act_two = dot(slabs[0], conv_taps[0]) + dot(slabs[1], conv_taps[1]) + dot(slabs[2], conv_taps[2])
    hat_two, scale_two = normalize(scatter_row(take_bands(act_two)))
    pre_two = hat_two * norm_vals[2] + norm_vals[3]
    low_two = jax.nn.silu(pre_two).astype(BF16)
    hat_three, scale_three = normalize(dot(low_two, last_full))
    summed = flat_in.astype(F32) + (hat_three * norm_vals[4] + norm_vals[5])
    pooled = jnp.mean(summed.reshape(slots, band // 2, 2, cols // 2, 2, width), axis=(2, 4)).astype(BF16)
    pooled = pooled.reshape(-1, width)
    pools = jnp.concatenate(gather_row(pooled), axis=0)
    logits = dot_t(pools, read_mine) + bias_mine
    mask = (jnp.arange(slots, dtype=jnp.int32) < live_count[0]).astype(F32)
    mask = jnp.broadcast_to(mask[None, :, None], (ranks, slots, pooled.shape[0] // slots)).reshape(-1, 1)
    shown = (jax.nn.gelu(logits, approximate=False) * mask).astype(BF16)
    shown = exchange_row(jnp.split(shown, ranks, axis=0))
    readout = jnp.zeros((pooled.shape[0], n, ranks, outs), BF16)
    for q in range(ranks):
        readout = lax.dynamic_update_slice(
            readout, shown[q].reshape(-1, n, 1, outs), (0, 0, rows_at[q], 0)
        )
    readout_out = readout.reshape(slots, band // 2, cols // 2, n * ranks * outs)

    grad_low = (cot.astype(F32) * mask * gelu_slope(logits)).astype(BF16)
    read_terms = t_dot(grad_low, pools).reshape(n, outs, width)
    bias_terms = jnp.sum(grad_low.astype(F32), axis=0).reshape(n, 1, outs)
    bias_terms = jnp.pad(bias_terms, ((0, 0), (0, 7), (0, width - outs)))
    read_sum = scatter_dp(jnp.concatenate([read_terms, bias_terms], axis=1), n)
    read_grad, bias_grad = read_sum[:outs].T, read_sum[outs, :outs]
    grad_pool = scatter_row(jnp.split(dot(grad_low, read_mine), ranks, axis=0))
    grad_sum = (
        jnp.broadcast_to(
            grad_pool.reshape(slots, band // 2, 1, cols // 2, 1, width),
            (slots, band // 2, 2, cols // 2, 2, width),
        )
        * 0.25
    ).reshape(-1, width)
    gain_three = jnp.sum(grad_sum * hat_three, axis=0)
    shift_three = jnp.sum(grad_sum, axis=0)
    grad_three = norm_backward(grad_sum, hat_three, scale_three, norm_vals[4]).astype(BF16)
    grad_pre_two = dot_t(grad_three, last_full) * silu_slope(pre_two)
    gain_two = jnp.sum(grad_pre_two * hat_two, axis=0)
    shift_two = jnp.sum(grad_pre_two, axis=0)
    grad_two = norm_backward(grad_pre_two, hat_two, scale_two, norm_vals[2]).astype(BF16)
    grad_full = stack_bands(gather_row(grad_two))
    grad_flat = grad_full.reshape(-1, width)

    def row_sums(terms):
        terms = terms.reshape(n, ranks, -1, width)
        return scatter_row(
            [lax.dynamic_index_in_dim(terms, rows_at[q], 1, keepdims=False) for q in range(ranks)]
        )

    conv_grad = []
    for u in range(3):
        terms = t_dot(slabs[u], grad_flat).reshape(3, n, own, width).transpose(1, 0, 2, 3)
        conv_grad.append(scatter_dp(terms.reshape(n, 3 * own, width), n).reshape(3, own, width))
    conv_grad = jnp.stack(conv_grad)
    wide_grad = jnp.pad(grad_full, ((0, 0), (1, 1), (1, 1), (0, 0)))
    grad_mid = jnp.zeros((slots * high * cols, group), F32)
    for u in range(3):
        for v in range(3):
            slab = wide_grad[:, 2 - u : 2 - u + high, 2 - v : 2 - v + cols].reshape(-1, width)
            grad_mid = grad_mid + dot_t(slab, conv_taps[u][v * group : (v + 1) * group])
    pieces = exchange_row(take_bands(grad_mid.astype(BF16)))
    grad_low_one = jnp.concatenate(
        [pick([pieces[i ^ q] for i in range(ranks)], row) for q in range(ranks)], axis=1
    ).astype(F32)
    last_sum = scatter_dp(row_sums(t_dot(low_two, grad_three)), n)

    grad_pre_one = grad_low_one * silu_slope(pre_one)
    gain_one = jnp.sum(grad_pre_one * hat_one, axis=0)
    shift_one = jnp.sum(grad_pre_one, axis=0)
    grad_one = norm_backward(grad_pre_one, hat_one, scale_one, norm_swap[0]).astype(BF16)
    image_grad = (grad_sum + dot_t(grad_one, first_full)).astype(BF16)
    image_grad = image_grad.reshape(slots, band, cols, width)

    swapped = jnp.stack([gain_one, shift_one]).reshape(2, ranks, n, own).transpose(2, 1, 0, 3)
    plain = jnp.stack([gain_two, shift_two, gain_three, shift_three])
    plain = plain.reshape(4, n, ranks, own).transpose(1, 2, 0, 3)
    norm_terms = jnp.concatenate([swapped, plain], axis=2).reshape(n, ranks, 1, 6 * own)
    norm_terms = jnp.pad(norm_terms, ((0, 0), (0, 0), (0, 7), (0, width - 6 * own)))
    first_terms = t_dot(flat_in, grad_one).reshape(n, ranks, own, width)
    first_sum = scatter_dp(row_sums(jnp.concatenate([first_terms, norm_terms], axis=2)), n)
    norm_grad = first_sum[own, : 6 * own].reshape(6, own)
    first_grad = first_sum[:own].reshape(own, ranks, n, own).transpose(0, 2, 1, 3).reshape(own, width)
    return (
        readout_out,
        image_grad,
        first_grad,
        conv_grad,
        last_sum,
        norm_grad,
        read_grad,
        bias_grad,
    )


VM = pl.BlockSpec(memory_space=pltpu.VMEM)
SM = pl.BlockSpec(memory_space=pltpu.SMEM)
HB = pl.BlockSpec(memory_space=pl.ANY)


def shape(dims, dtype):
    return jax.ShapeDtypeStruct(dims, dtype)


def kernel(body, outs, ins, scratch, flops, moved, *arrays):
    return pl.pallas_call(
        body,
        out_shape=outs,
        in_specs=ins,
        out_specs=jax.tree.map(lambda _: VM, outs),
        scratch_shapes=scratch,
        cost_estimate=pl.CostEstimate(flops=flops, bytes_accessed=moved, transcendentals=0),
    )(*arrays)


def at_row(where, q):
    return where[0] ^ q


def start_all(copies):
    for copy in copies:
        copy.start()


def wait_all(copies):
    for copy in copies:
        copy.wait()


def copies_of(pairs, sems):
    return [pltpu.make_async_copy(a, b, sems.at[i]) for i, (a, b) in enumerate(pairs)]


def ring_gather(x, low, high):
    right, left = ring_pairs(RING)
    half = RING // 2
    pieces = [None] * RING
    pieces[0] = x
    a, b = x, x
    for step in range(1, half):
        a = lax.ppermute(a, "dp", right)
        b = lax.ppermute(b, "dp", left)
        pieces[RING - step], pieces[step] = a, b
    pieces[half] = (lax.ppermute(low(a), "dp", right), lax.ppermute(high(b), "dp", left))
    return pieces


def ring_scatter(terms, low, high, join):
    right, left = ring_pairs(RING)
    half = RING // 2
    far = terms[half]
    a = lax.ppermute(low(far), "dp", right)
    b = lax.ppermute(high(far), "dp", left)
    for step in range(half - 1, 0, -1):
        up, down = terms[step].astype(F32), terms[RING - step].astype(F32)
        if step == half - 1:
            up = join(low(up) + a.astype(F32), high(up))
            down = join(low(down), high(down) + b.astype(F32))
        else:
            up, down = up + a.astype(F32), down + b.astype(F32)
        a = lax.ppermute(up.astype(BF16), "dp", right)
        b = lax.ppermute(down.astype(BF16), "dp", left)
    return terms[0].astype(F32) + a.astype(F32) + b.astype(F32)


def row_scatter(own, near, far):
    near = swap_row(near, 1)
    other = (far + near[1].astype(F32)).astype(BF16)
    return own, near[0], swap_row(other, 2)


def unpack_first(where, firsts, weight, sems):
    pairs = []
    for q in range(4):
        for k in range(RING):
            pairs.append((firsts[q].at[k, pl.ds(0, weight.shape[2])], weight.at[where[2 + k], at_row(where, q)]))
    return copies_of(pairs, sems)


def center(value):
    mean = jnp.mean(value, axis=-1, keepdims=True)
    gap = value - mean
    scale = lax.rsqrt(jnp.mean(gap * gap, axis=-1, keepdims=True) + eps)
    return gap * scale, scale


def stage_one(where, x, f0, f1, f2, f3, small, hat, scale, s0, s1, s2, s3, norms, weight, low, sems):
    copies = unpack_first(where, (f0, f1, f2, f3), weight, sems)
    start_all(copies)
    width = x.shape[1]
    total = jnp.zeros((16, width), F32)
    bias = total
    for q in range(4):
        for k in range(RING):
            block = small[q, k].astype(F32)
            total = total + block
            if q == 0:
                bias = bias + block
    line = lax.broadcasted_iota(jnp.int32, (16, width), 0)
    table = jnp.where(line == 6, bias, total)
    norms[...] = table
    wait_all(copies)
    act = dot(x[...], weight[...].reshape(width, width))
    normed, root = center(act)
    hat[...] = normed
    scale[...] = root
    pre = normed * norms[0:1, :] + norms[1:2, :]
    low[...] = (pre * jax.nn.sigmoid(pre)).astype(BF16)
    part = width // 4
    for q, out in enumerate((s0, s1, s2, s3)):
        out[...] = low[:, pl.ds(pl.multiple_of(at_row(where, q) * part, part), part)]


def conv_copies(where, pieces, weight, sems):
    half = RING // 2
    pairs = []
    for k in range(RING):
        if k == half:
            rows = pieces[half].shape[1]
            pairs.append((pieces[half], weight.at[:, where[2 + k], pl.ds(0, rows)]))
            pairs.append((pieces[RING], weight.at[:, where[2 + k], pl.ds(rows, rows)]))
        else:
            pairs.append((pieces[k], weight.at[:, where[2 + k]]))
    return copies_of(pairs, sems)


def flat_pieces(pieces):
    half = RING // 2
    return [p[0] if k == half else p for k, p in enumerate(pieces)] + [pieces[half][1]]


def conv_forward(dims, where, s0, s1, s2, s3, *refs):
    slots, rows, cols = dims
    pieces, (near, own, far, wide, weight, pad, out, sems) = refs[: RING + 1], refs[RING + 1 :]
    copies = conv_copies(where, pieces, weight, sems)
    start_all(copies)
    group = s0.shape[1]
    patches = rows * cols
    band = patches // 4
    pad[...] = jnp.zeros_like(pad)
    for q, piece in enumerate((s0, s1, s2, s3)):
        for i in range(slots):
            at = pl.multiple_of(cols + 8 + at_row(where, q) * band, 8)
            pad[i, pl.ds(at, band), :] = piece[i * band : (i + 1) * band, :].astype(F32)
    for i in range(slots):
        for v in range(3):
            shifted = pad[i, 8 + v - 1 : 8 + v - 1 + patches + 2 * cols, :]
            if v != 1:
                col = lax.broadcasted_iota(jnp.int32, shifted.shape, 0) % cols
                shifted = jnp.where(col == (0 if v == 0 else cols - 1), 0.0, shifted)
            for u in range(3):
                t = u * 3 + v
                wide[i * patches : (i + 1) * patches, t * group : (t + 1) * group] = shifted[
                    u * cols : u * cols + patches
                ].astype(BF16)
    wait_all(copies)
    width = out.shape[1]
    chunk = 256

    @pl.loop(0, width // chunk)
    def _(j):
        lanes = pl.ds(pl.multiple_of(j * chunk, chunk), chunk)
        taps = weight[:, :, :, lanes].reshape(-1, chunk)
        out[:, lanes] = dot(wide[...], taps)

    for q, (ref, slot) in enumerate(((own, None), (near, 0), (far, None), (near, 1))):
        for i in range(slots):
            at = pl.multiple_of(i * patches + at_row(where, q) * band, 8)
            value = out[pl.ds(at, band), :]
            here = pl.ds(i * band, band)
            if slot is None:
                ref[here, :] = value
            else:
                ref[slot, here, :] = value.astype(BF16)


def stage_two(dims, where, own, near, cross, x, norms, l0, l1, l2, l3, hat_two, scale_two, low, hat, scale, pooled, weight, pairs, sems):
    slots, rows, cols = dims
    copies = unpack_first(where, (l0, l1, l2, l3), weight, sems)
    start_all(copies)
    width = x.shape[1]
    act = own[...] + near[...].astype(F32) + cross[...].astype(F32)
    normed, root = center(act)
    hat_two[...] = normed
    scale_two[...] = root
    pre = normed * norms[2:3, :] + norms[3:4, :]
    low[...] = (pre * jax.nn.sigmoid(pre)).astype(BF16)
    wait_all(copies)
    normed, root = center(dot(low[...], weight[...].reshape(width, width)))
    hat[...] = normed
    scale[...] = root
    y = x[...].astype(F32) + (normed * norms[4:5, :] + norms[5:6, :])
    y = jnp.sum(y.reshape(slots * rows // 2, 2, cols, width), axis=1).reshape(-1, width)
    count = pooled.shape[0]
    for g in range(pairs.shape[0]):
        lanes = slice(g * 128, (g + 1) * 128)
        pairs[g] = y[:, lanes]
        pooled[:, lanes] = (
            0.25 * (pairs[g, pl.ds(0, count, stride=2), :] + pairs[g, pl.ds(1, count, stride=2), :])
        ).astype(BF16)


def read_copies(where, pieces, weight, sems):
    half = RING // 2
    pairs = []
    for k in range(RING):
        if k == half:
            rows = pieces[half].shape[0]
            pairs.append((pieces[half], weight.at[where[2 + k], pl.ds(0, rows)]))
            pairs.append((pieces[RING], weight.at[where[2 + k], pl.ds(rows, rows)]))
        else:
            pairs.append((pieces[k], weight.at[where[2 + k]]))
    return copies_of(pairs, sems)


def readout(slots, where, p0, p1, p2, p3, c0, c1, c2, c3, norms, *refs):
    pieces = refs[: RING + 1]
    o0, o1, o2, o3, low, own, near, far, weight, sems = refs[RING + 1 :]
    copies = read_copies(where, pieces, weight, sems)
    start_all(copies)
    count, width = p0.shape
    table = jnp.concatenate([p[...] for p in (p0, p1, p2, p3)], axis=0)
    line = lax.broadcasted_iota(jnp.int32, (count, width), 0)
    mask = jnp.where(line // (count // slots) < where[1], 1.0, 0.0)
    wait_all(copies)
    whole = weight[...].reshape(-1, width)
    logits = dot_t(table, whole) + norms[6:7, :]
    for q, (cot, out) in enumerate(((c0, o0), (c1, o1), (c2, o2), (c3, o3))):
        z = logits[q * count : (q + 1) * count]
        phi = 0.5 * (1.0 + lax.erf(z * 0.7071067811865476))
        out[...] = (z * phi * mask).astype(BF16)
        slope = phi + z * jnp.exp(-0.5 * z * z) * 0.3989422804014327
        low[q * count : (q + 1) * count, :] = (cot[...].astype(F32) * mask * slope).astype(BF16)
    back = dot(low[...], whole)
    own[...] = back[:count]
    near[0] = back[count : 2 * count].astype(BF16)
    far[...] = back[2 * count : 3 * count]
    near[1] = back[3 * count :].astype(BF16)


def readout_terms(where, low, p0, p1, p2, p3, out, terms):
    width = p0.shape[1]
    table = jnp.concatenate([p[...] for p in (p0, p1, p2, p3)], axis=0)
    terms[...] = t_dot(low[...], table).reshape(terms.shape)
    bias = jnp.sum(low[...].astype(F32), axis=0, keepdims=True)
    rows = terms.shape[1]
    for k in range(RING):
        out[k, :rows, :] = terms[where[2 + k]].astype(BF16)
        out[k, rows:, :] = jnp.broadcast_to(bias, (out.shape[1] - rows, width)).astype(BF16)


def spread(pairs, grad, dims):
    slots, rows, cols = dims
    count, width = grad.shape
    for g in range(pairs.shape[0]):
        lanes = slice(g * 128, (g + 1) * 128)
        pairs[g, pl.ds(0, count, stride=2), :] = grad[:, lanes]
        pairs[g, pl.ds(1, count, stride=2), :] = grad[:, lanes]
    half = slots * rows // 2
    both = jnp.concatenate([pairs[g] for g in range(pairs.shape[0])], axis=1)
    both = jnp.broadcast_to(both.reshape(half, 1, cols, width), (half, 2, cols, width))
    return both.reshape(-1, width) * 0.25


def back_norm(grad, normed, root, gain):
    weighted = grad * gain
    return root * (
        weighted
        - jnp.mean(weighted, axis=-1, keepdims=True)
        - normed * jnp.mean(weighted * normed, axis=-1, keepdims=True)
    )


def total_rows(value):
    return jnp.sum(value, axis=0, keepdims=True)


def stage_two_back(dims, where, own, near, cross, hat, scale, hat_two, scale_two, norms, l0, l1, l2, l3, grad_three, grad_two, pool_sum, sums, weight, pairs, sems):
    copies = unpack_first(where, (l0, l1, l2, l3), weight, sems)
    start_all(copies)
    width = hat.shape[1]
    grad = own[...] + near[...].astype(F32) + cross[...].astype(F32)
    pool_sum[...] = grad
    gy = spread(pairs, grad, dims)
    sums[...] = jnp.zeros_like(sums)
    sums[4:5, :] = total_rows(gy * hat[...])
    sums[5:6, :] = total_rows(gy)
    grad_three[...] = back_norm(gy, hat[...], scale[...], norms[4:5, :]).astype(BF16)
    wait_all(copies)
    gs = dot_t(grad_three[...], weight[...].reshape(width, width))
    pre = hat_two[...] * norms[2:3, :] + norms[3:4, :]
    gn = gs * silu_slope(pre)
    sums[2:3, :] = total_rows(gn * hat_two[...])
    sums[3:4, :] = total_rows(gn)
    grad_two[...] = back_norm(gn, hat_two[...], scale_two[...], norms[2:3, :]).astype(BF16)


def last_terms(where, low, grad, own, near, far, terms):
    terms[...] = t_dot(low[...], grad[...]).reshape(terms.shape)
    for k in range(RING):
        own[k] = terms[where[2 + k], at_row(where, 0)]
        near[0, k] = terms[where[2 + k], at_row(where, 1)].astype(BF16)
        far[k] = terms[where[2 + k], at_row(where, 2)]
        near[1, k] = terms[where[2 + k], at_row(where, 3)].astype(BF16)


def stack_grad(dims, where, pieces, whole):
    slots, rows, cols = dims
    band = rows * cols // 4
    for q, piece in enumerate(pieces):
        for i in range(slots):
            at = pl.multiple_of(i * rows * cols + at_row(where, q) * band, 16)
            whole[pl.ds(at, band), :] = piece[i * band : (i + 1) * band, :]


def conv_terms(dims, where, wide, g0, g1, g2, g3, out, whole):
    stack_grad(dims, where, (g0, g1, g2, g3), whole)
    taps, rows, width = out.shape[1:]
    group = RING * rows

    @pl.loop(0, taps)
    def _(t):
        lanes = pl.ds(pl.multiple_of(t * group, group), group)
        terms = t_dot(wide[:, lanes], whole[...]).astype(BF16).reshape(RING, rows, width)
        for k in range(RING):
            out[where[2 + RING + k], t] = terms[k]


def conv_back(dims, where, g0, g1, g2, g3, *refs):
    slots, rows, cols = dims
    pieces, (o0, o1, o2, o3, weight, whole, held, low, sems) = refs[: RING + 1], refs[RING + 1 :]
    copies = conv_copies(where, pieces, weight, sems)
    start_all(copies)
    stack_grad(dims, where, (g0, g1, g2, g3), whole)
    patches = rows * cols
    band = patches // 4
    group = o0.shape[1]
    width = whole.shape[1]
    held[...] = jnp.zeros_like(held)
    wait_all(copies)
    for u in range(3):
        for v in range(3):
            part = dot_t(whole[...], weight[u * 3 + v].reshape(group, width))
            for i in range(slots):
                held[v, i, 8 + u * cols : 8 + u * cols + patches, :] += part[i * patches : (i + 1) * patches]
    col = lax.broadcasted_iota(jnp.int32, (patches, group), 0) % cols
    for i in range(slots):
        value = held[1, i, 8 + cols : 8 + cols + patches, :]
        value += jnp.where(col == cols - 1, 0.0, held[0, i, 9 + cols : 9 + cols + patches, :])
        value += jnp.where(col == 0, 0.0, held[2, i, 7 + cols : 7 + cols + patches, :])
        low[i * patches : (i + 1) * patches, :] = value.astype(BF16)
    for q, out in enumerate((o0, o1, o2, o3)):
        for i in range(slots):
            at = pl.multiple_of(i * patches + at_row(where, q) * band, 16)
            out[i * band : (i + 1) * band, :] = low[pl.ds(at, band), :]


def stage_one_back(where, b0, b1, b2, b3, hat, scale, norms, x, sums, grad_one, own, near, far, low, terms):
    width = hat.shape[1]
    part = width // 4
    for q, piece in enumerate((b0, b1, b2, b3)):
        low[:, pl.ds(pl.multiple_of(at_row(where, q) * part, part), part)] = piece[...]
    pre = hat[...] * norms[0:1, :] + norms[1:2, :]
    gn = low[...].astype(F32) * silu_slope(pre)
    line = lax.broadcasted_iota(jnp.int32, (8, width), 0)
    tail = jnp.where(line == 0, total_rows(gn * hat[...]), jnp.where(line == 1, total_rows(gn), sums[...]))
    tail = jnp.concatenate([tail, tail], axis=0)
    grad_one[...] = back_norm(gn, hat[...], scale[...], norms[0:1, :]).astype(BF16)
    terms[...] = t_dot(x[...], grad_one[...]).reshape(terms.shape)
    rows = terms.shape[2]
    for k in range(RING):
        own[k, :rows] = terms[where[2 + k], at_row(where, 0)]
        near[0, k, :rows] = terms[where[2 + k], at_row(where, 1)].astype(BF16)
        far[k, :rows] = terms[where[2 + k], at_row(where, 2)]
        near[1, k, :rows] = terms[where[2 + k], at_row(where, 3)].astype(BF16)
        own[k, rows:] = tail
        near[0, k, rows:] = tail.astype(BF16)
        far[k, rows:] = tail
        near[1, k, rows:] = tail.astype(BF16)


def image_back(dims, where, grad_one, pool_sum, f0, f1, f2, f3, out, weight, pairs, sems):
    copies = unpack_first(where, (f0, f1, f2, f3), weight, sems)
    start_all(copies)
    width = grad_one.shape[1]
    gy = spread(pairs, pool_sum[...], dims)
    wait_all(copies)
    out[...] = (gy + dot_t(grad_one[...], weight[...].reshape(width, width))).astype(BF16)


def split_columns(where, x, o0, o1, o2, o3):
    lanes = x.shape[1] // (4 * RING)
    for q, out in enumerate((o0, o1, o2, o3)):
        for g in range(RING):
            at = pl.multiple_of((g * 4 + at_row(where, q)) * lanes, lanes)
            out[:, g * lanes : (g + 1) * lanes] = x[:, pl.ds(at, lanes)]


def join_columns(where, i0, i1, i2, i3, out):
    lanes = out.shape[1] // (4 * RING)
    for q, piece in enumerate((i0, i1, i2, i3)):
        for g in range(RING):
            at = pl.multiple_of((g * 4 + at_row(where, q)) * lanes, lanes)
            out[:, pl.ds(at, lanes)] = piece[:, g * lanes : (g + 1) * lanes]


def ringed(
    images,
    first_weight,
    conv_weight,
    last_weight,
    norm_rows,
    read_weight,
    read_bias,
    cotangent,
    live_count,
):
    dp, row = lax.axis_index("dp"), lax.axis_index("row")
    slots, band, cols, width = images.shape
    dims = (slots, band, cols)
    full = (slots, 4 * band, cols)
    patches = slots * band * cols
    count = patches // 4
    own = first_weight.shape[0]
    group = RING * own
    outs = read_weight.shape[1]
    taps = 9
    DMA = pltpu.SemaphoreType.DMA
    index = jnp.arange(18, dtype=jnp.int32)
    place_of = lambda d: jnp.where(d % 2 == 0, d // 2, RING - 1 - d // 2)
    place = (place_of(dp) + index - 2) % RING
    ahead = jnp.where(place < RING // 2, 2 * place, 2 * (RING - 1 - place) + 1)
    steps = (place_of(index - 10) - place_of(dp)) % RING
    where = jnp.where(index == 0, row, jnp.where(index == 1, live_count[0], jnp.where(index < 10, ahead, steps)))
    where = where.astype(jnp.int32)

    first_mine = first_weight.reshape(own, RING, 4, own).transpose(0, 2, 1, 3).reshape(own, width)
    lane = jnp.arange(width, dtype=jnp.int32)[None, :]
    tiled = jnp.tile(norm_rows, (1, width // own))
    at = jnp.where(jnp.arange(6)[:, None] < 2, row * RING + dp, dp * 4 + row)
    small = jnp.where(lane // own == at, tiled, 0).astype(BF16)
    bias = jnp.where(lane // outs == dp, jnp.tile(read_bias, width // outs)[None, :], 0).astype(BF16)
    small = jnp.concatenate([small, bias, jnp.zeros((9, width), BF16)], axis=0)
    cut = own + 16
    packed = jnp.concatenate([first_mine, small, last_weight], axis=0)
    ring = ring_gather(packed, lambda v: v[:cut], lambda v: v[cut:])
    far = RING // 2
    firsts = jnp.stack([ring[k][0] if k == far else ring[k][:cut] for k in range(RING)])
    lasts = jnp.stack([ring[k][1] if k == far else ring[k][cut:] for k in range(RING)])
    firsts = gather_row(firsts)
    smalls = jnp.stack([f[:, own:] for f in firsts])
    conv = conv_weight.reshape(taps, own, width)
    conv = ring_gather(conv, lambda v: v[:, : own // 2], lambda v: v[:, own // 2 :])
    conv = flat_pieces(conv)
    lasts = gather_row(lasts)
    read = ring_gather(read_weight.T, lambda v: v[: outs // 2], lambda v: v[outs // 2 :])
    read = flat_pieces(read)
    quarter = shape((count, width), BF16)
    cots = kernel(
        split_columns, [quarter] * 4, [SM, VM], [], 0, 2 * count * 4 * width * 2, where, cotangent.reshape(count, -1)
    )
    cots = exchange_row(cots)

    x = images.reshape(patches, width)
    wide_f32, thin_f32, wide_bf16 = (
        shape((patches, width), F32),
        shape((patches, 1), F32),
        shape((patches, width), BF16),
    )
    piece = shape((patches, group), BF16)
    whole = pltpu.VMEM((RING, 4, own, width), BF16)
    matmul = 2 * patches * width * width
    square = 2 * width * width
    hat_one, scale_one, *lows, norms = kernel(
        stage_one,
        [wide_f32, thin_f32] + [piece] * 4 + [shape((16, width), F32)],
        [SM, VM] + [HB] * 4 + [VM],
        [whole, pltpu.VMEM((patches, width), BF16), DMA((32,))],
        matmul,
        square + 8 * patches * width,
        where,
        x,
        *firsts,
        smalls,
    )
    lows = exchange_row(lows)
    conv_scratch = pltpu.VMEM((taps, RING, own, width), BF16)
    total = 4 * patches
    pad_rows = full[1] * cols + 2 * cols + 16
    near, mine, away, spans = kernel(
        functools.partial(conv_forward, full),
        [shape((2, patches, width), BF16), wide_f32, wide_f32, shape((total, taps * group), BF16)],
        [SM] + [VM] * 4 + [HB] * (RING + 1),
        [
            conv_scratch,
            pltpu.VMEM((slots, pad_rows, group), F32),
            pltpu.VMEM((total, width), F32),
            DMA((RING + 1,)),
        ],
        9 * matmul,
        9 * square + 12 * patches * width + 2 * total * taps * group,
        where,
        *lows,
        *conv,
    )
    hat_two, scale_two, low_two, hat_three, scale_three, pooled = kernel(
        functools.partial(stage_two, dims),
        [wide_f32, thin_f32, wide_bf16, wide_f32, thin_f32, quarter],
        [SM] + [VM] * 5 + [HB] * 4,
        [whole, pltpu.VMEM((width // 128, patches // 2, 128), F32), DMA((32,))],
        matmul,
        square + 24 * patches * width,
        where,
        *row_scatter(mine, near, away),
        x,
        norms,
        *lasts,
    )
    pools = gather_row(pooled)
    quarter_f32, near_quarter = shape((count, width), F32), shape((2, count, width), BF16)
    *shown, grad_low, mine, near, away = kernel(
        functools.partial(readout, slots),
        [quarter] * 4 + [wide_bf16, quarter_f32, near_quarter, quarter_f32],
        [SM] + [VM] * 9 + [HB] * (RING + 1),
        [pltpu.VMEM((RING, outs, width), BF16), DMA((RING + 1,))],
        2 * matmul,
        square + 12 * patches * width,
        where,
        *pools,
        *cots,
        norms,
        *read,
    )

    grad_three, grad_two, pool_sum, sums = kernel(
        functools.partial(stage_two_back, dims),
        [wide_bf16, wide_bf16, quarter_f32, shape((8, width), F32)],
        [SM] + [VM] * 8 + [HB] * 4,
        [whole, pltpu.VMEM((width // 128, patches // 2, 128), F32), DMA((32,))],
        matmul,
        square + 14 * patches * width,
        where,
        *row_scatter(mine, near, away),
        hat_three,
        scale_three,
        hat_two,
        scale_two,
        norms,
        *lasts,
    )
    grads = gather_row(grad_two)
    read_terms = kernel(
        readout_terms,
        shape((RING, outs + 16, width), BF16),
        [SM] + [VM] * 5,
        [pltpu.VMEM((RING, outs, width), F32)],
        matmul,
        2 * square,
        where,
        grad_low,
        *pools,
    )
    cut_read = outs // 2 + 8
    read_sum = ring_scatter(
        read_terms, lambda v: v[:cut_read], lambda v: v[cut_read:], lambda a, b: jnp.concatenate([a, b], axis=0)
    )
    read_grad, bias_row = read_sum[:outs].T, read_sum[outs]
    bias_grad = lax.dynamic_slice_in_dim(bias_row, dp * outs, outs)
    shown = exchange_row(shown)
    readout_out = kernel(
        join_columns,
        shape((count, 4 * width), BF16),
        [SM] + [VM] * 4,
        [],
        0,
        16 * count * width,
        where,
        *shown,
    ).reshape(slots, band // 2, cols // 2, 4 * width)

    wgrad = kernel(
        functools.partial(conv_terms, full),
        shape((RING, taps, own, width), BF16),
        [SM] + [VM] * 5,
        [pltpu.VMEM((total, width), BF16)],
        9 * matmul,
        18 * square,
        where,
        spans,
        *grads,
    )
    conv_grad = ring_scatter(
        wgrad,
        lambda v: v[:, : own // 2],
        lambda v: v[:, own // 2 :],
        lambda a, b: jnp.concatenate([a, b], axis=1),
    ).reshape(3, 3, own, width)
    backs = kernel(
        functools.partial(conv_back, full),
        [piece] * 4,
        [SM] + [VM] * 4 + [HB] * (RING + 1),
        [
            conv_scratch,
            pltpu.VMEM((total, width), BF16),
            pltpu.VMEM((3, slots, pad_rows, group), F32),
            pltpu.VMEM((total, group), BF16),
            DMA((RING + 1,)),
        ],
        9 * matmul,
        9 * square + 12 * patches * width,
        where,
        *grads,
        *conv,
    )
    backs = exchange_row(backs)
    block = (RING, own, width)
    last_own, last_near, last_far = kernel(
        last_terms,
        [shape(block, F32), shape((2,) + block, BF16), shape(block, F32)],
        [SM, VM, VM],
        [pltpu.VMEM((RING, 4, own, width), F32)],
        matmul,
        3 * square,
        where,
        low_two,
        grad_three,
    )
    block = (RING, own + 16, width)
    grad_one, first_own, first_near, first_far = kernel(
        stage_one_back,
        [wide_bf16, shape(block, F32), shape((2,) + block, BF16), shape(block, F32)],
        [SM] + [VM] * 9,
        [pltpu.VMEM((patches, width), BF16), pltpu.VMEM((RING, 4, own, width), F32)],
        matmul,
        3 * square + 8 * patches * width,
        where,
        *backs,
        hat_one,
        scale_one,
        norms,
        x,
        sums,
    )
    image_grad = kernel(
        functools.partial(image_back, dims),
        wide_bf16,
        [SM, VM, VM] + [HB] * 4,
        [whole, pltpu.VMEM((width // 128, patches // 2, 128), F32), DMA((32,))],
        matmul,
        square + 8 * patches * width,
        where,
        grad_one,
        pool_sum,
        *firsts,
    ).reshape(slots, band, cols, width)
    add = lambda parts: sum(part.astype(F32) for part in parts)
    firsts_sum = add(row_scatter(first_own, first_near, first_far))
    lasts_sum = add(row_scatter(last_own, last_near, last_far))
    tail = ring_scatter(
        jnp.concatenate([firsts_sum, lasts_sum], axis=1).astype(BF16),
        lambda v: v[:cut],
        lambda v: v[cut:],
        lambda a, b: jnp.concatenate([a, b], axis=0),
    )
    first_grad = tail[:own].reshape(own, 4, RING, own).transpose(0, 2, 1, 3).reshape(own, width)
    last_grad = tail[cut:]
    swapped = lax.dynamic_slice(tail, (own, (row * RING + dp) * own), (2, own))
    plain = lax.dynamic_slice(tail, (own + 2, (dp * 4 + row) * own), (4, own))
    norm_grad = jnp.concatenate([swapped, plain], axis=0)
    return (
        readout_out,
        image_grad,
        first_grad,
        conv_grad,
        last_grad,
        norm_grad,
        read_grad,
        bias_grad,
    )


def per_device(*arrays):
    if lax.axis_size("dp") == RING and lax.axis_size("row") == 4:
        return ringed(*arrays)
    return generic(*arrays)


def solution(mesh):
    return jax.shard_map(
        per_device,
        mesh=mesh,
        in_specs=(
            P("dp", "row", None, None),
            P(("dp", "row"), None),
            P(None, None, ("dp", "row"), None),
            P(("dp", "row"), None),
            P(None, ("dp", "row")),
            P(None, ("dp", "row")),
            P(("dp", "row")),
            P("dp", "row", None, None),
            P("dp"),
        ),
        out_specs=(
            P("dp", "row", None, None),
            P("dp", "row", None, None),
            P(("dp", "row"), None),
            P(None, None, ("dp", "row"), None),
            P(("dp", "row"), None),
            P(None, ("dp", "row")),
            P(None, ("dp", "row")),
            P(("dp", "row")),
        ),
        check_vma=False,
    )
```

```python
import functools

import jax
import jax.numpy as jnp
from jax import lax
from jax.experimental import pallas as pl
from jax.experimental.pallas import tpu as pltpu

from jax.sharding import PartitionSpec as P

eps = 1e-06
F32 = jnp.float32
BF16 = jnp.bfloat16
RING = 8


def ring_order(n):
    return list(range(0, n, 2)) + list(range(n - 1, 0, -2))


def ring_pairs(n):
    order = ring_order(n)
    right = [(order[i], order[(i + 1) % n]) for i in range(n)]
    left = [(b, a) for a, b in right]
    return right, left


def ring_index(n, step):
    me = lax.axis_index("dp")
    place = jnp.where(me % 2 == 0, me // 2, n - 1 - me // 2)
    place = (place + step) % n
    return jnp.where(place < n // 2, 2 * place, 2 * (n - 1 - place) + 1)


def gather_dp(x, n):
    return lax.all_gather(x, "dp", axis=0, tiled=False)


def scatter_dp(parts, n):
    return lax.psum_scatter(parts.astype(F32), "dp", scatter_dimension=0, tiled=False)


def swap_row(x, q):
    return lax.ppermute(x, "row", [(i, i ^ q) for i in range(4)])


def gather_row(x):
    two = swap_row(x, 2)
    one = swap_row(x, 1)
    return [x, one, two, swap_row(two, 1)]


def exchange_row(pieces):
    return [pieces[0]] + [swap_row(pieces[q], q) for q in (1, 2, 3)]


def scatter_row(pieces):
    near = swap_row(jnp.stack([pieces[1], pieces[3]]).astype(BF16), 1).astype(F32)
    mine = pieces[0].astype(F32) + near[0]
    other = (pieces[2].astype(F32) + near[1]).astype(BF16)
    return mine + swap_row(other, 2).astype(F32)


def pick(choices, index):
    value = choices[0]
    for i in range(1, len(choices)):
        value = jnp.where(index == i, choices[i], value)
    return value


def dot(left, right):
    return jnp.dot(left, right, preferred_element_type=F32)


def dot_t(left, right):
    return lax.dot_general(left, right, (((1,), (1,)), ((), ())), preferred_element_type=F32)


def t_dot(left, right):
    return lax.dot_general(left, right, (((0,), (0,)), ((), ())), preferred_element_type=F32)


def normalize(value):
    centred = value - jnp.mean(value, axis=-1, keepdims=True)
    scale = lax.rsqrt(jnp.mean(centred * centred, axis=-1, keepdims=True) + eps)
    return centred * scale, scale


def norm_backward(grad_out, normed, scale, gain):
    weighted = grad_out * gain
    return scale * (
        weighted
        - jnp.mean(weighted, axis=-1, keepdims=True)
        - normed * jnp.mean(weighted * normed, axis=-1, keepdims=True)
    )


def silu_slope(value):
    gate = jax.nn.sigmoid(value)
    return gate * (1.0 + value * (1.0 - gate))


def gelu_slope(value):
    return (
        0.5 * (1.0 + lax.erf(value * 0.7071067811865476))
        + value * jnp.exp(-0.5 * value * value) * 0.3989422804014327
    )


def columns(value):
    cols = value.shape[2]
    wide = jnp.pad(value, ((0, 0), (1, 1), (1, 1), (0, 0)))
    return jnp.concatenate([wide[:, :, v : v + cols] for v in range(3)], axis=3)


def generic(
    images,
    first_weight,
    conv_weight,
    last_weight,
    norm_rows,
    read_weight,
    read_bias,
    cotangent,
    live_count,
):
    n, ranks = lax.axis_size("dp"), lax.axis_size("row")
    row = lax.axis_index("row")
    slots, band, cols, width = images.shape
    patches = slots * band * cols
    high = ranks * band
    own = first_weight.shape[0]
    group = n * own
    outs = read_weight.shape[1]
    rows_at = [row ^ q for q in range(ranks)]

    first_mine = first_weight.reshape(own, n, ranks, own).transpose(0, 2, 1, 3).reshape(own, width)
    small = jnp.concatenate([norm_rows.reshape(-1), read_bias])
    small = jnp.pad(small, (0, 8 * width - small.shape[0])).reshape(8, width)
    first_ring = gather_dp(jnp.concatenate([first_mine, small], axis=0), n)
    first_parts = gather_row(first_ring)

    def interleave(parts):
        whole = jnp.zeros((n, ranks) + parts[0].shape[1:], parts[0].dtype)
        for q in range(ranks):
            whole = lax.dynamic_update_slice(whole, parts[q][:, None], (0, rows_at[q], 0, 0))
        return whole

    first_all = interleave(first_parts)
    first_full = first_all[:, :, :own].reshape(width, width)
    norms = first_all[:, :, own].reshape(n, ranks, width)[:, :, : 6 * own]
    norms = norms.reshape(n, ranks, 6, own).astype(F32)
    norm_vals = norms.transpose(2, 0, 1, 3).reshape(6, width)
    norm_swap = norms.transpose(2, 1, 0, 3).reshape(6, width)
    bias_mine = first_ring[:, own, 6 * own : 6 * own + outs].reshape(n * outs).astype(F32)

    conv_taps = [gather_dp(conv_weight[u].reshape(3 * own, width), n) for u in range(3)]
    conv_taps = [
        tap.reshape(n, 3, own, width).transpose(1, 0, 2, 3).reshape(3 * group, width) for tap in conv_taps
    ]
    last_full = interleave(gather_row(gather_dp(last_weight, n))).reshape(width, width)
    read_mine = gather_dp(read_weight.T, n).reshape(n * outs, width)

    cot = cotangent.reshape(-1, n, ranks, outs)
    cot = exchange_row([pick([cot[:, :, i] for i in range(ranks)], rows_at[q]) for q in range(ranks)])
    cot = jnp.concatenate(cot, axis=0).reshape(-1, n * outs)

    flat_in = images.reshape(patches, width)
    hat_one, scale_one = normalize(dot(flat_in, first_full))
    pre_one = hat_one * norm_swap[0] + norm_swap[1]
    low_one = jax.nn.silu(pre_one).astype(BF16)
    split = [low_one[:, i * group : (i + 1) * group] for i in range(ranks)]
    bands = exchange_row([pick(split, rows_at[q]) for q in range(ranks)])

    def stack_bands(pieces):
        whole = jnp.zeros((slots, ranks, band, cols, pieces[0].shape[-1]), pieces[0].dtype)
        for q in range(ranks):
            piece = pieces[q].reshape(slots, 1, band, cols, -1)
            whole = lax.dynamic_update_slice(whole, piece, (0, rows_at[q], 0, 0, 0))
        return whole.reshape(slots, high, cols, -1)

    def take_bands(value):
        value = value.reshape(slots, ranks, band * cols, -1)
        return [
            lax.dynamic_index_in_dim(value, rows_at[q], 1, keepdims=False).reshape(patches, -1)
            for q in range(ranks)
        ]

    wide_one = columns(stack_bands(bands))
    slabs = [wide_one[:, u : u + high].reshape(slots * high * cols, 3 * group) for u in range(3)]
    act_two = dot(slabs[0], conv_taps[0]) + dot(slabs[1], conv_taps[1]) + dot(slabs[2], conv_taps[2])
    hat_two, scale_two = normalize(scatter_row(take_bands(act_two)))
    pre_two = hat_two * norm_vals[2] + norm_vals[3]
    low_two = jax.nn.silu(pre_two).astype(BF16)
    hat_three, scale_three = normalize(dot(low_two, last_full))
    summed = flat_in.astype(F32) + (hat_three * norm_vals[4] + norm_vals[5])
    pooled = jnp.mean(summed.reshape(slots, band // 2, 2, cols // 2, 2, width), axis=(2, 4)).astype(BF16)
    pooled = pooled.reshape(-1, width)
    pools = jnp.concatenate(gather_row(pooled), axis=0)
    logits = dot_t(pools, read_mine) + bias_mine
    mask = (jnp.arange(slots, dtype=jnp.int32) < live_count[0]).astype(F32)
    mask = jnp.broadcast_to(mask[None, :, None], (ranks, slots, pooled.shape[0] // slots)).reshape(-1, 1)
    shown = (jax.nn.gelu(logits, approximate=False) * mask).astype(BF16)
    shown = exchange_row(jnp.split(shown, ranks, axis=0))
    readout = jnp.zeros((pooled.shape[0], n, ranks, outs), BF16)
    for q in range(ranks):
        readout = lax.dynamic_update_slice(
            readout, shown[q].reshape(-1, n, 1, outs), (0, 0, rows_at[q], 0)
        )
    readout_out = readout.reshape(slots, band // 2, cols // 2, n * ranks * outs)

    grad_low = (cot.astype(F32) * mask * gelu_slope(logits)).astype(BF16)
    read_terms = t_dot(grad_low, pools).reshape(n, outs, width)
    bias_terms = jnp.sum(grad_low.astype(F32), axis=0).reshape(n, 1, outs)
    bias_terms = jnp.pad(bias_terms, ((0, 0), (0, 7), (0, width - outs)))
    read_sum = scatter_dp(jnp.concatenate([read_terms, bias_terms], axis=1), n)
    read_grad, bias_grad = read_sum[:outs].T, read_sum[outs, :outs]
    grad_pool = scatter_row(jnp.split(dot(grad_low, read_mine), ranks, axis=0))
    grad_sum = (
        jnp.broadcast_to(
            grad_pool.reshape(slots, band // 2, 1, cols // 2, 1, width),
            (slots, band // 2, 2, cols // 2, 2, width),
        )
        * 0.25
    ).reshape(-1, width)
    gain_three = jnp.sum(grad_sum * hat_three, axis=0)
    shift_three = jnp.sum(grad_sum, axis=0)
    grad_three = norm_backward(grad_sum, hat_three, scale_three, norm_vals[4]).astype(BF16)
    grad_pre_two = dot_t(grad_three, last_full) * silu_slope(pre_two)
    gain_two = jnp.sum(grad_pre_two * hat_two, axis=0)
    shift_two = jnp.sum(grad_pre_two, axis=0)
    grad_two = norm_backward(grad_pre_two, hat_two, scale_two, norm_vals[2]).astype(BF16)
    grad_full = stack_bands(gather_row(grad_two))
    grad_flat = grad_full.reshape(-1, width)

    def row_sums(terms):
        terms = terms.reshape(n, ranks, -1, width)
        return scatter_row(
            [lax.dynamic_index_in_dim(terms, rows_at[q], 1, keepdims=False) for q in range(ranks)]
        )

    conv_grad = []
    for u in range(3):
        terms = t_dot(slabs[u], grad_flat).reshape(3, n, own, width).transpose(1, 0, 2, 3)
        conv_grad.append(scatter_dp(terms.reshape(n, 3 * own, width), n).reshape(3, own, width))
    conv_grad = jnp.stack(conv_grad)
    wide_grad = jnp.pad(grad_full, ((0, 0), (1, 1), (1, 1), (0, 0)))
    grad_mid = jnp.zeros((slots * high * cols, group), F32)
    for u in range(3):
        for v in range(3):
            slab = wide_grad[:, 2 - u : 2 - u + high, 2 - v : 2 - v + cols].reshape(-1, width)
            grad_mid = grad_mid + dot_t(slab, conv_taps[u][v * group : (v + 1) * group])
    pieces = exchange_row(take_bands(grad_mid.astype(BF16)))
    grad_low_one = jnp.concatenate(
        [pick([pieces[i ^ q] for i in range(ranks)], row) for q in range(ranks)], axis=1
    ).astype(F32)
    last_sum = scatter_dp(row_sums(t_dot(low_two, grad_three)), n)

    grad_pre_one = grad_low_one * silu_slope(pre_one)
    gain_one = jnp.sum(grad_pre_one * hat_one, axis=0)
    shift_one = jnp.sum(grad_pre_one, axis=0)
    grad_one = norm_backward(grad_pre_one, hat_one, scale_one, norm_swap[0]).astype(BF16)
    image_grad = (grad_sum + dot_t(grad_one, first_full)).astype(BF16)
    image_grad = image_grad.reshape(slots, band, cols, width)

    swapped = jnp.stack([gain_one, shift_one]).reshape(2, ranks, n, own).transpose(2, 1, 0, 3)
    plain = jnp.stack([gain_two, shift_two, gain_three, shift_three])
    plain = plain.reshape(4, n, ranks, own).transpose(1, 2, 0, 3)
    norm_terms = jnp.concatenate([swapped, plain], axis=2).reshape(n, ranks, 1, 6 * own)
    norm_terms = jnp.pad(norm_terms, ((0, 0), (0, 0), (0, 7), (0, width - 6 * own)))
    first_terms = t_dot(flat_in, grad_one).reshape(n, ranks, own, width)
    first_sum = scatter_dp(row_sums(jnp.concatenate([first_terms, norm_terms], axis=2)), n)
    norm_grad = first_sum[own, : 6 * own].reshape(6, own)
    first_grad = first_sum[:own].reshape(own, ranks, n, own).transpose(0, 2, 1, 3).reshape(own, width)
    return (
        readout_out,
        image_grad,
        first_grad,
        conv_grad,
        last_sum,
        norm_grad,
        read_grad,
        bias_grad,
    )


VM = pl.BlockSpec(memory_space=pltpu.VMEM)
SM = pl.BlockSpec(memory_space=pltpu.SMEM)
HB = pl.BlockSpec(memory_space=pltpu.HBM)


def shape(dims, dtype):
    return jax.ShapeDtypeStruct(dims, dtype)


def kernel(body, outs, ins, scratch, flops, moved, *arrays, specs=None, room=24):
    return pl.pallas_call(
        body,
        out_shape=outs,
        in_specs=ins,
        out_specs=jax.tree.map(lambda _: VM, outs) if specs is None else specs,
        scratch_shapes=scratch,
        cost_estimate=pl.CostEstimate(flops=flops // 64, bytes_accessed=moved // 64, transcendentals=0),
        compiler_params=pltpu.CompilerParams(vmem_limit_bytes=room << 20),
    )(*arrays)


def at_row(where, q):
    return where[0] ^ q


def start_all(copies):
    for copy in copies:
        copy.start()


def wait_all(copies):
    for copy in copies:
        copy.wait()


def copies_of(pairs, sems):
    return [pltpu.make_async_copy(a, b, sems.at[i]) for i, (a, b) in enumerate(pairs)]


def hop(x, turn):
    right, left = ring_pairs(RING)
    return lax.ppermute(x, "dp", right if turn else left)


def gather_step(state, step, low=None, high=None):
    pieces, a, b = state
    pieces = list(pieces)
    if step < RING // 2:
        a, b = hop(a, True), hop(b, False)
        pieces[RING - step], pieces[step] = a, b
    else:
        pieces[step] = (hop(low(a), True), hop(high(b), False))
    return pieces, a, b


def gather_state(x):
    return [x] * RING, x, x


def scatter_step(low, high, terms, a, b, step):
    half = RING // 2
    if step == half:
        return hop(low, True), hop(high, False)
    right, left = terms[step].astype(F32), terms[RING - step].astype(F32)
    if step == half - 1:
        cut = low.shape[0]
        right = jnp.concatenate([right[:cut] + a.astype(F32), right[cut:]], axis=0)
        left = jnp.concatenate([left[:cut], left[cut:] + b.astype(F32)], axis=0)
    else:
        right, left = right + a.astype(F32), left + b.astype(F32)
    return hop(right.astype(BF16), True), hop(left.astype(BF16), False)


def scatter_end(terms, a, b):
    return terms[0].astype(F32) + a.astype(F32) + b.astype(F32)


def fence(*values):
    return lax.optimization_barrier(values)


def unpack_first(where, firsts, weight, sems):
    pairs = []
    for q in range(4):
        for k in range(RING):
            pairs.append((firsts[q].at[k, pl.ds(0, weight.shape[2])], weight.at[where[2 + k], at_row(where, q)]))
    return copies_of(pairs, sems)


def center(value):
    mean = jnp.mean(value, axis=-1, keepdims=True)
    gap = value - mean
    scale = lax.rsqrt(jnp.mean(gap * gap, axis=-1, keepdims=True) + eps)
    return gap * scale, scale


def flat_pieces(pieces):
    half = RING // 2
    return [p[0] if k == half else p for k, p in enumerate(pieces)] + [pieces[half][1]]


def stage_one(where, x, f0, f1, f2, f3, small, hat, scale, s0, s1, s2, s3, norms, weight, low, sems):
    copies = unpack_first(where, (f0, f1, f2, f3), weight, sems)
    start_all(copies)
    width = x.shape[1]
    total = jnp.zeros((8, width), F32)
    bias = total
    for q in range(4):
        for k in range(RING):
            block = small[q, k].astype(F32)
            total = total + block
            if q == 0:
                bias = bias + block
    line = lax.broadcasted_iota(jnp.int32, (8, width), 0)
    table = jnp.where(line == 6, bias, total)
    norms[...] = table
    wait_all(copies)
    act = dot(x[...], weight[...].reshape(width, width))
    normed, root = center(act)
    hat[...] = normed
    scale[...] = root
    pre = normed * norms[0:1, :] + norms[1:2, :]
    low[...] = (pre * jax.nn.sigmoid(pre)).astype(BF16)
    part = width // 4
    for q, out in enumerate((s0, s1, s2, s3)):
        out[...] = low[:, pl.ds(pl.multiple_of(at_row(where, q) * part, part), part)]


def conv_copies(where, one, two, weight, sems):
    (pieces, at), own, far = one, weight.shape[2], RING // 2
    pairs = []
    for k in range(RING):
        pairs.append((pieces[k].at[pl.ds(0 if k == far else at, own)], weight.at[0, where[2 + k]]))
        if k == far:
            number = two[far].shape[0]
            pairs.append((two[far], weight.at[pl.ds(1, number), where[2 + k]]))
            pairs.append((two[RING], weight.at[pl.ds(1 + number, number), where[2 + k]]))
        else:
            pairs.append((two[k], weight.at[pl.ds(1, two[k].shape[0]), where[2 + k]]))
    return copies_of(pairs, sems)


def conv_forward(dims, at_one, first, where, s0, s1, s2, s3, *refs):
    slots, rows, cols = dims
    own, near, spans, weight, pad, moved, wide, sems, done = refs[2 * RING + 1 :]
    copies = conv_copies(where, (refs[:RING], at_one), refs[RING : 2 * RING + 1], weight, sems)
    start_all(copies)
    group = s0.shape[1]
    patches = rows * cols
    band = patches // 4
    pad[...] = jnp.zeros_like(pad)
    for q, piece in enumerate((s0, s1, s2, s3)):
        for i in range(slots):
            at = pl.multiple_of(cols + 8 + at_row(where, q) * band, 8)
            pad[i, pl.ds(at, band), :] = piece[i * band : (i + 1) * band, :].astype(F32)
    for v in range(3):
        for i in range(slots):
            shifted = pad[i, 8 + v - 1 : 8 + v - 1 + patches + 2 * cols, :]
            if v != 1:
                col = lax.broadcasted_iota(jnp.int32, shifted.shape, 0) % cols
                shifted = jnp.where(col == (0 if v == 0 else cols - 1), 0.0, shifted)
            moved[i] = shifted
        for q in range(2):
            for i in range(slots):
                for u in range(3):
                    at = pl.multiple_of(at_row(where, first + q) * band + u * cols, 8)
                    t = u * 3 + v
                    here = (q * slots + i) * band
                    wide[here : here + band, t * group : (t + 1) * group] = moved[i, pl.ds(at, band), :].astype(BF16)
    keep = pltpu.make_async_copy(wide, spans, done)
    keep.start()
    wait_all(copies)
    width = own.shape[1]
    chunk = 256
    patches = slots * band

    @pl.loop(0, width // chunk)
    def _(j):
        lanes = pl.ds(pl.multiple_of(j * chunk, chunk), chunk)
        terms = dot(wide[...], weight[:, :, :, lanes].reshape(-1, chunk))
        own[:, lanes] = terms[:patches]
        near[:, lanes] = terms[patches:].astype(BF16)

    keep.wait()


def stage_two(dims, where, own, near, cross, x, norms, l0, l1, l2, l3, hat_two, scale_two, low, hat, scale, pooled, weight, pairs, sems):
    slots, rows, cols = dims
    copies = unpack_first(where, (l0, l1, l2, l3), weight, sems)
    start_all(copies)
    width = x.shape[1]
    act = own[...] + near[...].astype(F32) + cross[...].astype(F32)
    normed, root = center(act)
    hat_two[...] = normed
    scale_two[...] = root
    pre = normed * norms[2:3, :] + norms[3:4, :]
    low[...] = (pre * jax.nn.sigmoid(pre)).astype(BF16)
    wait_all(copies)
    normed, root = center(dot(low[...], weight[...].reshape(width, width)))
    hat[...] = normed
    scale[...] = root
    y = x[...].astype(F32) + (normed * norms[4:5, :] + norms[5:6, :])
    y = jnp.sum(y.reshape(slots * rows // 2, 2, cols, width), axis=1).reshape(-1, width)
    count = pooled.shape[0]
    for g in range(pairs.shape[0]):
        lanes = slice(g * 128, (g + 1) * 128)
        pairs[g] = y[:, lanes]
        pooled[:, lanes] = (
            0.25 * (pairs[g, pl.ds(0, count, stride=2), :] + pairs[g, pl.ds(1, count, stride=2), :])
        ).astype(BF16)


def read_copies(where, pieces, weight, sems):
    half = RING // 2
    pairs = []
    for k in range(RING):
        if k == half:
            rows = pieces[half].shape[0]
            pairs.append((pieces[half], weight.at[where[2 + k], pl.ds(0, rows)]))
            pairs.append((pieces[RING], weight.at[where[2 + k], pl.ds(rows, rows)]))
        else:
            pairs.append((pieces[k], weight.at[where[2 + k]]))
    return copies_of(pairs, sems)


def readout(slots, where, p0, p1, p2, p3, c0, c1, c2, c3, norms, *refs):
    pieces = refs[: RING + 1]
    o0, o1, o2, o3, low, own, near, far, weight, sems = refs[RING + 1 :]
    copies = read_copies(where, pieces, weight, sems)
    start_all(copies)
    count, width = p0.shape
    table = jnp.concatenate([p[...] for p in (p0, p1, p2, p3)], axis=0)
    line = lax.broadcasted_iota(jnp.int32, (count, width), 0)
    mask = jnp.where(line // (count // slots) < where[1], 1.0, 0.0)
    wait_all(copies)
    whole = weight[...].reshape(-1, width)
    logits = dot_t(table, whole) + norms[6:7, :]
    for q, (cot, out) in enumerate(((c0, o0), (c1, o1), (c2, o2), (c3, o3))):
        z = logits[q * count : (q + 1) * count]
        phi = 0.5 * (1.0 + lax.erf(z * 0.7071067811865476))
        out[...] = (z * phi * mask).astype(BF16)
        slope = phi + z * jnp.exp(-0.5 * z * z) * 0.3989422804014327
        low[q * count : (q + 1) * count, :] = (cot[...].astype(F32) * mask * slope).astype(BF16)
    back = dot(low[...], whole)
    own[...] = back[:count]
    near[0] = back[count : 2 * count].astype(BF16)
    far[...] = back[2 * count : 3 * count]
    near[1] = back[3 * count :].astype(BF16)


def readout_terms(where, low, p0, p1, p2, p3, upper, lower, out, terms):
    width = p0.shape[1]
    table = jnp.concatenate([p[...] for p in (p0, p1, p2, p3)], axis=0)
    terms[...] = t_dot(low[...], table).reshape(terms.shape)
    bias = jnp.sum(low[...].astype(F32), axis=0, keepdims=True)
    rows = terms.shape[1]
    for k in range(RING):
        out[k, :rows, :] = terms[where[2 + k]].astype(BF16)
        out[k, rows:, :] = jnp.broadcast_to(bias, (out.shape[1] - rows, width)).astype(BF16)
    upper[...] = out[RING // 2, : upper.shape[0]]
    lower[...] = out[RING // 2, upper.shape[0] :]


def spread(pairs, grad, dims):
    slots, rows, cols = dims
    count, width = grad.shape
    for g in range(pairs.shape[0]):
        lanes = slice(g * 128, (g + 1) * 128)
        pairs[g, pl.ds(0, count, stride=2), :] = grad[:, lanes]
        pairs[g, pl.ds(1, count, stride=2), :] = grad[:, lanes]
    half = slots * rows // 2
    both = jnp.concatenate([pairs[g] for g in range(pairs.shape[0])], axis=1)
    both = jnp.broadcast_to(both.reshape(half, 1, cols, width), (half, 2, cols, width))
    return both.reshape(-1, width) * 0.25


def back_norm(grad, normed, root, gain):
    weighted = grad * gain
    return root * (
        weighted
        - jnp.mean(weighted, axis=-1, keepdims=True)
        - normed * jnp.mean(weighted * normed, axis=-1, keepdims=True)
    )


def total_rows(value):
    return jnp.sum(value, axis=0, keepdims=True)


def stage_two_back(dims, where, own, near, cross, hat, scale, hat_two, scale_two, norms, l0, l1, l2, l3, grad_three, grad_two, pool_sum, sums, weight, pairs, sems):
    copies = unpack_first(where, (l0, l1, l2, l3), weight, sems)
    start_all(copies)
    width = hat.shape[1]
    grad = own[...] + near[...].astype(F32) + cross[...].astype(F32)
    pool_sum[...] = grad
    gy = spread(pairs, grad, dims)
    sums[...] = jnp.zeros_like(sums)
    sums[4:5, :] = total_rows(gy * hat[...])
    sums[5:6, :] = total_rows(gy)
    grad_three[...] = back_norm(gy, hat[...], scale[...], norms[4:5, :]).astype(BF16)
    wait_all(copies)
    gs = dot_t(grad_three[...], weight[...].reshape(width, width))
    pre = hat_two[...] * norms[2:3, :] + norms[3:4, :]
    gn = gs * silu_slope(pre)
    sums[2:3, :] = total_rows(gn * hat_two[...])
    sums[3:4, :] = total_rows(gn)
    grad_two[...] = back_norm(gn, hat_two[...], scale_two[...], norms[2:3, :]).astype(BF16)


def last_terms(where, low, grad, own, near, far, terms):
    terms[...] = t_dot(low[...], grad[...]).reshape(terms.shape)
    for k in range(RING):
        own[k] = terms[where[2 + k], at_row(where, 0)]
        near[0, k] = terms[where[2 + k], at_row(where, 1)].astype(BF16)
        far[k] = terms[where[2 + k], at_row(where, 2)]
        near[1, k] = terms[where[2 + k], at_row(where, 3)].astype(BF16)


def stack_grad(dims, where, pieces, whole):
    slots, rows, cols = dims
    band = rows * cols // 4
    for q, piece in enumerate(pieces):
        for i in range(slots):
            at = pl.multiple_of(i * rows * cols + at_row(where, q) * band, 16)
            whole[pl.ds(at, band), :] = piece[i * band : (i + 1) * band, :]


def conv_terms(first, number, next_to, where, here, there, g0, g1, g2, g3, *refs):
    parts, (far, side, out, one, two) = refs[:-5], refs[-5:]
    count = g0.shape[0]
    one[:count], one[count:], two[:count], two[count:] = g0[...], g1[...], g2[...], g3[...]
    rows, width = out.shape[2:]
    group = RING * rows

    @pl.loop(0, number)
    def _(t):
        lanes = pl.ds(pl.multiple_of((first + t) * group, group), group)
        terms = t_dot(here[:, lanes], one[...]) + t_dot(there[:, lanes], two[...])
        terms = terms.astype(BF16).reshape(RING, rows, width)
        for k in range(RING):
            out[where[2 + RING + k], t] = terms[k]

    if parts:
        own, near, cross = parts
        out[:, number] = (own[...] + near[0].astype(F32) + cross[...].astype(F32)).astype(BF16)
    far[...] = out[RING // 2]
    side[...] = out[next_to]


def conv_back(dims, at_one, where, g0, g1, g2, g3, *refs):
    slots, rows, cols = dims
    o0, o1, o2, o3, weight, whole, held, low, sems = refs[2 * RING + 1 :]
    copies = conv_copies(where, (refs[:RING], at_one), refs[RING : 2 * RING + 1], weight, sems)
    start_all(copies)
    stack_grad(dims, where, (g0, g1, g2, g3), whole)
    patches = rows * cols
    band = patches // 4
    group = o0.shape[1]
    width = whole.shape[1]
    held[...] = jnp.zeros_like(held)
    wait_all(copies)
    for u in range(3):
        for v in range(3):
            part = dot_t(whole[...], weight[u * 3 + v].reshape(group, width))
            for i in range(slots):
                held[v, i, 8 + u * cols : 8 + u * cols + patches, :] += part[i * patches : (i + 1) * patches]
    col = lax.broadcasted_iota(jnp.int32, (patches, group), 0) % cols
    for i in range(slots):
        value = held[1, i, 8 + cols : 8 + cols + patches, :]
        value += jnp.where(col == cols - 1, 0.0, held[0, i, 9 + cols : 9 + cols + patches, :])
        value += jnp.where(col == 0, 0.0, held[2, i, 7 + cols : 7 + cols + patches, :])
        low[i * patches : (i + 1) * patches, :] = value.astype(BF16)
    for q, out in enumerate((o0, o1, o2, o3)):
        for i in range(slots):
            at = pl.multiple_of(i * patches + at_row(where, q) * band, 16)
            out[i * band : (i + 1) * band, :] = low[pl.ds(at, band), :]


def stage_one_back(where, b0, b1, b2, b3, hat, scale, norms, x, sums, grad_one, own, near, far, low, terms):
    width = hat.shape[1]
    part = width // 4
    for q, piece in enumerate((b0, b1, b2, b3)):
        low[:, pl.ds(pl.multiple_of(at_row(where, q) * part, part), part)] = piece[...]
    pre = hat[...] * norms[0:1, :] + norms[1:2, :]
    gn = low[...].astype(F32) * silu_slope(pre)
    line = lax.broadcasted_iota(jnp.int32, (8, width), 0)
    tail = jnp.where(line == 0, total_rows(gn * hat[...]), jnp.where(line == 1, total_rows(gn), sums[...]))
    tail = jnp.concatenate([tail, tail], axis=0)
    grad_one[...] = back_norm(gn, hat[...], scale[...], norms[0:1, :]).astype(BF16)
    terms[...] = t_dot(x[...], grad_one[...]).reshape(terms.shape)
    rows = terms.shape[2]
    for k in range(RING):
        own[k, :rows] = terms[k, at_row(where, 0)]
        near[0, k, :rows] = terms[k, at_row(where, 1)].astype(BF16)
        far[k, :rows] = terms[k, at_row(where, 2)]
        near[1, k, :rows] = terms[k, at_row(where, 3)].astype(BF16)
        own[k, rows:] = tail
        near[0, k, rows:] = tail.astype(BF16)
        far[k, rows:] = tail
        near[1, k, rows:] = tail.astype(BF16)


def image_back(dims, where, grad_one, pool_sum, f0, f1, f2, f3, out, weight, pairs, sems):
    copies = unpack_first(where, (f0, f1, f2, f3), weight, sems)
    start_all(copies)
    width = grad_one.shape[1]
    gy = spread(pairs, pool_sum[...], dims)
    wait_all(copies)
    out[...] = (gy + dot_t(grad_one[...], weight[...].reshape(width, width))).astype(BF16)


def split_columns(where, x, o0, o1, o2, o3):
    lanes = x.shape[1] // (4 * RING)
    for q, out in enumerate((o0, o1, o2, o3)):
        for g in range(RING):
            at = pl.multiple_of((g * 4 + at_row(where, q)) * lanes, lanes)
            out[:, g * lanes : (g + 1) * lanes] = x[:, pl.ds(at, lanes)]


def join_columns(where, i0, i1, i2, i3, out):
    lanes = out.shape[1] // (4 * RING)
    for q, piece in enumerate((i0, i1, i2, i3)):
        for g in range(RING):
            at = pl.multiple_of((g * 4 + at_row(where, q)) * lanes, lanes)
            out[:, pl.ds(at, lanes)] = piece[:, g * lanes : (g + 1) * lanes]


def ringed(
    images,
    first_weight,
    conv_weight,
    last_weight,
    norm_rows,
    read_weight,
    read_bias,
    cotangent,
    live_count,
):
    dp, row = lax.axis_index("dp"), lax.axis_index("row")
    slots, band, cols, width = images.shape
    dims = (slots, band, cols)
    full = (slots, 4 * band, cols)
    patches = slots * band * cols
    count = patches // 4
    own = first_weight.shape[0]
    group = RING * own
    outs = read_weight.shape[1]
    taps = 9
    DMA = pltpu.SemaphoreType.DMA
    index = jnp.arange(18, dtype=jnp.int32)
    place_of = lambda d: jnp.where(d % 2 == 0, d // 2, RING - 1 - d // 2)
    place = (place_of(dp) + index - 2) % RING
    ahead = jnp.where(place < RING // 2, 2 * place, 2 * (RING - 1 - place) + 1)
    steps = (place_of(index - 10) - place_of(dp)) % RING
    where = jnp.where(index == 0, row, jnp.where(index == 1, live_count[0], jnp.where(index < 10, ahead, steps)))
    where = where.astype(jnp.int32)

    first_mine = first_weight.reshape(own, RING, 4, own).transpose(0, 2, 1, 3).reshape(own, width)
    lane = jnp.arange(width, dtype=jnp.int32)[None, :]
    tiled = jnp.tile(norm_rows, (1, width // own))
    at = jnp.where(jnp.arange(6)[:, None] < 2, row * RING + dp, dp * 4 + row)
    small = jnp.where(lane // own == at, tiled, 0).astype(BF16)
    bias = jnp.where(lane // outs == dp, jnp.tile(read_bias, width // outs)[None, :], 0).astype(BF16)
    small = jnp.concatenate([small, bias, jnp.zeros((1, width), BF16)], axis=0)
    first_mine = jnp.concatenate([first_mine, small], axis=0)
    conv = conv_weight.reshape(taps, own, width)
    quarter = shape((count, width), BF16)
    wide_f32, thin_f32, wide_bf16 = (
        shape((patches, width), F32),
        shape((patches, 1), F32),
        shape((patches, width), BF16),
    )
    quarter_f32, near_quarter = shape((count, width), F32), shape((2, count, width), BF16)
    piece = shape((patches, group), BF16)
    block = (RING, own, width)
    matmul = 2 * patches * width * width
    square = 2 * width * width
    whole = pltpu.VMEM((RING, 4, own, width), BF16)
    conv_scratch = pltpu.VMEM((taps, RING, own, width), BF16)
    total = 4 * patches
    pad_rows = full[1] * cols + 2 * cols + 16
    pair_scratch = pltpu.VMEM((width // 128, patches // 2, 128), F32)
    x = images.reshape(patches, width)

    far = RING // 2
    cut = 2 * own + 8
    low, high = lambda v: v[: own + 8], lambda v: v[own + 8 :]
    ring = jnp.concatenate([first_mine, last_weight, conv[0]], axis=0)
    ring = gather_step(gather_state(ring), 1)
    read = read_weight.T
    cots = cotangent.reshape(count, -1)
    ring, where, read, cots, x = fence(ring, where, read, cots, x)
    ring = gather_step(ring, 2)
    cots = kernel(split_columns, [quarter] * 4, [SM, VM], [], 0, 2 * count * 4 * width * 2, where, cots)
    ring, cots = fence(ring, cots)
    ring = gather_step(ring, 3)
    ring = fence(ring)[0]
    ring = gather_step(ring, 4, low, high)
    more, ring = fence(conv[1:], ring)
    ring = ring[0]
    firsts = jnp.stack([ring[far][0] if k == far else low(ring[k]) for k in range(RING)])
    lasts = jnp.stack([ring[far][1][:own] if k == far else ring[k][own + 8 : cut] for k in range(RING)])
    starts = [ring[far][1][own:] if k == far else ring[k] for k in range(RING)]
    more = gather_step(gather_state(more), 1)
    first_two, first_one = swap_row(firsts, 2), swap_row(firsts, 1)
    more, firsts, first_two, first_one, lasts = fence(more, firsts, first_two, first_one, lasts)
    more = gather_step(more, 2)
    firsts = [firsts, first_one, first_two, swap_row(first_two, 1)]
    smalls = jnp.stack([f[:, own:] for f in firsts])
    last_two, last_one = swap_row(lasts, 2), swap_row(lasts, 1)
    hat_one, scale_one, *lows, norms = kernel(
        stage_one,
        [wide_f32, thin_f32] + [piece] * 4 + [shape((8, width), F32)],
        [SM, VM] + [HB] * 4 + [VM],
        [whole, pltpu.VMEM((patches, width), BF16), DMA((32,))],
        matmul,
        square + 8 * patches * width,
        where,
        x,
        *firsts,
        smalls,
    )
    more, lows, lasts, last_two, last_one = fence(more, lows, lasts, last_two, last_one)
    more = gather_step(more, 3)
    lows = exchange_row(lows)
    lasts = [lasts, last_one, last_two, swap_row(last_two, 1)]
    more, lows, lasts = fence(more, lows, lasts)
    taps_half = (taps - 1) // 2
    more = gather_step(more, 4, lambda v: v[:taps_half], lambda v: v[taps_half:])
    weights = starts + flat_pieces(more[0])
    weights, read, cots = fence(weights, read, cots)

    def conv_half(first):
        return kernel(
            functools.partial(conv_forward, full, cut, first),
            [wide_f32, wide_bf16, shape((2 * patches, taps * group), BF16)],
            [SM] + [VM] * 4 + [HB] * (2 * RING + 1),
            [
                conv_scratch,
                pltpu.VMEM((slots, pad_rows, group), F32),
                pltpu.VMEM((slots, pad_rows - 16, group), F32),
                pltpu.VMEM((2 * patches, taps * group), BF16),
                DMA((2 * RING + 2,)),
                DMA,
            ],
            9 * matmul // 2,
            9 * square + 6 * patches * width + 4 * patches * taps * group,
            where,
            *lows,
            *weights,
            specs=[VM, VM, HB],
        )

    read = gather_step(gather_state(read), 1)
    cots = exchange_row(cots)
    away, near, spans_far = conv_half(2)
    away, near, read, cots = fence(away, near, read, cots)
    other = (away + swap_row(near, 1).astype(F32)).astype(BF16)
    other, lows, read = fence(other, lows, read)
    cross = swap_row(other, 2)
    read = gather_step(read, 2)
    mine, near, spans_near = conv_half(0)
    near, read = fence(near, read)
    near = swap_row(near, 1)
    mine, near, cross, read = fence(mine, near, cross, read)
    read = gather_step(read, 3)
    hat_two, scale_two, low_two, hat_three, scale_three, pooled = kernel(
        functools.partial(stage_two, dims),
        [wide_f32, thin_f32, wide_bf16, wide_f32, thin_f32, quarter],
        [SM] + [VM] * 5 + [HB] * 4,
        [whole, pair_scratch, DMA((32,))],
        matmul,
        square + 24 * patches * width,
        where,
        mine,
        near,
        cross,
        x,
        norms,
        *lasts,
    )
    pooled, read = fence(pooled, read)
    read = gather_step(read, 4, lambda v: v[: outs // 2], lambda v: v[outs // 2 :])
    pools = gather_row(pooled)
    *shown, grad_low, mine, near, away = kernel(
        functools.partial(readout, slots),
        [quarter] * 4 + [wide_bf16, quarter_f32, near_quarter, quarter_f32],
        [SM] + [VM] * 9 + [HB] * (RING + 1),
        [pltpu.VMEM((RING, outs, width), BF16), DMA((RING + 1,))],
        2 * matmul,
        square + 12 * patches * width,
        where,
        *pools,
        *cots,
        norms,
        *flat_pieces(read[0]),
    )

    near = swap_row(near, 1)
    other = (away + near[1].astype(F32)).astype(BF16)
    other, grad_low, near = fence(other, grad_low, near)
    cross = swap_row(other, 2)
    half_read = shape(((outs + 16) // 2, width), BF16)
    *read_far, read_terms = kernel(
        readout_terms,
        [half_read, half_read, shape((RING, outs + 16, width), BF16)],
        [SM] + [VM] * 5,
        [pltpu.VMEM((RING, outs, width), F32)],
        matmul,
        2 * square,
        where,
        grad_low,
        *pools,
    )
    cross, read_far, read_terms, near = fence(cross, read_far, read_terms, near)
    read_a, read_b = scatter_step(*read_far, read_terms, None, None, 4)
    grad_three, grad_two, pool_sum, sums = kernel(
        functools.partial(stage_two_back, dims),
        [wide_bf16, wide_bf16, quarter_f32, shape((8, width), F32)],
        [SM] + [VM] * 8 + [HB] * 4,
        [whole, pair_scratch, DMA((32,))],
        matmul,
        square + 14 * patches * width,
        where,
        mine,
        near[0],
        cross,
        hat_three,
        scale_three,
        hat_two,
        scale_two,
        norms,
        *lasts,
    )
    grad_three, grad_two, read_a, read_b = fence(grad_three, grad_two, read_a, read_b)
    grad_far, grad_next = swap_row(grad_two, 2), swap_row(grad_two, 1)
    read_a, read_b = scatter_step(*read_far, read_terms, read_a, read_b, 3)
    last_own, last_near, last_far = kernel(
        last_terms,
        [shape(block, F32), shape((2,) + block, BF16), shape(block, F32)],
        [SM, VM, VM],
        [pltpu.VMEM((RING, 4, own, width), F32)],
        matmul,
        3 * square,
        where,
        low_two,
        grad_three,
    )
    grad_two, grad_far, grad_next, last_near, last_far, read_a, read_b = fence(
        grad_two, grad_far, grad_next, last_near, last_far, read_a, read_b
    )
    grads = [grad_two, grad_next, grad_far, swap_row(grad_far, 1)]
    last_near = swap_row(last_near, 1)
    last_far = (last_far + last_near[1].astype(F32)).astype(BF16)
    grads, last_near, last_far = fence(grads, last_near, last_far)
    last_cross = swap_row(last_far, 2)
    read_a, read_b = scatter_step(*read_far, read_terms, read_a, read_b, 2)

    def weight_terms(first, number, next_to, parts):
        held = number + len(parts) // 3
        some = shape((held, own, width), BF16)
        return kernel(
            functools.partial(conv_terms, first, number, next_to),
            [some, some, shape((RING, held, own, width), BF16)],
            [SM] + [VM] * (6 + len(parts)),
            [pltpu.VMEM((2 * patches, width), BF16)] * 2,
            matmul * number,
            2 * square * number,
            where,
            spans_near,
            spans_far,
            *grads,
            *parts,
        )

    def add_to(terms, k, value):
        return (terms[k % RING].astype(F32) + value.astype(F32)).astype(BF16)

    one_far, one_side, one = weight_terms(0, 5, 5, ())
    one_far, one_side, one, grads, last_cross, read_a, read_b = fence(
        one_far, one_side, one, grads, last_cross, read_a, read_b
    )
    one_a, one_b = hop(one_far, True), hop(one_side, False)
    two_far, two_side, two = weight_terms(5, 4, 3, (last_own, last_near, last_cross))
    one_a, one_b, two_far, two_side, two, grads, shown, read_a, read_b = fence(
        one_a, one_b, two_far, two_side, two, grads, shown, read_a, read_b
    )
    two_a, two_b = hop(two_side, True), hop(two_far, False)
    one_a, one_b = add_to(one, 3, one_a), add_to(one, -2, one_b)
    shown = exchange_row(shown)
    backs = kernel(
        functools.partial(conv_back, full, cut),
        [piece] * 4,
        [SM] + [VM] * 4 + [HB] * (2 * RING + 1),
        [
            conv_scratch,
            pltpu.VMEM((total, width), BF16),
            pltpu.VMEM((3, slots, pad_rows, group), F32),
            pltpu.VMEM((total, group), BF16),
            DMA((2 * RING + 2,)),
        ],
        9 * matmul,
        9 * square + 12 * patches * width,
        where,
        *grads,
        *weights,
    )
    one_a, one_b, two_a, two_b, backs, shown = fence(one_a, one_b, two_a, two_b, backs, shown)
    one_a, one_b = hop(one_a, True), hop(one_b, False)
    two_a, two_b = add_to(two, 2, two_a), add_to(two, -3, two_b)
    backs = exchange_row(backs)
    one_a, one_b, two_a, two_b, backs = fence(one_a, one_b, two_a, two_b, backs)
    two_a, two_b = hop(two_a, True), hop(two_b, False)
    one_a, one_b = add_to(one, 2, one_a), add_to(one, -1, one_b)
    block = (RING, own + 16, width)
    grad_one, first_own, first_near, first_far = kernel(
        stage_one_back,
        [wide_bf16, shape(block, F32), shape((2,) + block, BF16), shape(block, F32)],
        [SM] + [VM] * 9,
        [pltpu.VMEM((patches, width), BF16), pltpu.VMEM((RING, 4, own, width), F32)],
        matmul,
        3 * square + 8 * patches * width,
        where,
        *backs,
        hat_one,
        scale_one,
        norms,
        x,
        sums,
    )
    one_a, one_b, two_a, two_b, first_near, first_far, grad_one = fence(
        one_a, one_b, two_a, two_b, first_near, first_far, grad_one
    )
    one_a, one_b_end = hop(one_a, True), hop(one_b, False)
    two_a, two_b = add_to(two, 1, two_a), add_to(two, -2, two_b)
    first_near = swap_row(first_near, 1)
    first_far = (first_far + first_near[1].astype(F32)).astype(BF16)
    one_a, one_b, two_a, two_b, first_near, first_far, grad_one, read_a, read_b = fence(
        one_a, one_b_end, two_a, two_b, first_near, first_far, grad_one, read_a, read_b
    )
    first_cross = swap_row(first_far, 2)
    two_a, two_b = hop(two_a, True), hop(two_b, False)
    one_a = add_to(one, 1, one_a)
    read_a, read_b = scatter_step(*read_far, read_terms, read_a, read_b, 1)
    image_grad = kernel(
        functools.partial(image_back, dims),
        wide_bf16,
        [SM, VM, VM] + [HB] * 4,
        [whole, pair_scratch, DMA((32,))],
        matmul,
        square + 8 * patches * width,
        where,
        grad_one,
        pool_sum,
        *firsts,
    ).reshape(slots, band, cols, width)
    one_a, two_a, two_b, first_cross, shown, image_grad = fence(one_a, two_a, two_b, first_cross, shown, image_grad)
    first_sum = (first_own + first_near[0].astype(F32) + first_cross.astype(F32)).astype(BF16)
    first_sum = lax.all_to_all(first_sum, "dp", 0, 0)
    one_a = hop(one_a, True)
    two_b = hop(add_to(two, -1, two_b), False)
    readout_out = kernel(
        join_columns,
        shape((count, 4 * width), BF16),
        [SM] + [VM] * 4,
        [],
        0,
        16 * count * width,
        where,
        *shown,
    ).reshape(slots, band // 2, cols // 2, 4 * width)
    tail = jnp.sum(first_sum.astype(F32), axis=0)
    read_sum = scatter_end(read_terms, read_a, read_b)
    read_grad, bias_row = read_sum[:outs].T, read_sum[outs]
    bias_grad = lax.dynamic_slice_in_dim(bias_row, dp * outs, outs)
    two_sum = scatter_end(two, two_a, two_b)
    conv_grad = jnp.concatenate([scatter_end(one, one_a, one_b), two_sum[:4]], axis=0)
    conv_grad = conv_grad.reshape(3, 3, own, width)
    first_grad = tail[:own].reshape(own, 4, RING, own).transpose(0, 2, 1, 3).reshape(own, width)
    last_grad = two_sum[4]
    swapped = lax.dynamic_slice(tail, (own, (row * RING + dp) * own), (2, own))
    plain = lax.dynamic_slice(tail, (own + 2, (dp * 4 + row) * own), (4, own))
    norm_grad = jnp.concatenate([swapped, plain], axis=0)
    return (
        readout_out,
        image_grad,
        first_grad,
        conv_grad,
        last_grad,
        norm_grad,
        read_grad,
        bias_grad,
    )


def per_device(*arrays):
    if lax.axis_size("dp") == RING and lax.axis_size("row") == 4:
        return ringed(*arrays)
    return generic(*arrays)


def solution(mesh):
    return jax.shard_map(
        per_device,
        mesh=mesh,
        in_specs=(
            P("dp", "row", None, None),
            P(("dp", "row"), None),
            P(None, None, ("dp", "row"), None),
            P(("dp", "row"), None),
            P(None, ("dp", "row")),
            P(None, ("dp", "row")),
            P(("dp", "row")),
            P("dp", "row", None, None),
            P("dp"),
        ),
        out_specs=(
            P("dp", "row", None, None),
            P("dp", "row", None, None),
            P(("dp", "row"), None),
            P(None, None, ("dp", "row"), None),
            P(("dp", "row"), None),
            P(None, ("dp", "row")),
            P(None, ("dp", "row")),
            P(("dp", "row")),
        ),
        check_vma=False,
    )
```

```python
import functools

import jax
import jax.numpy as jnp
from jax import lax
from jax.experimental import pallas as pl
from jax.experimental.pallas import tpu as pltpu

from jax.sharding import PartitionSpec as P

eps = 1e-06
F32 = jnp.float32
BF16 = jnp.bfloat16
RING = 8


def ring_order(n):
    return list(range(0, n, 2)) + list(range(n - 1, 0, -2))


def ring_pairs(n):
    order = ring_order(n)
    right = [(order[i], order[(i + 1) % n]) for i in range(n)]
    left = [(b, a) for a, b in right]
    return right, left


def ring_index(n, step):
    me = lax.axis_index("dp")
    place = jnp.where(me % 2 == 0, me // 2, n - 1 - me // 2)
    place = (place + step) % n
    return jnp.where(place < n // 2, 2 * place, 2 * (n - 1 - place) + 1)


def gather_dp(x, n):
    return lax.all_gather(x, "dp", axis=0, tiled=False)


def scatter_dp(parts, n):
    return lax.psum_scatter(parts.astype(F32), "dp", scatter_dimension=0, tiled=False)


def swap_row(x, q):
    return lax.ppermute(x, "row", [(i, i ^ q) for i in range(4)])


def gather_row(x):
    two = swap_row(x, 2)
    one = swap_row(x, 1)
    return [x, one, two, swap_row(two, 1)]


def exchange_row(pieces):
    return [pieces[0]] + [swap_row(pieces[q], q) for q in (1, 2, 3)]


def scatter_row(pieces):
    near = swap_row(jnp.stack([pieces[1], pieces[3]]).astype(BF16), 1).astype(F32)
    mine = pieces[0].astype(F32) + near[0]
    other = (pieces[2].astype(F32) + near[1]).astype(BF16)
    return mine + swap_row(other, 2).astype(F32)


def pick(choices, index):
    value = choices[0]
    for i in range(1, len(choices)):
        value = jnp.where(index == i, choices[i], value)
    return value


def dot(left, right):
    return jnp.dot(left, right, preferred_element_type=F32)


def dot_t(left, right):
    return lax.dot_general(left, right, (((1,), (1,)), ((), ())), preferred_element_type=F32)


def t_dot(left, right):
    return lax.dot_general(left, right, (((0,), (0,)), ((), ())), preferred_element_type=F32)


def normalize(value):
    centred = value - jnp.mean(value, axis=-1, keepdims=True)
    scale = lax.rsqrt(jnp.mean(centred * centred, axis=-1, keepdims=True) + eps)
    return centred * scale, scale


def norm_backward(grad_out, normed, scale, gain):
    weighted = grad_out * gain
    return scale * (
        weighted
        - jnp.mean(weighted, axis=-1, keepdims=True)
        - normed * jnp.mean(weighted * normed, axis=-1, keepdims=True)
    )


def silu_slope(value):
    gate = jax.nn.sigmoid(value)
    return gate * (1.0 + value * (1.0 - gate))


def gelu_slope(value):
    return (
        0.5 * (1.0 + lax.erf(value * 0.7071067811865476))
        + value * jnp.exp(-0.5 * value * value) * 0.3989422804014327
    )


def columns(value):
    cols = value.shape[2]
    wide = jnp.pad(value, ((0, 0), (1, 1), (1, 1), (0, 0)))
    return jnp.concatenate([wide[:, :, v : v + cols] for v in range(3)], axis=3)


def generic(
    images,
    first_weight,
    conv_weight,
    last_weight,
    norm_rows,
    read_weight,
    read_bias,
    cotangent,
    live_count,
):
    n, ranks = lax.axis_size("dp"), lax.axis_size("row")
    row = lax.axis_index("row")
    slots, band, cols, width = images.shape
    patches = slots * band * cols
    high = ranks * band
    own = first_weight.shape[0]
    group = n * own
    outs = read_weight.shape[1]
    rows_at = [row ^ q for q in range(ranks)]

    first_mine = first_weight.reshape(own, n, ranks, own).transpose(0, 2, 1, 3).reshape(own, width)
    small = jnp.concatenate([norm_rows.reshape(-1), read_bias])
    small = jnp.pad(small, (0, 8 * width - small.shape[0])).reshape(8, width)
    first_ring = gather_dp(jnp.concatenate([first_mine, small], axis=0), n)
    first_parts = gather_row(first_ring)

    def interleave(parts):
        whole = jnp.zeros((n, ranks) + parts[0].shape[1:], parts[0].dtype)
        for q in range(ranks):
            whole = lax.dynamic_update_slice(whole, parts[q][:, None], (0, rows_at[q], 0, 0))
        return whole

    first_all = interleave(first_parts)
    first_full = first_all[:, :, :own].reshape(width, width)
    norms = first_all[:, :, own].reshape(n, ranks, width)[:, :, : 6 * own]
    norms = norms.reshape(n, ranks, 6, own).astype(F32)
    norm_vals = norms.transpose(2, 0, 1, 3).reshape(6, width)
    norm_swap = norms.transpose(2, 1, 0, 3).reshape(6, width)
    bias_mine = first_ring[:, own, 6 * own : 6 * own + outs].reshape(n * outs).astype(F32)

    conv_taps = [gather_dp(conv_weight[u].reshape(3 * own, width), n) for u in range(3)]
    conv_taps = [
        tap.reshape(n, 3, own, width).transpose(1, 0, 2, 3).reshape(3 * group, width) for tap in conv_taps
    ]
    last_full = interleave(gather_row(gather_dp(last_weight, n))).reshape(width, width)
    read_mine = gather_dp(read_weight.T, n).reshape(n * outs, width)

    cot = cotangent.reshape(-1, n, ranks, outs)
    cot = exchange_row([pick([cot[:, :, i] for i in range(ranks)], rows_at[q]) for q in range(ranks)])
    cot = jnp.concatenate(cot, axis=0).reshape(-1, n * outs)

    flat_in = images.reshape(patches, width)
    hat_one, scale_one = normalize(dot(flat_in, first_full))
    pre_one = hat_one * norm_swap[0] + norm_swap[1]
    low_one = jax.nn.silu(pre_one).astype(BF16)
    split = [low_one[:, i * group : (i + 1) * group] for i in range(ranks)]
    bands = exchange_row([pick(split, rows_at[q]) for q in range(ranks)])

    def stack_bands(pieces):
        whole = jnp.zeros((slots, ranks, band, cols, pieces[0].shape[-1]), pieces[0].dtype)
        for q in range(ranks):
            piece = pieces[q].reshape(slots, 1, band, cols, -1)
            whole = lax.dynamic_update_slice(whole, piece, (0, rows_at[q], 0, 0, 0))
        return whole.reshape(slots, high, cols, -1)

    def take_bands(value):
        value = value.reshape(slots, ranks, band * cols, -1)
        return [
            lax.dynamic_index_in_dim(value, rows_at[q], 1, keepdims=False).reshape(patches, -1)
            for q in range(ranks)
        ]

    wide_one = columns(stack_bands(bands))
    slabs = [wide_one[:, u : u + high].reshape(slots * high * cols, 3 * group) for u in range(3)]
    act_two = dot(slabs[0], conv_taps[0]) + dot(slabs[1], conv_taps[1]) + dot(slabs[2], conv_taps[2])
    hat_two, scale_two = normalize(scatter_row(take_bands(act_two)))
    pre_two = hat_two * norm_vals[2] + norm_vals[3]
    low_two = jax.nn.silu(pre_two).astype(BF16)
    hat_three, scale_three = normalize(dot(low_two, last_full))
    summed = flat_in.astype(F32) + (hat_three * norm_vals[4] + norm_vals[5])
    pooled = jnp.mean(summed.reshape(slots, band // 2, 2, cols // 2, 2, width), axis=(2, 4)).astype(BF16)
    pooled = pooled.reshape(-1, width)
    pools = jnp.concatenate(gather_row(pooled), axis=0)
    logits = dot_t(pools, read_mine) + bias_mine
    mask = (jnp.arange(slots, dtype=jnp.int32) < live_count[0]).astype(F32)
    mask = jnp.broadcast_to(mask[None, :, None], (ranks, slots, pooled.shape[0] // slots)).reshape(-1, 1)
    shown = (jax.nn.gelu(logits, approximate=False) * mask).astype(BF16)
    shown = exchange_row(jnp.split(shown, ranks, axis=0))
    readout = jnp.zeros((pooled.shape[0], n, ranks, outs), BF16)
    for q in range(ranks):
        readout = lax.dynamic_update_slice(
            readout, shown[q].reshape(-1, n, 1, outs), (0, 0, rows_at[q], 0)
        )
    readout_out = readout.reshape(slots, band // 2, cols // 2, n * ranks * outs)

    grad_low = (cot.astype(F32) * mask * gelu_slope(logits)).astype(BF16)
    read_terms = t_dot(grad_low, pools).reshape(n, outs, width)
    bias_terms = jnp.sum(grad_low.astype(F32), axis=0).reshape(n, 1, outs)
    bias_terms = jnp.pad(bias_terms, ((0, 0), (0, 7), (0, width - outs)))
    read_sum = scatter_dp(jnp.concatenate([read_terms, bias_terms], axis=1), n)
    read_grad, bias_grad = read_sum[:outs].T, read_sum[outs, :outs]
    grad_pool = scatter_row(jnp.split(dot(grad_low, read_mine), ranks, axis=0))
    grad_sum = (
        jnp.broadcast_to(
            grad_pool.reshape(slots, band // 2, 1, cols // 2, 1, width),
            (slots, band // 2, 2, cols // 2, 2, width),
        )
        * 0.25
    ).reshape(-1, width)
    gain_three = jnp.sum(grad_sum * hat_three, axis=0)
    shift_three = jnp.sum(grad_sum, axis=0)
    grad_three = norm_backward(grad_sum, hat_three, scale_three, norm_vals[4]).astype(BF16)
    grad_pre_two = dot_t(grad_three, last_full) * silu_slope(pre_two)
    gain_two = jnp.sum(grad_pre_two * hat_two, axis=0)
    shift_two = jnp.sum(grad_pre_two, axis=0)
    grad_two = norm_backward(grad_pre_two, hat_two, scale_two, norm_vals[2]).astype(BF16)
    grad_full = stack_bands(gather_row(grad_two))
    grad_flat = grad_full.reshape(-1, width)

    def row_sums(terms):
        terms = terms.reshape(n, ranks, -1, width)
        return scatter_row(
            [lax.dynamic_index_in_dim(terms, rows_at[q], 1, keepdims=False) for q in range(ranks)]
        )

    conv_grad = []
    for u in range(3):
        terms = t_dot(slabs[u], grad_flat).reshape(3, n, own, width).transpose(1, 0, 2, 3)
        conv_grad.append(scatter_dp(terms.reshape(n, 3 * own, width), n).reshape(3, own, width))
    conv_grad = jnp.stack(conv_grad)
    wide_grad = jnp.pad(grad_full, ((0, 0), (1, 1), (1, 1), (0, 0)))
    grad_mid = jnp.zeros((slots * high * cols, group), F32)
    for u in range(3):
        for v in range(3):
            slab = wide_grad[:, 2 - u : 2 - u + high, 2 - v : 2 - v + cols].reshape(-1, width)
            grad_mid = grad_mid + dot_t(slab, conv_taps[u][v * group : (v + 1) * group])
    pieces = exchange_row(take_bands(grad_mid.astype(BF16)))
    grad_low_one = jnp.concatenate(
        [pick([pieces[i ^ q] for i in range(ranks)], row) for q in range(ranks)], axis=1
    ).astype(F32)
    last_sum = scatter_dp(row_sums(t_dot(low_two, grad_three)), n)

    grad_pre_one = grad_low_one * silu_slope(pre_one)
    gain_one = jnp.sum(grad_pre_one * hat_one, axis=0)
    shift_one = jnp.sum(grad_pre_one, axis=0)
    grad_one = norm_backward(grad_pre_one, hat_one, scale_one, norm_swap[0]).astype(BF16)
    image_grad = (grad_sum + dot_t(grad_one, first_full)).astype(BF16)
    image_grad = image_grad.reshape(slots, band, cols, width)

    swapped = jnp.stack([gain_one, shift_one]).reshape(2, ranks, n, own).transpose(2, 1, 0, 3)
    plain = jnp.stack([gain_two, shift_two, gain_three, shift_three])
    plain = plain.reshape(4, n, ranks, own).transpose(1, 2, 0, 3)
    norm_terms = jnp.concatenate([swapped, plain], axis=2).reshape(n, ranks, 1, 6 * own)
    norm_terms = jnp.pad(norm_terms, ((0, 0), (0, 0), (0, 7), (0, width - 6 * own)))
    first_terms = t_dot(flat_in, grad_one).reshape(n, ranks, own, width)
    first_sum = scatter_dp(row_sums(jnp.concatenate([first_terms, norm_terms], axis=2)), n)
    norm_grad = first_sum[own, : 6 * own].reshape(6, own)
    first_grad = first_sum[:own].reshape(own, ranks, n, own).transpose(0, 2, 1, 3).reshape(own, width)
    return (
        readout_out,
        image_grad,
        first_grad,
        conv_grad,
        last_sum,
        norm_grad,
        read_grad,
        bias_grad,
    )


VM = pl.BlockSpec(memory_space=pltpu.VMEM)
SM = pl.BlockSpec(memory_space=pltpu.SMEM)
HB = pl.BlockSpec(memory_space=pltpu.HBM)


def shape(dims, dtype):
    return jax.ShapeDtypeStruct(dims, dtype)


def kernel(body, outs, ins, scratch, flops, moved, *arrays, specs=None, room=24):
    return pl.pallas_call(
        body,
        out_shape=outs,
        in_specs=ins,
        out_specs=jax.tree.map(lambda _: VM, outs) if specs is None else specs,
        scratch_shapes=scratch,
        cost_estimate=pl.CostEstimate(flops=flops // 64, bytes_accessed=moved // 64, transcendentals=0),
        compiler_params=pltpu.CompilerParams(vmem_limit_bytes=room << 20),
    )(*arrays)


def at_row(where, q):
    return where[0] ^ q


def start_all(copies):
    for copy in copies:
        copy.start()


def wait_all(copies):
    for copy in copies:
        copy.wait()


def copies_of(pairs, sems):
    return [pltpu.make_async_copy(a, b, sems.at[i]) for i, (a, b) in enumerate(pairs)]


def hop(x, turn):
    right, left = ring_pairs(RING)
    return lax.ppermute(x, "dp", right if turn else left)


def gather_step(state, step, low=None, high=None):
    pieces, a, b = state
    pieces = list(pieces)
    if step < RING // 2:
        a, b = hop(a, True), hop(b, False)
        pieces[RING - step], pieces[step] = a, b
    else:
        pieces[step] = (hop(low(a), True), hop(high(b), False))
    return pieces, a, b


def gather_state(x):
    return [x] * RING, x, x


def scatter_step(low, high, terms, a, b, step):
    half = RING // 2
    if step == half:
        return hop(low, True), hop(high, False)
    right, left = terms[step].astype(F32), terms[RING - step].astype(F32)
    if step == half - 1:
        cut = low.shape[0]
        right = jnp.concatenate([right[:cut] + a.astype(F32), right[cut:]], axis=0)
        left = jnp.concatenate([left[:cut], left[cut:] + b.astype(F32)], axis=0)
    else:
        right, left = right + a.astype(F32), left + b.astype(F32)
    return hop(right.astype(BF16), True), hop(left.astype(BF16), False)


def scatter_end(terms, a, b):
    return terms[0].astype(F32) + a.astype(F32) + b.astype(F32)


def fence(*values):
    return lax.optimization_barrier(values)


def line_up(where, *refs):
    pieces, (first, last) = refs[: RING + 1], refs[RING + 1 :]
    rows = last.shape[1]
    for k in range(RING):
        if k == RING // 2:
            last[where[2 + k]] = pieces[k][...]
            first[where[2 + k]] = pieces[RING][...]
        else:
            last[where[2 + k]] = pieces[k][:rows]
            first[where[2 + k]] = pieces[k][rows:]


def fill(where, weight, parts):
    rows = weight.shape[2]
    for q, part in enumerate(parts):
        weight[:, at_row(where, q)] = part[:, :rows, :]


def center(value):
    mean = jnp.mean(value, axis=-1, keepdims=True)
    gap = value - mean
    scale = lax.rsqrt(jnp.mean(gap * gap, axis=-1, keepdims=True) + eps)
    return gap * scale, scale


def flat_pieces(pieces):
    half = RING // 2
    return [p[0] if k == half else p for k, p in enumerate(pieces)] + [pieces[half][1]]


def stage_one(where, x, f0, f1, f2, f3, hat, scale, s0, s1, s2, s3, norms, weight, low):
    firsts = (f0, f1, f2, f3)
    fill(where, weight, firsts)
    width, rows = x.shape[1], weight.shape[2]
    total = jnp.zeros((8, width), F32)
    bias = total
    for q, first in enumerate(firsts):
        for k in range(RING):
            block = first[k, rows:, :].astype(F32)
            total = total + block
            if q == 0:
                bias = bias + block
    line = lax.broadcasted_iota(jnp.int32, (8, width), 0)
    table = jnp.where(line == 6, bias, total)
    norms[...] = table
    act = dot(x[...], weight[...].reshape(width, width))
    normed, root = center(act)
    hat[...] = normed
    scale[...] = root
    pre = normed * norms[0:1, :] + norms[1:2, :]
    low[...] = (pre * jax.nn.sigmoid(pre)).astype(BF16)
    part = width // 4
    for q, out in enumerate((s0, s1, s2, s3)):
        out[...] = low[:, pl.ds(pl.multiple_of(at_row(where, q) * part, part), part)]


def conv_copies(where, pieces, weight, sems):
    far = RING // 2
    pairs = []
    for k in range(RING):
        if k == far:
            number = pieces[far].shape[0]
            pairs.append((pieces[far], weight.at[pl.ds(0, number), where[2 + k]]))
            pairs.append((pieces[RING], weight.at[pl.ds(number, pieces[RING].shape[0]), where[2 + k]]))
        else:
            pairs.append((pieces[k], weight.at[:, where[2 + k]]))
    return copies_of(pairs, sems)


def conv_forward(dims, first, where, s0, s1, s2, s3, *refs):
    slots, rows, cols = dims
    if first:
        own, near, spans, weight, pad, moved, wide, sems, done = refs[RING + 1 :]
        copies = conv_copies(where, refs[: RING + 1], weight, sems)
        start_all(copies)
    else:
        weight, own, near, spans, pad, moved, wide, done = refs
    group = s0.shape[1]
    patches = rows * cols
    band = patches // 4
    pad[...] = jnp.zeros_like(pad)
    for q, piece in enumerate((s0, s1, s2, s3)):
        for i in range(slots):
            at = pl.multiple_of(cols + 8 + at_row(where, q) * band, 8)
            pad[i, pl.ds(at, band), :] = piece[i * band : (i + 1) * band, :].astype(F32)
    for v in range(3):
        for i in range(slots):
            shifted = pad[i, 8 + v - 1 : 8 + v - 1 + patches + 2 * cols, :]
            if v != 1:
                col = lax.broadcasted_iota(jnp.int32, shifted.shape, 0) % cols
                shifted = jnp.where(col == (0 if v == 0 else cols - 1), 0.0, shifted)
            moved[i] = shifted
        for q in range(2):
            for i in range(slots):
                for u in range(3):
                    at = pl.multiple_of(at_row(where, first + q) * band + u * cols, 8)
                    t = u * 3 + v
                    here = (q * slots + i) * band
                    wide[here : here + band, t * group : (t + 1) * group] = moved[i, pl.ds(at, band), :].astype(BF16)
    keep = pltpu.make_async_copy(wide, spans, done)
    keep.start()
    if first:
        wait_all(copies)
    width = own.shape[1]
    chunk = 256
    patches = slots * band

    @pl.loop(0, width // chunk)
    def _(j):
        lanes = pl.ds(pl.multiple_of(j * chunk, chunk), chunk)
        terms = dot(wide[...], weight[:, :, :, lanes].reshape(-1, chunk))
        own[:, lanes] = terms[:patches]
        near[:, lanes] = terms[patches:].astype(BF16)

    keep.wait()


def stage_two(dims, where, own, near, cross, x, norms, l0, l1, l2, l3, hat_two, scale_two, low, hat, scale, pooled, weight, pairs):
    slots, rows, cols = dims
    fill(where, weight, (l0, l1, l2, l3))
    width = x.shape[1]
    act = own[...] + near[...].astype(F32) + cross[...].astype(F32)
    normed, root = center(act)
    hat_two[...] = normed
    scale_two[...] = root
    pre = normed * norms[2:3, :] + norms[3:4, :]
    low[...] = (pre * jax.nn.sigmoid(pre)).astype(BF16)
    normed, root = center(dot(low[...], weight[...].reshape(width, width)))
    hat[...] = normed
    scale[...] = root
    y = x[...].astype(F32) + (normed * norms[4:5, :] + norms[5:6, :])
    y = jnp.sum(y.reshape(slots * rows // 2, 2, cols, width), axis=1).reshape(-1, width)
    count = pooled.shape[0]
    for g in range(pairs.shape[0]):
        lanes = slice(g * 128, (g + 1) * 128)
        pairs[g] = y[:, lanes]
        pooled[:, lanes] = (
            0.25 * (pairs[g, pl.ds(0, count, stride=2), :] + pairs[g, pl.ds(1, count, stride=2), :])
        ).astype(BF16)


def read_copies(where, pieces, weight, sems):
    half = RING // 2
    pairs = []
    for k in range(RING):
        if k == half:
            rows = pieces[half].shape[0]
            pairs.append((pieces[half], weight.at[where[2 + k], pl.ds(0, rows)]))
            pairs.append((pieces[RING], weight.at[where[2 + k], pl.ds(rows, rows)]))
        else:
            pairs.append((pieces[k], weight.at[where[2 + k]]))
    return copies_of(pairs, sems)


def readout(slots, where, p0, p1, p2, p3, c0, c1, c2, c3, norms, *refs):
    pieces = refs[: RING + 1]
    o0, o1, o2, o3, low, own, near, far, weight, sems = refs[RING + 1 :]
    copies = read_copies(where, pieces, weight, sems)
    start_all(copies)
    count, width = p0.shape
    table = jnp.concatenate([p[...] for p in (p0, p1, p2, p3)], axis=0)
    line = lax.broadcasted_iota(jnp.int32, (count, width), 0)
    mask = jnp.where(line // (count // slots) < where[1], 1.0, 0.0)
    wait_all(copies)
    whole = weight[...].reshape(-1, width)
    logits = dot_t(table, whole) + norms[6:7, :]
    for q, (cot, out) in enumerate(((c0, o0), (c1, o1), (c2, o2), (c3, o3))):
        z = logits[q * count : (q + 1) * count]
        phi = 0.5 * (1.0 + lax.erf(z * 0.7071067811865476))
        out[...] = (z * phi * mask).astype(BF16)
        slope = phi + z * jnp.exp(-0.5 * z * z) * 0.3989422804014327
        low[q * count : (q + 1) * count, :] = (cot[...].astype(F32) * mask * slope).astype(BF16)
    back = dot(low[...], whole)
    own[...] = back[:count]
    near[0] = back[count : 2 * count].astype(BF16)
    far[...] = back[2 * count : 3 * count]
    near[1] = back[3 * count :].astype(BF16)


def readout_terms(where, low, p0, p1, p2, p3, upper, lower, out, terms):
    width = p0.shape[1]
    table = jnp.concatenate([p[...] for p in (p0, p1, p2, p3)], axis=0)
    terms[...] = t_dot(low[...], table).reshape(terms.shape)
    bias = jnp.sum(low[...].astype(F32), axis=0, keepdims=True)
    rows = terms.shape[1]
    for k in range(RING):
        out[k, :rows, :] = terms[where[2 + k]].astype(BF16)
        out[k, rows:, :] = jnp.broadcast_to(bias, (out.shape[1] - rows, width)).astype(BF16)
    upper[...] = out[RING // 2, : upper.shape[0]]
    lower[...] = out[RING // 2, upper.shape[0] :]


def spread(pairs, grad, dims):
    slots, rows, cols = dims
    count, width = grad.shape
    for g in range(pairs.shape[0]):
        lanes = slice(g * 128, (g + 1) * 128)
        pairs[g, pl.ds(0, count, stride=2), :] = grad[:, lanes]
        pairs[g, pl.ds(1, count, stride=2), :] = grad[:, lanes]
    half = slots * rows // 2
    both = jnp.concatenate([pairs[g] for g in range(pairs.shape[0])], axis=1)
    both = jnp.broadcast_to(both.reshape(half, 1, cols, width), (half, 2, cols, width))
    return both.reshape(-1, width) * 0.25


def back_norm(grad, normed, root, gain):
    weighted = grad * gain
    return root * (
        weighted
        - jnp.mean(weighted, axis=-1, keepdims=True)
        - normed * jnp.mean(weighted * normed, axis=-1, keepdims=True)
    )


def total_rows(value):
    return jnp.sum(value, axis=0, keepdims=True)


def stage_two_back(dims, where, own, near, cross, hat, scale, hat_two, scale_two, norms, weight, grad_three, grad_two, pool_sum, sums, pairs):
    width = hat.shape[1]
    grad = own[...] + near[...].astype(F32) + cross[...].astype(F32)
    pool_sum[...] = grad
    gy = spread(pairs, grad, dims)
    sums[...] = jnp.zeros_like(sums)
    sums[4:5, :] = total_rows(gy * hat[...])
    sums[5:6, :] = total_rows(gy)
    grad_three[...] = back_norm(gy, hat[...], scale[...], norms[4:5, :]).astype(BF16)
    gs = dot_t(grad_three[...], weight[...].reshape(width, width))
    pre = hat_two[...] * norms[2:3, :] + norms[3:4, :]
    gn = gs * silu_slope(pre)
    sums[2:3, :] = total_rows(gn * hat_two[...])
    sums[3:4, :] = total_rows(gn)
    grad_two[...] = back_norm(gn, hat_two[...], scale_two[...], norms[2:3, :]).astype(BF16)


def last_terms(where, low, grad, own, near, far, terms):
    terms[...] = t_dot(low[...], grad[...]).reshape(terms.shape)
    for k in range(RING):
        own[k] = terms[where[2 + k], at_row(where, 0)]
        near[0, k] = terms[where[2 + k], at_row(where, 1)].astype(BF16)
        far[k] = terms[where[2 + k], at_row(where, 2)]
        near[1, k] = terms[where[2 + k], at_row(where, 3)].astype(BF16)


def stack_grad(dims, where, pieces, whole):
    slots, rows, cols = dims
    band = rows * cols // 4
    for q, piece in enumerate(pieces):
        for i in range(slots):
            at = pl.multiple_of(i * rows * cols + at_row(where, q) * band, 16)
            whole[pl.ds(at, band), :] = piece[i * band : (i + 1) * band, :]


def conv_half_terms(where, here, g0, g1, out, one):
    count = g0.shape[0]
    one[:count], one[count:] = g0[...], g1[...]
    group = out.shape[1]

    @pl.loop(0, out.shape[0])
    def _(t):
        lanes = pl.ds(pl.multiple_of(t * group, group), group)
        out[t] = t_dot(here[:, lanes], one[...])


def conv_terms(first, number, next_to, where, half, there, g2, g3, *refs):
    parts, (far, side, out, two) = refs[:-4], refs[-4:]
    count = g2.shape[0]
    two[:count], two[count:] = g2[...], g3[...]
    rows, width = out.shape[2:]
    group = RING * rows

    @pl.loop(0, number)
    def _(t):
        lanes = pl.ds(pl.multiple_of((first + t) * group, group), group)
        terms = half[first + t] + t_dot(there[:, lanes], two[...])
        terms = terms.astype(BF16).reshape(RING, rows, width)
        for k in range(RING):
            out[where[2 + RING + k], t] = terms[k]

    if parts:
        own, near, low, high = parts
        half_way = RING // 2
        for a, b, cross in ((0, half_way, low), (half_way, RING, high)):
            out[a:b, number] = (own[a:b] + near[0, a:b].astype(F32) + cross[...].astype(F32)).astype(BF16)
    far[...] = out[RING // 2]
    side[...] = out[next_to]


def conv_back(dims, where, g0, g1, g2, g3, weight, o0, o1, o2, o3, whole, held, low):
    slots, rows, cols = dims
    stack_grad(dims, where, (g0, g1, g2, g3), whole)
    patches = rows * cols
    band = patches // 4
    group = o0.shape[1]
    width = whole.shape[1]
    held[...] = jnp.zeros_like(held)
    for u in range(3):
        for v in range(3):
            part = dot_t(whole[...], weight[u * 3 + v].reshape(group, width))
            for i in range(slots):
                held[v, i, 8 + u * cols : 8 + u * cols + patches, :] += part[i * patches : (i + 1) * patches]
    col = lax.broadcasted_iota(jnp.int32, (patches, group), 0) % cols
    for i in range(slots):
        value = held[1, i, 8 + cols : 8 + cols + patches, :]
        value += jnp.where(col == cols - 1, 0.0, held[0, i, 9 + cols : 9 + cols + patches, :])
        value += jnp.where(col == 0, 0.0, held[2, i, 7 + cols : 7 + cols + patches, :])
        low[i * patches : (i + 1) * patches, :] = value.astype(BF16)
    for q, out in enumerate((o0, o1, o2, o3)):
        for i in range(slots):
            at = pl.multiple_of(i * patches + at_row(where, q) * band, 16)
            out[i * band : (i + 1) * band, :] = low[pl.ds(at, band), :]


def stage_one_back(where, b0, b1, b2, b3, hat, scale, norms, x, sums, grad_one, own, near, far, low, terms):
    width = hat.shape[1]
    part = width // 4
    for q, piece in enumerate((b0, b1, b2, b3)):
        low[:, pl.ds(pl.multiple_of(at_row(where, q) * part, part), part)] = piece[...]
    pre = hat[...] * norms[0:1, :] + norms[1:2, :]
    gn = low[...].astype(F32) * silu_slope(pre)
    line = lax.broadcasted_iota(jnp.int32, (8, width), 0)
    tail = jnp.where(line == 0, total_rows(gn * hat[...]), jnp.where(line == 1, total_rows(gn), sums[...]))
    tail = jnp.concatenate([tail, tail], axis=0)
    grad_one[...] = back_norm(gn, hat[...], scale[...], norms[0:1, :]).astype(BF16)
    terms[...] = t_dot(x[...], grad_one[...]).reshape(terms.shape)
    rows = terms.shape[2]
    for k in range(RING):
        own[k, :rows] = terms[where[2 + k], at_row(where, 0)]
        near[0, k, :rows] = terms[where[2 + k], at_row(where, 1)].astype(BF16)
        far[k, :rows] = terms[where[2 + k], at_row(where, 2)]
        near[1, k, :rows] = terms[where[2 + k], at_row(where, 3)].astype(BF16)
        own[k, rows:] = tail
        near[0, k, rows:] = tail.astype(BF16)
        far[k, rows:] = tail
        near[1, k, rows:] = tail.astype(BF16)


def image_back(dims, where, grad_one, pool_sum, weight, out, pairs):
    width = grad_one.shape[1]
    gy = spread(pairs, pool_sum[...], dims)
    out[...] = (gy + dot_t(grad_one[...], weight[...].reshape(width, width))).astype(BF16)


def split_columns(where, x, o0, o1, o2, o3):
    lanes = x.shape[1] // (4 * RING)
    for q, out in enumerate((o0, o1, o2, o3)):
        for g in range(RING):
            at = pl.multiple_of((g * 4 + at_row(where, q)) * lanes, lanes)
            out[:, g * lanes : (g + 1) * lanes] = x[:, pl.ds(at, lanes)]


def join_columns(where, i0, i1, i2, i3, out):
    lanes = out.shape[1] // (4 * RING)
    for q, piece in enumerate((i0, i1, i2, i3)):
        for g in range(RING):
            at = pl.multiple_of((g * 4 + at_row(where, q)) * lanes, lanes)
            out[:, pl.ds(at, lanes)] = piece[:, g * lanes : (g + 1) * lanes]


def ringed(
    images,
    first_weight,
    conv_weight,
    last_weight,
    norm_rows,
    read_weight,
    read_bias,
    cotangent,
    live_count,
):
    dp, row = lax.axis_index("dp"), lax.axis_index("row")
    slots, band, cols, width = images.shape
    dims = (slots, band, cols)
    full = (slots, 4 * band, cols)
    patches = slots * band * cols
    count = patches // 4
    own = first_weight.shape[0]
    group = RING * own
    outs = read_weight.shape[1]
    taps = 9
    DMA = pltpu.SemaphoreType.DMA
    index = jnp.arange(18, dtype=jnp.int32)
    place_of = lambda d: jnp.where(d % 2 == 0, d // 2, RING - 1 - d // 2)
    place = (place_of(dp) + index - 2) % RING
    ahead = jnp.where(place < RING // 2, 2 * place, 2 * (RING - 1 - place) + 1)
    steps = (place_of(index - 10) - place_of(dp)) % RING
    where = jnp.where(index == 0, row, jnp.where(index == 1, live_count[0], jnp.where(index < 10, ahead, steps)))
    where = where.astype(jnp.int32)

    first_mine = first_weight.reshape(own, RING, 4, own).transpose(0, 2, 1, 3).reshape(own, width)
    lane = jnp.arange(width, dtype=jnp.int32)[None, :]
    tiled = jnp.tile(norm_rows, (1, width // own))
    at = jnp.where(jnp.arange(6)[:, None] < 2, row * RING + dp, dp * 4 + row)
    small = jnp.where(lane // own == at, tiled, 0).astype(BF16)
    bias = jnp.where(lane // outs == dp, jnp.tile(read_bias, width // outs)[None, :], 0).astype(BF16)
    small = jnp.concatenate([small, bias, jnp.zeros((1, width), BF16)], axis=0)
    first_mine = jnp.concatenate([first_mine, small], axis=0)
    conv = conv_weight.reshape(taps, own, width)
    quarter = shape((count, width), BF16)
    wide_f32, thin_f32, wide_bf16 = (
        shape((patches, width), F32),
        shape((patches, 1), F32),
        shape((patches, width), BF16),
    )
    quarter_f32, near_quarter = shape((count, width), F32), shape((2, count, width), BF16)
    piece = shape((patches, group), BF16)
    block = (RING, own, width)
    matmul = 2 * patches * width * width
    square = 2 * width * width
    square_of = shape((RING, 4, own, width), BF16)
    total = 4 * patches
    pad_rows = full[1] * cols + 2 * cols + 16
    pair_scratch = pltpu.VMEM((width // 128, patches // 2, 128), F32)
    x = images.reshape(patches, width)

    far = RING // 2
    cut = own + 8
    low, high = lambda v: v[:own], lambda v: v[own:]
    more = gather_step(gather_state(conv), 1)
    ring = gather_step(gather_state(jnp.concatenate([last_weight, first_mine], axis=0)), 1)
    read = read_weight.T
    cots = cotangent.reshape(count, -1)
    more, ring, where, read, cots, x = fence(more, ring, where, read, cots, x)
    ring = gather_step(ring, 2)
    cots = kernel(split_columns, [quarter] * 4, [SM, VM], [], 0, 2 * count * 4 * width * 2, where, cots)
    ring, cots = fence(ring, cots)
    ring = gather_step(ring, 3)
    ring = fence(ring)[0]
    ring = gather_step(ring, 4, low, high)
    more, ring = fence(more, ring)
    ring = ring[0]
    firsts, lasts = kernel(
        line_up,
        [shape((RING, cut, width), BF16), shape((RING, own, width), BF16)],
        [SM] + [VM] * (RING + 1),
        [],
        0,
        4 * RING * (cut + own) * width,
        where,
        *flat_pieces(ring),
    )
    more = gather_step(more, 2)
    first_two, first_one = swap_row(firsts, 2), swap_row(firsts, 1)
    more, firsts, first_two, first_one, lasts = fence(more, firsts, first_two, first_one, lasts)
    more = gather_step(more, 3)
    firsts = [firsts, first_one, first_two, swap_row(first_two, 1)]
    last_two, last_one = swap_row(lasts, 2), swap_row(lasts, 1)
    hat_one, scale_one, *lows, norms, first_full = kernel(
        stage_one,
        [wide_f32, thin_f32] + [piece] * 4 + [shape((8, width), F32), square_of],
        [SM] + [VM] * 5,
        [pltpu.VMEM((patches, width), BF16)],
        matmul,
        square + 8 * patches * width,
        where,
        x,
        *firsts,
    )
    more, lows, lasts, last_two, last_one = fence(more, lows, lasts, last_two, last_one)
    taps_half = (taps + 1) // 2
    more = gather_step(more, 4, lambda v: v[:taps_half], lambda v: v[taps_half:])
    lows = exchange_row(lows)
    lasts = [lasts, last_one, last_two, swap_row(last_two, 1)]
    weights = flat_pieces(more[0])
    weights, lows, lasts, read, cots = fence(weights, lows, lasts, read, cots)

    conv_whole = (taps, RING, own, width)

    def conv_half(first, weights):
        return kernel(
            functools.partial(conv_forward, full, first),
            [wide_f32, wide_bf16, shape((2 * patches, taps * group), BF16)]
            + ([shape(conv_whole, BF16)] if first else []),
            [SM] + [VM] * 4 + ([HB] * (RING + 1) if first else [VM]),
            [
                pltpu.VMEM((slots, pad_rows, group), F32),
                pltpu.VMEM((slots, pad_rows - 16, group), F32),
                pltpu.VMEM((2 * patches, taps * group), BF16),
            ]
            + ([DMA((RING + 1,))] if first else [])
            + [DMA],
            9 * matmul // 2,
            9 * square + 6 * patches * width + 4 * patches * taps * group,
            where,
            *lows,
            *weights,
            specs=[VM, VM, HB] + ([VM] if first else []),
        )

    read = gather_step(gather_state(read), 1)
    cots = exchange_row(cots)
    away, near, spans_far, conv_full = conv_half(2, weights)
    away, near, read, cots = fence(away, near, read, cots)
    other = (away + swap_row(near, 1).astype(F32)).astype(BF16)
    other, lows, read = fence(other, lows, read)
    cross = swap_row(other, 2)
    read = gather_step(read, 2)
    mine, near, spans_near = conv_half(0, (conv_full,))
    near, read = fence(near, read)
    near = swap_row(near, 1)
    mine, near, cross, read = fence(mine, near, cross, read)
    read = gather_step(read, 3)
    hat_two, scale_two, low_two, hat_three, scale_three, pooled, last_full = kernel(
        functools.partial(stage_two, dims),
        [wide_f32, thin_f32, wide_bf16, wide_f32, thin_f32, quarter, square_of],
        [SM] + [VM] * 9,
        [pair_scratch],
        matmul,
        square + 24 * patches * width,
        where,
        mine,
        near,
        cross,
        x,
        norms,
        *lasts,
    )
    pooled, read = fence(pooled, read)
    read = gather_step(read, 4, lambda v: v[: outs // 2], lambda v: v[outs // 2 :])
    pool_two, pool_one = swap_row(pooled, 2), swap_row(pooled, 1)
    pooled, pool_two, pool_one, read = fence(pooled, pool_two, pool_one, read)
    pools = [pooled, pool_one, pool_two, swap_row(pool_two, 1)]
    *shown, grad_low, mine, near, away = kernel(
        functools.partial(readout, slots),
        [quarter] * 4 + [wide_bf16, quarter_f32, near_quarter, quarter_f32],
        [SM] + [VM] * 9 + [HB] * (RING + 1),
        [pltpu.VMEM((RING, outs, width), BF16), DMA((RING + 1,))],
        2 * matmul,
        square + 12 * patches * width,
        where,
        *pools,
        *cots,
        norms,
        *flat_pieces(read[0]),
    )

    near = swap_row(near, 1)
    other = (away + near[1].astype(F32)).astype(BF16)
    other, grad_low, near = fence(other, grad_low, near)
    cross = swap_row(other, 2)
    half_read = shape(((outs + 16) // 2, width), BF16)
    *read_far, read_terms = kernel(
        readout_terms,
        [half_read, half_read, shape((RING, outs + 16, width), BF16)],
        [SM] + [VM] * 5,
        [pltpu.VMEM((RING, outs, width), F32)],
        matmul,
        2 * square,
        where,
        grad_low,
        *pools,
    )
    cross, read_far, read_terms, near = fence(cross, read_far, read_terms, near)
    read_a, read_b = scatter_step(*read_far, read_terms, None, None, 4)
    grad_three, grad_two, pool_sum, sums = kernel(
        functools.partial(stage_two_back, dims),
        [wide_bf16, wide_bf16, quarter_f32, shape((8, width), F32)],
        [SM] + [VM] * 9,
        [pair_scratch],
        matmul,
        square + 14 * patches * width,
        where,
        mine,
        near[0],
        cross,
        hat_three,
        scale_three,
        hat_two,
        scale_two,
        norms,
        last_full,
    )
    grad_three, grad_two, read_a, read_b = fence(grad_three, grad_two, read_a, read_b)
    grad_far, grad_next = swap_row(grad_two, 2), swap_row(grad_two, 1)
    read_a, read_b = scatter_step(*read_far, read_terms, read_a, read_b, 3)
    read_a, read_b = scatter_step(*read_far, read_terms, read_a, read_b, 2)
    here = kernel(
        conv_half_terms,
        shape((taps, group, width), F32),
        [SM] + [VM] * 3,
        [pltpu.VMEM((2 * patches, width), BF16)],
        9 * matmul // 2,
        18 * square,
        where,
        spans_near,
        grad_two,
        grad_next,
    )
    last_own, last_near, last_far = kernel(
        last_terms,
        [shape(block, F32), shape((2,) + block, BF16), shape(block, F32)],
        [SM, VM, VM],
        [pltpu.VMEM((RING, 4, own, width), F32)],
        matmul,
        3 * square,
        where,
        low_two,
        grad_three,
    )
    grad_two, grad_far, grad_next, last_near, last_far, read_a, read_b, here = fence(
        grad_two, grad_far, grad_next, last_near, last_far, read_a, read_b, here
    )
    grads = [grad_two, grad_next, grad_far, swap_row(grad_far, 1)]
    last_near = swap_row(last_near, 1)
    last_low = (last_far[:far] + last_near[1, :far].astype(F32)).astype(BF16)
    last_high = (last_far[far:] + last_near[1, far:].astype(F32)).astype(BF16)
    grads, last_near, last_low, last_high = fence(grads, last_near, last_low, last_high)
    last_low = swap_row(last_low, 2)
    read_a, read_b = scatter_step(*read_far, read_terms, read_a, read_b, 1)

    def weight_terms(first, number, next_to, parts):
        held = number + len(parts) // 4
        some = shape((held, own, width), BF16)
        return kernel(
            functools.partial(conv_terms, first, number, next_to),
            [some, some, shape((RING, held, own, width), BF16)],
            [SM] + [VM] * (4 + len(parts)),
            [pltpu.VMEM((2 * patches, width), BF16)],
            matmul * number,
            2 * square * number,
            where,
            here,
            spans_far,
            *grads[2:],
            *parts,
        )

    def add_to(terms, k, value):
        return (terms[k % RING].astype(F32) + value.astype(F32)).astype(BF16)

    one_far, one_side, one = weight_terms(0, 5, 5, ())
    one_far, one_side, one, grads, last_low, last_high, read_a, read_b = fence(
        one_far, one_side, one, grads, last_low, last_high, read_a, read_b
    )
    last_high = swap_row(last_high, 2)
    one_a, one_b = hop(one_far, True), hop(one_side, False)
    backs = kernel(
        functools.partial(conv_back, full),
        [piece] * 4,
        [SM] + [VM] * 5,
        [
            pltpu.VMEM((total, width), BF16),
            pltpu.VMEM((3, slots, pad_rows, group), F32),
            pltpu.VMEM((total, group), BF16),
        ],
        9 * matmul,
        9 * square + 12 * patches * width,
        where,
        *grads,
        conv_full,
    )
    one_a, one_b, backs, grads, last_high = fence(one_a, one_b, backs, grads, last_high)
    one_a, one_b = hop(add_to(one, 3, one_a), True), hop(add_to(one, -2, one_b), False)
    backs = exchange_row(backs)
    two_far, two_side, two = weight_terms(5, 4, 3, (last_own, last_near, last_low, last_high))
    one_a, one_b, two_far, two_side, two, backs = fence(one_a, one_b, two_far, two_side, two, backs)
    two_a, two_b = hop(two_side, True), hop(two_far, False)
    one_a, one_b = add_to(one, 2, one_a), add_to(one, -1, one_b)
    block = (RING, own + 16, width)
    grad_one, first_own, first_near, first_far = kernel(
        stage_one_back,
        [wide_bf16, shape(block, F32), shape((2,) + block, BF16), shape(block, F32)],
        [SM] + [VM] * 9,
        [pltpu.VMEM((patches, width), BF16), pltpu.VMEM((RING, 4, own, width), F32)],
        matmul,
        3 * square + 8 * patches * width,
        where,
        *backs,
        hat_one,
        scale_one,
        norms,
        x,
        sums,
    )
    one_a, one_b, two_a, two_b, grad_one, first_own, first_near, first_far, shown = fence(
        one_a, one_b, two_a, two_b, grad_one, first_own, first_near, first_far, shown
    )
    one_a, one_b = hop(one_a, True), hop(one_b, False)
    two_a, two_b = add_to(two, 2, two_a), add_to(two, -3, two_b)
    first_near = swap_row(first_near, 1)
    shown = exchange_row(shown)
    first_low = (first_far[:far] + first_near[1, :far].astype(F32)).astype(BF16)
    first_high = (first_far[far:] + first_near[1, far:].astype(F32)).astype(BF16)
    one_a, one_b_end, two_a, two_b, first_near, first_low, first_high, shown = fence(
        one_a, one_b, two_a, two_b, first_near, first_low, first_high, shown
    )
    two_a, two_b = hop(two_a, True), hop(two_b, False)
    one_a = add_to(one, 1, one_a)
    first_high = swap_row(first_high, 2)
    image_grad = kernel(
        functools.partial(image_back, dims),
        wide_bf16,
        [SM, VM, VM, VM],
        [pair_scratch],
        matmul,
        square + 8 * patches * width,
        where,
        grad_one,
        pool_sum,
        first_full,
    ).reshape(slots, band, cols, width)
    one_a, two_a, two_b, first_low, first_high, image_grad = fence(
        one_a, two_a, two_b, first_low, first_high, image_grad
    )
    one_a, two_b = hop(one_a, True), hop(add_to(two, -2, two_b), False)
    two_a = add_to(two, 1, two_a)
    first_low = swap_row(first_low, 2)
    first_high = (first_own[far:] + first_near[0, far:].astype(F32) + first_high.astype(F32)).astype(BF16)
    one_a, two_a, two_b, first_low, first_high, shown = fence(one_a, two_a, two_b, first_low, first_high, shown)
    first_a, first_b = hop(first_high[0], True), hop(first_high[1], False)
    two_a, two_b = hop(two_a, True), hop(add_to(two, -1, two_b), False)
    first_low = (first_own[:far] + first_near[0, :far].astype(F32) + first_low.astype(F32)).astype(BF16)
    readout_out = kernel(
        join_columns,
        shape((count, 4 * width), BF16),
        [SM] + [VM] * 4,
        [],
        0,
        16 * count * width,
        where,
        *shown,
    ).reshape(slots, band // 2, cols // 2, 4 * width)
    read_sum = scatter_end(read_terms, read_a, read_b)
    two_a, two_b, first_a, first_b, first_low, readout_out, read_sum = fence(
        two_a, two_b, first_a, first_b, first_low, readout_out, read_sum
    )
    first_a, first_b = hop(add_to(first_low, 3, first_a), True), hop(add_to(first_high[far - 2 :], 0, first_b), False)
    read_grad, bias_row = read_sum[:outs].T, read_sum[outs]
    bias_grad = lax.dynamic_slice_in_dim(bias_row, dp * outs, outs)
    first_a, first_b, read_grad = fence(first_a, first_b, read_grad)
    first_a, first_b = hop(add_to(first_low, 2, first_a), True), hop(add_to(first_high[far - 1 :], 0, first_b), False)
    two_sum = scatter_end(two, two_a, two_b)
    conv_grad = jnp.concatenate([scatter_end(one, one_a, one_b_end), two_sum[:4]], axis=0)
    conv_grad = conv_grad.reshape(3, 3, own, width)
    first_a, first_b, conv_grad = fence(first_a, first_b, conv_grad)
    first_a = hop(add_to(first_low, 1, first_a), True)
    tail = first_low[0].astype(F32) + first_a.astype(F32) + first_b.astype(F32)
    first_grad = tail[:own].reshape(own, 4, RING, own).transpose(0, 2, 1, 3).reshape(own, width)
    last_grad = two_sum[4]
    swapped = lax.dynamic_slice(tail, (own, (row * RING + dp) * own), (2, own))
    plain = lax.dynamic_slice(tail, (own + 2, (dp * 4 + row) * own), (4, own))
    norm_grad = jnp.concatenate([swapped, plain], axis=0)
    return (
        readout_out,
        image_grad,
        first_grad,
        conv_grad,
        last_grad,
        norm_grad,
        read_grad,
        bias_grad,
    )


def per_device(*arrays):
    if lax.axis_size("dp") == RING and lax.axis_size("row") == 4:
        return ringed(*arrays)
    return generic(*arrays)


def solution(mesh):
    return jax.shard_map(
        per_device,
        mesh=mesh,
        in_specs=(
            P("dp", "row", None, None),
            P(("dp", "row"), None),
            P(None, None, ("dp", "row"), None),
            P(("dp", "row"), None),
            P(None, ("dp", "row")),
            P(None, ("dp", "row")),
            P(("dp", "row")),
            P("dp", "row", None, None),
            P("dp"),
        ),
        out_specs=(
            P("dp", "row", None, None),
            P("dp", "row", None, None),
            P(("dp", "row"), None),
            P(None, None, ("dp", "row"), None),
            P(("dp", "row"), None),
            P(None, ("dp", "row")),
            P(None, ("dp", "row")),
            P(("dp", "row")),
        ),
        check_vma=False,
    )
```

```python
import functools

import jax
import jax.numpy as jnp
from jax import lax
from jax.experimental import pallas as pl
from jax.experimental.pallas import tpu as pltpu

from jax.sharding import PartitionSpec as P

eps = 1e-06
F32 = jnp.float32
BF16 = jnp.bfloat16
RING = 8


def ring_order(n):
    return list(range(0, n, 2)) + list(range(n - 1, 0, -2))


def ring_pairs(n):
    order = ring_order(n)
    right = [(order[i], order[(i + 1) % n]) for i in range(n)]
    left = [(b, a) for a, b in right]
    return right, left


def ring_index(n, step):
    me = lax.axis_index("dp")
    place = jnp.where(me % 2 == 0, me // 2, n - 1 - me // 2)
    place = (place + step) % n
    return jnp.where(place < n // 2, 2 * place, 2 * (n - 1 - place) + 1)


def gather_dp(x, n):
    return lax.all_gather(x, "dp", axis=0, tiled=False)


def scatter_dp(parts, n):
    return lax.psum_scatter(parts.astype(F32), "dp", scatter_dimension=0, tiled=False)


def swap_row(x, q):
    return lax.ppermute(x, "row", [(i, i ^ q) for i in range(4)])


def gather_row(x):
    two = swap_row(x, 2)
    one = swap_row(x, 1)
    return [x, one, two, swap_row(two, 1)]


def exchange_row(pieces):
    return [pieces[0]] + [swap_row(pieces[q], q) for q in (1, 2, 3)]


def scatter_row(pieces):
    near = swap_row(jnp.stack([pieces[1], pieces[3]]).astype(BF16), 1).astype(F32)
    mine = pieces[0].astype(F32) + near[0]
    other = (pieces[2].astype(F32) + near[1]).astype(BF16)
    return mine + swap_row(other, 2).astype(F32)


def pick(choices, index):
    value = choices[0]
    for i in range(1, len(choices)):
        value = jnp.where(index == i, choices[i], value)
    return value


def dot(left, right):
    return jnp.dot(left, right, preferred_element_type=F32)


def dot_t(left, right):
    return lax.dot_general(left, right, (((1,), (1,)), ((), ())), preferred_element_type=F32)


def t_dot(left, right):
    return lax.dot_general(left, right, (((0,), (0,)), ((), ())), preferred_element_type=F32)


def normalize(value):
    centred = value - jnp.mean(value, axis=-1, keepdims=True)
    scale = lax.rsqrt(jnp.mean(centred * centred, axis=-1, keepdims=True) + eps)
    return centred * scale, scale


def norm_backward(grad_out, normed, scale, gain):
    weighted = grad_out * gain
    return scale * (
        weighted
        - jnp.mean(weighted, axis=-1, keepdims=True)
        - normed * jnp.mean(weighted * normed, axis=-1, keepdims=True)
    )


def silu_slope(value):
    gate = jax.nn.sigmoid(value)
    return gate * (1.0 + value * (1.0 - gate))


def gelu_slope(value):
    return (
        0.5 * (1.0 + lax.erf(value * 0.7071067811865476))
        + value * jnp.exp(-0.5 * value * value) * 0.3989422804014327
    )


def columns(value):
    cols = value.shape[2]
    wide = jnp.pad(value, ((0, 0), (1, 1), (1, 1), (0, 0)))
    return jnp.concatenate([wide[:, :, v : v + cols] for v in range(3)], axis=3)


def generic(
    images,
    first_weight,
    conv_weight,
    last_weight,
    norm_rows,
    read_weight,
    read_bias,
    cotangent,
    live_count,
):
    n, ranks = lax.axis_size("dp"), lax.axis_size("row")
    row = lax.axis_index("row")
    slots, band, cols, width = images.shape
    patches = slots * band * cols
    high = ranks * band
    own = first_weight.shape[0]
    group = n * own
    outs = read_weight.shape[1]
    rows_at = [row ^ q for q in range(ranks)]

    first_mine = first_weight.reshape(own, n, ranks, own).transpose(0, 2, 1, 3).reshape(own, width)
    small = jnp.concatenate([norm_rows.reshape(-1), read_bias])
    small = jnp.pad(small, (0, 8 * width - small.shape[0])).reshape(8, width)
    first_ring = gather_dp(jnp.concatenate([first_mine, small], axis=0), n)
    first_parts = gather_row(first_ring)

    def interleave(parts):
        whole = jnp.zeros((n, ranks) + parts[0].shape[1:], parts[0].dtype)
        for q in range(ranks):
            whole = lax.dynamic_update_slice(whole, parts[q][:, None], (0, rows_at[q], 0, 0))
        return whole

    first_all = interleave(first_parts)
    first_full = first_all[:, :, :own].reshape(width, width)
    norms = first_all[:, :, own].reshape(n, ranks, width)[:, :, : 6 * own]
    norms = norms.reshape(n, ranks, 6, own).astype(F32)
    norm_vals = norms.transpose(2, 0, 1, 3).reshape(6, width)
    norm_swap = norms.transpose(2, 1, 0, 3).reshape(6, width)
    bias_mine = first_ring[:, own, 6 * own : 6 * own + outs].reshape(n * outs).astype(F32)

    conv_taps = [gather_dp(conv_weight[u].reshape(3 * own, width), n) for u in range(3)]
    conv_taps = [
        tap.reshape(n, 3, own, width).transpose(1, 0, 2, 3).reshape(3 * group, width) for tap in conv_taps
    ]
    last_full = interleave(gather_row(gather_dp(last_weight, n))).reshape(width, width)
    read_mine = gather_dp(read_weight.T, n).reshape(n * outs, width)

    cot = cotangent.reshape(-1, n, ranks, outs)
    cot = exchange_row([pick([cot[:, :, i] for i in range(ranks)], rows_at[q]) for q in range(ranks)])
    cot = jnp.concatenate(cot, axis=0).reshape(-1, n * outs)

    flat_in = images.reshape(patches, width)
    hat_one, scale_one = normalize(dot(flat_in, first_full))
    pre_one = hat_one * norm_swap[0] + norm_swap[1]
    low_one = jax.nn.silu(pre_one).astype(BF16)
    split = [low_one[:, i * group : (i + 1) * group] for i in range(ranks)]
    bands = exchange_row([pick(split, rows_at[q]) for q in range(ranks)])

    def stack_bands(pieces):
        whole = jnp.zeros((slots, ranks, band, cols, pieces[0].shape[-1]), pieces[0].dtype)
        for q in range(ranks):
            piece = pieces[q].reshape(slots, 1, band, cols, -1)
            whole = lax.dynamic_update_slice(whole, piece, (0, rows_at[q], 0, 0, 0))
        return whole.reshape(slots, high, cols, -1)

    def take_bands(value):
        value = value.reshape(slots, ranks, band * cols, -1)
        return [
            lax.dynamic_index_in_dim(value, rows_at[q], 1, keepdims=False).reshape(patches, -1)
            for q in range(ranks)
        ]

    wide_one = columns(stack_bands(bands))
    slabs = [wide_one[:, u : u + high].reshape(slots * high * cols, 3 * group) for u in range(3)]
    act_two = dot(slabs[0], conv_taps[0]) + dot(slabs[1], conv_taps[1]) + dot(slabs[2], conv_taps[2])
    hat_two, scale_two = normalize(scatter_row(take_bands(act_two)))
    pre_two = hat_two * norm_vals[2] + norm_vals[3]
    low_two = jax.nn.silu(pre_two).astype(BF16)
    hat_three, scale_three = normalize(dot(low_two, last_full))
    summed = flat_in.astype(F32) + (hat_three * norm_vals[4] + norm_vals[5])
    pooled = jnp.mean(summed.reshape(slots, band // 2, 2, cols // 2, 2, width), axis=(2, 4)).astype(BF16)
    pooled = pooled.reshape(-1, width)
    pools = jnp.concatenate(gather_row(pooled), axis=0)
    logits = dot_t(pools, read_mine) + bias_mine
    mask = (jnp.arange(slots, dtype=jnp.int32) < live_count[0]).astype(F32)
    mask = jnp.broadcast_to(mask[None, :, None], (ranks, slots, pooled.shape[0] // slots)).reshape(-1, 1)
    shown = (jax.nn.gelu(logits, approximate=False) * mask).astype(BF16)
    shown = exchange_row(jnp.split(shown, ranks, axis=0))
    readout = jnp.zeros((pooled.shape[0], n, ranks, outs), BF16)
    for q in range(ranks):
        readout = lax.dynamic_update_slice(
            readout, shown[q].reshape(-1, n, 1, outs), (0, 0, rows_at[q], 0)
        )
    readout_out = readout.reshape(slots, band // 2, cols // 2, n * ranks * outs)

    grad_low = (cot.astype(F32) * mask * gelu_slope(logits)).astype(BF16)
    read_terms = t_dot(grad_low, pools).reshape(n, outs, width)
    bias_terms = jnp.sum(grad_low.astype(F32), axis=0).reshape(n, 1, outs)
    bias_terms = jnp.pad(bias_terms, ((0, 0), (0, 7), (0, width - outs)))
    read_sum = scatter_dp(jnp.concatenate([read_terms, bias_terms], axis=1), n)
    read_grad, bias_grad = read_sum[:outs].T, read_sum[outs, :outs]
    grad_pool = scatter_row(jnp.split(dot(grad_low, read_mine), ranks, axis=0))
    grad_sum = (
        jnp.broadcast_to(
            grad_pool.reshape(slots, band // 2, 1, cols // 2, 1, width),
            (slots, band // 2, 2, cols // 2, 2, width),
        )
        * 0.25
    ).reshape(-1, width)
    gain_three = jnp.sum(grad_sum * hat_three, axis=0)
    shift_three = jnp.sum(grad_sum, axis=0)
    grad_three = norm_backward(grad_sum, hat_three, scale_three, norm_vals[4]).astype(BF16)
    grad_pre_two = dot_t(grad_three, last_full) * silu_slope(pre_two)
    gain_two = jnp.sum(grad_pre_two * hat_two, axis=0)
    shift_two = jnp.sum(grad_pre_two, axis=0)
    grad_two = norm_backward(grad_pre_two, hat_two, scale_two, norm_vals[2]).astype(BF16)
    grad_full = stack_bands(gather_row(grad_two))
    grad_flat = grad_full.reshape(-1, width)

    def row_sums(terms):
        terms = terms.reshape(n, ranks, -1, width)
        return scatter_row(
            [lax.dynamic_index_in_dim(terms, rows_at[q], 1, keepdims=False) for q in range(ranks)]
        )

    conv_grad = []
    for u in range(3):
        terms = t_dot(slabs[u], grad_flat).reshape(3, n, own, width).transpose(1, 0, 2, 3)
        conv_grad.append(scatter_dp(terms.reshape(n, 3 * own, width), n).reshape(3, own, width))
    conv_grad = jnp.stack(conv_grad)
    wide_grad = jnp.pad(grad_full, ((0, 0), (1, 1), (1, 1), (0, 0)))
    grad_mid = jnp.zeros((slots * high * cols, group), F32)
    for u in range(3):
        for v in range(3):
            slab = wide_grad[:, 2 - u : 2 - u + high, 2 - v : 2 - v + cols].reshape(-1, width)
            grad_mid = grad_mid + dot_t(slab, conv_taps[u][v * group : (v + 1) * group])
    pieces = exchange_row(take_bands(grad_mid.astype(BF16)))
    grad_low_one = jnp.concatenate(
        [pick([pieces[i ^ q] for i in range(ranks)], row) for q in range(ranks)], axis=1
    ).astype(F32)
    last_sum = scatter_dp(row_sums(t_dot(low_two, grad_three)), n)

    grad_pre_one = grad_low_one * silu_slope(pre_one)
    gain_one = jnp.sum(grad_pre_one * hat_one, axis=0)
    shift_one = jnp.sum(grad_pre_one, axis=0)
    grad_one = norm_backward(grad_pre_one, hat_one, scale_one, norm_swap[0]).astype(BF16)
    image_grad = (grad_sum + dot_t(grad_one, first_full)).astype(BF16)
    image_grad = image_grad.reshape(slots, band, cols, width)

    swapped = jnp.stack([gain_one, shift_one]).reshape(2, ranks, n, own).transpose(2, 1, 0, 3)
    plain = jnp.stack([gain_two, shift_two, gain_three, shift_three])
    plain = plain.reshape(4, n, ranks, own).transpose(1, 2, 0, 3)
    norm_terms = jnp.concatenate([swapped, plain], axis=2).reshape(n, ranks, 1, 6 * own)
    norm_terms = jnp.pad(norm_terms, ((0, 0), (0, 0), (0, 7), (0, width - 6 * own)))
    first_terms = t_dot(flat_in, grad_one).reshape(n, ranks, own, width)
    first_sum = scatter_dp(row_sums(jnp.concatenate([first_terms, norm_terms], axis=2)), n)
    norm_grad = first_sum[own, : 6 * own].reshape(6, own)
    first_grad = first_sum[:own].reshape(own, ranks, n, own).transpose(0, 2, 1, 3).reshape(own, width)
    return (
        readout_out,
        image_grad,
        first_grad,
        conv_grad,
        last_sum,
        norm_grad,
        read_grad,
        bias_grad,
    )


VM = pl.BlockSpec(memory_space=pltpu.VMEM)
SM = pl.BlockSpec(memory_space=pltpu.SMEM)
HB = pl.BlockSpec(memory_space=pltpu.HBM)


def shape(dims, dtype):
    return jax.ShapeDtypeStruct(dims, dtype)


def kernel(body, outs, ins, scratch, flops, moved, *arrays, specs=None, room=24):
    return pl.pallas_call(
        body,
        out_shape=outs,
        in_specs=ins,
        out_specs=jax.tree.map(lambda _: VM, outs) if specs is None else specs,
        scratch_shapes=scratch,
        cost_estimate=pl.CostEstimate(flops=flops // 64, bytes_accessed=moved // 64, transcendentals=0),
        compiler_params=pltpu.CompilerParams(vmem_limit_bytes=room << 20),
    )(*arrays)


def at_row(where, q):
    return where[0] ^ q


def start_all(copies):
    for copy in copies:
        copy.start()


def wait_all(copies):
    for copy in copies:
        copy.wait()


def copies_of(pairs, sems):
    return [pltpu.make_async_copy(a, b, sems.at[i]) for i, (a, b) in enumerate(pairs)]


def hop(x, turn):
    right, left = ring_pairs(RING)
    return lax.ppermute(x, "dp", right if turn else left)


def gather_step(state, step, low=None, high=None):
    pieces, a, b = state
    pieces = list(pieces)
    if step < RING // 2:
        a, b = hop(a, True), hop(b, False)
        pieces[RING - step], pieces[step] = a, b
    else:
        pieces[step] = (hop(low(a), True), hop(high(b), False))
    return pieces, a, b


def gather_state(x):
    return [x] * RING, x, x


def scatter_step(low, high, terms, a, b, step):
    half = RING // 2
    if step == half:
        return hop(low, True), hop(high, False)
    right, left = terms[step].astype(F32), terms[RING - step].astype(F32)
    if step == half - 1:
        cut = low.shape[0]
        right = jnp.concatenate([right[:cut] + a.astype(F32), right[cut:]], axis=0)
        left = jnp.concatenate([left[:cut], left[cut:] + b.astype(F32)], axis=0)
    else:
        right, left = right + a.astype(F32), left + b.astype(F32)
    return hop(right.astype(BF16), True), hop(left.astype(BF16), False)


def scatter_end(terms, a, b):
    return terms[0].astype(F32) + a.astype(F32) + b.astype(F32)


def fence(*values):
    return lax.optimization_barrier(values)


def line_up(where, *refs):
    pieces, (first, last) = refs[: RING + 1], refs[RING + 1 :]
    rows = last.shape[1]
    for k in range(RING):
        if k == RING // 2:
            last[where[2 + k]] = pieces[k][...]
            first[where[2 + k]] = pieces[RING][...]
        else:
            last[where[2 + k]] = pieces[k][:rows]
            first[where[2 + k]] = pieces[k][rows:]


def fill(where, weight, parts):
    rows = weight.shape[2]
    for q, part in enumerate(parts):
        weight[:, at_row(where, q)] = part[:, :rows, :]


def center(value):
    mean = jnp.mean(value, axis=-1, keepdims=True)
    gap = value - mean
    scale = lax.rsqrt(jnp.mean(gap * gap, axis=-1, keepdims=True) + eps)
    return gap * scale, scale


def flat_pieces(pieces):
    half = RING // 2
    return [p[0] if k == half else p for k, p in enumerate(pieces)] + [pieces[half][1]]


def stage_one(where, x, f0, f1, f2, f3, hat, scale, s0, s1, s2, s3, norms, weight, low):
    firsts = (f0, f1, f2, f3)
    fill(where, weight, firsts)
    width, rows = x.shape[1], weight.shape[2]
    total = jnp.zeros((8, width), F32)
    bias = total
    for q, first in enumerate(firsts):
        for k in range(RING):
            block = first[k, rows:, :].astype(F32)
            total = total + block
            if q == 0:
                bias = bias + block
    line = lax.broadcasted_iota(jnp.int32, (8, width), 0)
    table = jnp.where(line == 6, bias, total)
    norms[...] = table
    act = dot(x[...], weight[...].reshape(width, width))
    normed, root = center(act)
    hat[...] = normed
    scale[...] = root
    pre = normed * norms[0:1, :] + norms[1:2, :]
    low[...] = (pre * jax.nn.sigmoid(pre)).astype(BF16)
    part = width // 4
    for q, out in enumerate((s0, s1, s2, s3)):
        out[...] = low[:, pl.ds(pl.multiple_of(at_row(where, q) * part, part), part)]


def conv_copies(where, pieces, weight, sems):
    far = RING // 2
    pairs = []
    for k in range(RING):
        if k == far:
            number = pieces[far].shape[0]
            pairs.append((pieces[far], weight.at[pl.ds(0, number), where[2 + k]]))
            pairs.append((pieces[RING], weight.at[pl.ds(number, pieces[RING].shape[0]), where[2 + k]]))
        else:
            pairs.append((pieces[k], weight.at[:, where[2 + k]]))
    return copies_of(pairs, sems)


def conv_forward(dims, first, where, s0, s1, s2, s3, *refs):
    slots, rows, cols = dims
    if first:
        own, near, spans, weight, pad, moved, wide, sems, done = refs[RING + 1 :]
        copies = conv_copies(where, refs[: RING + 1], weight, sems)
        start_all(copies)
    else:
        weight, own, near, spans, pad, moved, wide, done = refs
    group = s0.shape[1]
    patches = rows * cols
    band = patches // 4
    pad[...] = jnp.zeros_like(pad)
    for q, piece in enumerate((s0, s1, s2, s3)):
        for i in range(slots):
            at = pl.multiple_of(cols + 8 + at_row(where, q) * band, 8)
            pad[i, pl.ds(at, band), :] = piece[i * band : (i + 1) * band, :].astype(F32)
    for v in range(3):
        for i in range(slots):
            shifted = pad[i, 8 + v - 1 : 8 + v - 1 + patches + 2 * cols, :]
            if v != 1:
                col = lax.broadcasted_iota(jnp.int32, shifted.shape, 0) % cols
                shifted = jnp.where(col == (0 if v == 0 else cols - 1), 0.0, shifted)
            moved[i] = shifted

        @pl.loop(0, 2 * slots)
        def _(j):
            q, i = j // slots, j % slots
            here = pl.ds(pl.multiple_of(j * band, 16), band)
            for u in range(3):
                at = pl.multiple_of(at_row(where, first + q) * band + u * cols, 8)
                t = u * 3 + v
                wide[here, t * group : (t + 1) * group] = moved[i, pl.ds(at, band), :].astype(BF16)

    keep = pltpu.make_async_copy(wide, spans, done)
    keep.start()
    if first:
        wait_all(copies)
    width = own.shape[1]
    chunk = 256
    patches = slots * band

    @pl.loop(0, width // chunk)
    def _(j):
        lanes = pl.ds(pl.multiple_of(j * chunk, chunk), chunk)
        terms = dot(wide[...], weight[:, :, :, lanes].reshape(-1, chunk))
        own[:, lanes] = terms[:patches]
        near[:, lanes] = terms[patches:].astype(BF16)

    keep.wait()


def stage_two(dims, where, own, near, cross, x, norms, l0, l1, l2, l3, hat_two, scale_two, low, hat, scale, pooled, weight, pairs):
    slots, rows, cols = dims
    fill(where, weight, (l0, l1, l2, l3))
    width = x.shape[1]
    act = own[...] + near[...].astype(F32) + cross[...].astype(F32)
    normed, root = center(act)
    hat_two[...] = normed
    scale_two[...] = root
    pre = normed * norms[2:3, :] + norms[3:4, :]
    low[...] = (pre * jax.nn.sigmoid(pre)).astype(BF16)
    normed, root = center(dot(low[...], weight[...].reshape(width, width)))
    hat[...] = normed
    scale[...] = root
    y = x[...].astype(F32) + (normed * norms[4:5, :] + norms[5:6, :])
    y = jnp.sum(y.reshape(slots * rows // 2, 2, cols, width), axis=1).reshape(-1, width)
    count = pooled.shape[0]
    for g in range(pairs.shape[0]):
        lanes = slice(g * 128, (g + 1) * 128)
        pairs[g] = y[:, lanes]
        pooled[:, lanes] = (
            0.25 * (pairs[g, pl.ds(0, count, stride=2), :] + pairs[g, pl.ds(1, count, stride=2), :])
        ).astype(BF16)


def read_copies(where, pieces, weight, sems):
    half = RING // 2
    pairs = []
    for k in range(RING):
        if k == half:
            rows = pieces[half].shape[0]
            pairs.append((pieces[half], weight.at[where[2 + k], pl.ds(0, rows)]))
            pairs.append((pieces[RING], weight.at[where[2 + k], pl.ds(rows, rows)]))
        else:
            pairs.append((pieces[k], weight.at[where[2 + k]]))
    return copies_of(pairs, sems)


def readout(slots, where, p0, p1, p2, p3, c0, c1, c2, c3, norms, *refs):
    pieces = refs[: RING + 1]
    o0, o1, o2, o3, low, own, near, far, weight, sems = refs[RING + 1 :]
    copies = read_copies(where, pieces, weight, sems)
    start_all(copies)
    count, width = p0.shape
    table = jnp.concatenate([p[...] for p in (p0, p1, p2, p3)], axis=0)
    line = lax.broadcasted_iota(jnp.int32, (count, width), 0)
    mask = jnp.where(line // (count // slots) < where[1], 1.0, 0.0)
    wait_all(copies)
    whole = weight[...].reshape(-1, width)
    logits = dot_t(table, whole) + norms[6:7, :]
    for q, (cot, out) in enumerate(((c0, o0), (c1, o1), (c2, o2), (c3, o3))):
        z = logits[q * count : (q + 1) * count]
        phi = 0.5 * (1.0 + lax.erf(z * 0.7071067811865476))
        out[...] = (z * phi * mask).astype(BF16)
        slope = phi + z * jnp.exp(-0.5 * z * z) * 0.3989422804014327
        low[q * count : (q + 1) * count, :] = (cot[...].astype(F32) * mask * slope).astype(BF16)
    back = dot(low[...], whole)
    own[...] = back[:count]
    near[0] = back[count : 2 * count].astype(BF16)
    far[...] = back[2 * count : 3 * count]
    near[1] = back[3 * count :].astype(BF16)


def readout_terms(where, low, p0, p1, p2, p3, upper, lower, out, terms):
    width = p0.shape[1]
    table = jnp.concatenate([p[...] for p in (p0, p1, p2, p3)], axis=0)
    terms[...] = t_dot(low[...], table).reshape(terms.shape)
    bias = jnp.sum(low[...].astype(F32), axis=0, keepdims=True)
    rows = terms.shape[1]
    for k in range(RING):
        out[k, :rows, :] = terms[where[2 + k]].astype(BF16)
        out[k, rows:, :] = jnp.broadcast_to(bias, (out.shape[1] - rows, width)).astype(BF16)
    upper[...] = out[RING // 2, : upper.shape[0]]
    lower[...] = out[RING // 2, upper.shape[0] :]


def spread(pairs, grad, dims):
    slots, rows, cols = dims
    count, width = grad.shape
    for g in range(pairs.shape[0]):
        lanes = slice(g * 128, (g + 1) * 128)
        pairs[g, pl.ds(0, count, stride=2), :] = grad[:, lanes]
        pairs[g, pl.ds(1, count, stride=2), :] = grad[:, lanes]
    half = slots * rows // 2
    both = jnp.concatenate([pairs[g] for g in range(pairs.shape[0])], axis=1)
    both = jnp.broadcast_to(both.reshape(half, 1, cols, width), (half, 2, cols, width))
    return both.reshape(-1, width) * 0.25


def back_norm(grad, normed, root, gain):
    weighted = grad * gain
    return root * (
        weighted
        - jnp.mean(weighted, axis=-1, keepdims=True)
        - normed * jnp.mean(weighted * normed, axis=-1, keepdims=True)
    )


def total_rows(value):
    return jnp.sum(value, axis=0, keepdims=True)


def stage_two_back(dims, where, own, near, cross, hat, scale, hat_two, scale_two, norms, weight, grad_three, grad_two, pool_sum, sums, pairs):
    width = hat.shape[1]
    grad = own[...] + near[...].astype(F32) + cross[...].astype(F32)
    pool_sum[...] = grad
    gy = spread(pairs, grad, dims)
    sums[...] = jnp.zeros_like(sums)
    sums[4:5, :] = total_rows(gy * hat[...])
    sums[5:6, :] = total_rows(gy)
    grad_three[...] = back_norm(gy, hat[...], scale[...], norms[4:5, :]).astype(BF16)
    gs = dot_t(grad_three[...], weight[...].reshape(width, width))
    pre = hat_two[...] * norms[2:3, :] + norms[3:4, :]
    gn = gs * silu_slope(pre)
    sums[2:3, :] = total_rows(gn * hat_two[...])
    sums[3:4, :] = total_rows(gn)
    grad_two[...] = back_norm(gn, hat_two[...], scale_two[...], norms[2:3, :]).astype(BF16)


def last_terms(where, low, grad, own, near, far, terms):
    terms[...] = t_dot(low[...], grad[...]).reshape(terms.shape)
    for k in range(RING):
        own[k] = terms[where[2 + k], at_row(where, 0)]
        near[0, k] = terms[where[2 + k], at_row(where, 1)].astype(BF16)
        far[k] = terms[where[2 + k], at_row(where, 2)]
        near[1, k] = terms[where[2 + k], at_row(where, 3)].astype(BF16)


def stack_grad(dims, where, pieces, whole):
    slots, rows, cols = dims
    band = rows * cols // 4
    for q, piece in enumerate(pieces):
        for i in range(slots):
            at = pl.multiple_of(i * rows * cols + at_row(where, q) * band, 16)
            whole[pl.ds(at, band), :] = piece[i * band : (i + 1) * band, :]


def conv_half_terms(where, here, g0, g1, out, one):
    count = g0.shape[0]
    one[:count], one[count:] = g0[...], g1[...]
    group = out.shape[1]

    @pl.loop(0, out.shape[0])
    def _(t):
        lanes = pl.ds(pl.multiple_of(t * group, group), group)
        out[t] = t_dot(here[:, lanes], one[...])


def conv_terms(first, number, next_to, where, half, there, g2, g3, *refs):
    parts, (far, side, out, two) = refs[:-4], refs[-4:]
    count = g2.shape[0]
    two[:count], two[count:] = g2[...], g3[...]
    rows, width = out.shape[2:]
    group = RING * rows

    @pl.loop(0, number)
    def _(t):
        lanes = pl.ds(pl.multiple_of((first + t) * group, group), group)
        terms = half[first + t] + t_dot(there[:, lanes], two[...])
        terms = terms.astype(BF16).reshape(RING, rows, width)
        for k in range(RING):
            out[where[2 + RING + k], t] = terms[k]

    if parts:
        own, near, low, high = parts
        half_way = RING // 2
        for a, b, cross in ((0, half_way, low), (half_way, RING, high)):
            out[a:b, number] = (own[a:b] + near[0, a:b].astype(F32) + cross[...].astype(F32)).astype(BF16)
    far[...] = out[RING // 2]
    side[...] = out[next_to]


def conv_back(dims, where, g0, g1, g2, g3, weight, o0, o1, o2, o3, whole, held, low):
    slots, rows, cols = dims
    stack_grad(dims, where, (g0, g1, g2, g3), whole)
    patches = rows * cols
    band = patches // 4
    group = o0.shape[1]
    width = whole.shape[1]
    held[...] = jnp.zeros_like(held)
    @pl.loop(0, 3)
    def _(u):
        at = pl.ds(pl.multiple_of(8 + u * cols, 8), patches)
        for v in range(3):
            part = dot_t(whole[...], weight[u * 3 + v].reshape(group, width))
            for i in range(slots):
                held[v, i, at, :] += part[i * patches : (i + 1) * patches]

    col = lax.broadcasted_iota(jnp.int32, (patches, group), 0) % cols
    for i in range(slots):
        value = held[1, i, 8 + cols : 8 + cols + patches, :]
        value += jnp.where(col == cols - 1, 0.0, held[0, i, 9 + cols : 9 + cols + patches, :])
        value += jnp.where(col == 0, 0.0, held[2, i, 7 + cols : 7 + cols + patches, :])
        low[i * patches : (i + 1) * patches, :] = value.astype(BF16)
    for q, out in enumerate((o0, o1, o2, o3)):
        for i in range(slots):
            at = pl.multiple_of(i * patches + at_row(where, q) * band, 16)
            out[i * band : (i + 1) * band, :] = low[pl.ds(at, band), :]


def stage_one_back(where, b0, b1, b2, b3, hat, scale, norms, x, sums, grad_one, own, near, far, low, terms):
    width = hat.shape[1]
    part = width // 4
    for q, piece in enumerate((b0, b1, b2, b3)):
        low[:, pl.ds(pl.multiple_of(at_row(where, q) * part, part), part)] = piece[...]
    pre = hat[...] * norms[0:1, :] + norms[1:2, :]
    gn = low[...].astype(F32) * silu_slope(pre)
    line = lax.broadcasted_iota(jnp.int32, (8, width), 0)
    tail = jnp.where(line == 0, total_rows(gn * hat[...]), jnp.where(line == 1, total_rows(gn), sums[...]))
    grad_one[...] = back_norm(gn, hat[...], scale[...], norms[0:1, :]).astype(BF16)
    terms[...] = t_dot(x[...], grad_one[...]).reshape(terms.shape)
    rows = terms.shape[2]
    for k in range(RING):
        own[k, :rows] = terms[where[2 + k], at_row(where, 0)]
        near[0, k, :rows] = terms[where[2 + k], at_row(where, 1)].astype(BF16)
        far[k, :rows] = terms[where[2 + k], at_row(where, 2)]
        near[1, k, :rows] = terms[where[2 + k], at_row(where, 3)].astype(BF16)
        own[k, rows:] = tail
        near[0, k, rows:] = tail.astype(BF16)
        far[k, rows:] = tail
        near[1, k, rows:] = tail.astype(BF16)


def image_back(dims, where, grad_one, pool_sum, weight, out, pairs):
    width = grad_one.shape[1]
    gy = spread(pairs, pool_sum[...], dims)
    out[...] = (gy + dot_t(grad_one[...], weight[...].reshape(width, width))).astype(BF16)


def split_columns(where, x, o0, o1, o2, o3):
    lanes = x.shape[1] // (4 * RING)
    for q, out in enumerate((o0, o1, o2, o3)):
        for g in range(RING):
            at = pl.multiple_of((g * 4 + at_row(where, q)) * lanes, lanes)
            out[:, g * lanes : (g + 1) * lanes] = x[:, pl.ds(at, lanes)]


def join_columns(where, i0, i1, i2, i3, out):
    lanes = out.shape[1] // (4 * RING)
    for q, piece in enumerate((i0, i1, i2, i3)):
        for g in range(RING):
            at = pl.multiple_of((g * 4 + at_row(where, q)) * lanes, lanes)
            out[:, pl.ds(at, lanes)] = piece[:, g * lanes : (g + 1) * lanes]


def ringed(
    images,
    first_weight,
    conv_weight,
    last_weight,
    norm_rows,
    read_weight,
    read_bias,
    cotangent,
    live_count,
):
    dp, row = lax.axis_index("dp"), lax.axis_index("row")
    slots, band, cols, width = images.shape
    dims = (slots, band, cols)
    full = (slots, 4 * band, cols)
    patches = slots * band * cols
    count = patches // 4
    own = first_weight.shape[0]
    group = RING * own
    outs = read_weight.shape[1]
    taps = 9
    DMA = pltpu.SemaphoreType.DMA
    index = jnp.arange(18, dtype=jnp.int32)
    place_of = lambda d: jnp.where(d % 2 == 0, d // 2, RING - 1 - d // 2)
    place = (place_of(dp) + index - 2) % RING
    ahead = jnp.where(place < RING // 2, 2 * place, 2 * (RING - 1 - place) + 1)
    steps = (place_of(index - 10) - place_of(dp)) % RING
    where = jnp.where(index == 0, row, jnp.where(index == 1, live_count[0], jnp.where(index < 10, ahead, steps)))
    where = where.astype(jnp.int32)

    first_mine = first_weight.reshape(own, RING, 4, own).transpose(0, 2, 1, 3).reshape(own, width)
    lane = jnp.arange(width, dtype=jnp.int32)[None, :]
    tiled = jnp.tile(norm_rows, (1, width // own))
    at = jnp.where(jnp.arange(6)[:, None] < 2, row * RING + dp, dp * 4 + row)
    small = jnp.where(lane // own == at, tiled, 0).astype(BF16)
    bias = jnp.where(lane // outs == dp, jnp.tile(read_bias, width // outs)[None, :], 0).astype(BF16)
    small = jnp.concatenate([small, bias, jnp.zeros((1, width), BF16)], axis=0)
    first_mine = jnp.concatenate([first_mine, small], axis=0)
    conv = conv_weight.reshape(taps, own, width)
    quarter = shape((count, width), BF16)
    wide_f32, thin_f32, wide_bf16 = (
        shape((patches, width), F32),
        shape((patches, 1), F32),
        shape((patches, width), BF16),
    )
    quarter_f32, near_quarter = shape((count, width), F32), shape((2, count, width), BF16)
    piece = shape((patches, group), BF16)
    block = (RING, own, width)
    matmul = 2 * patches * width * width
    square = 2 * width * width
    square_of = shape((RING, 4, own, width), BF16)
    total = 4 * patches
    pad_rows = full[1] * cols + 2 * cols + 16
    pair_scratch = pltpu.VMEM((width // 128, patches // 2, 128), F32)
    x = images.reshape(patches, width)

    far = RING // 2
    cut = own + 8
    low, high = lambda v: v[:own], lambda v: v[own:]
    more = gather_step(gather_state(conv), 1)
    ring = gather_step(gather_state(jnp.concatenate([last_weight, first_mine], axis=0)), 1)
    read = read_weight.T
    cots = cotangent.reshape(count, -1)
    more, ring, where, read, cots, x = fence(more, ring, where, read, cots, x)
    ring = gather_step(ring, 2)
    cots = kernel(split_columns, [quarter] * 4, [SM, VM], [], 0, 2 * count * 4 * width * 2, where, cots)
    ring, cots = fence(ring, cots)
    ring = gather_step(ring, 3)
    ring = fence(ring)[0]
    ring = gather_step(ring, 4, low, high)
    more, ring = fence(more, ring)
    ring = ring[0]
    firsts, lasts = kernel(
        line_up,
        [shape((RING, cut, width), BF16), shape((RING, own, width), BF16)],
        [SM] + [VM] * (RING + 1),
        [],
        0,
        4 * RING * (cut + own) * width,
        where,
        *flat_pieces(ring),
    )
    more = gather_step(more, 2)
    first_two, first_one = swap_row(firsts, 2), swap_row(firsts, 1)
    more, firsts, first_two, first_one, lasts = fence(more, firsts, first_two, first_one, lasts)
    more = gather_step(more, 3)
    firsts = [firsts, first_one, first_two, swap_row(first_two, 1)]
    last_two, last_one = swap_row(lasts, 2), swap_row(lasts, 1)
    hat_one, scale_one, *lows, norms, first_full = kernel(
        stage_one,
        [wide_f32, thin_f32] + [piece] * 4 + [shape((8, width), F32), square_of],
        [SM] + [VM] * 5,
        [pltpu.VMEM((patches, width), BF16)],
        matmul,
        square + 8 * patches * width,
        where,
        x,
        *firsts,
    )
    more, lows, lasts, last_two, last_one = fence(more, lows, lasts, last_two, last_one)
    taps_half = (taps + 1) // 2
    more = gather_step(more, 4, lambda v: v[:taps_half], lambda v: v[taps_half:])
    lows = exchange_row(lows)
    lasts = [lasts, last_one, last_two, swap_row(last_two, 1)]
    weights = flat_pieces(more[0])
    weights, lows, lasts, read, cots = fence(weights, lows, lasts, read, cots)

    conv_whole = (taps, RING, own, width)

    def conv_half(first, weights):
        return kernel(
            functools.partial(conv_forward, full, first),
            [wide_f32, wide_bf16, shape((2 * patches, taps * group), BF16)]
            + ([shape(conv_whole, BF16)] if first else []),
            [SM] + [VM] * 4 + ([HB] * (RING + 1) if first else [VM]),
            [
                pltpu.VMEM((slots, pad_rows, group), F32),
                pltpu.VMEM((slots, pad_rows - 16, group), F32),
                pltpu.VMEM((2 * patches, taps * group), BF16),
            ]
            + ([DMA((RING + 1,))] if first else [])
            + [DMA],
            9 * matmul // 2,
            9 * square + 6 * patches * width + 4 * patches * taps * group,
            where,
            *lows,
            *weights,
            specs=[VM, VM, HB] + ([VM] if first else []),
        )

    read = gather_step(gather_state(read), 1)
    cots = exchange_row(cots)
    away, near, spans_far, conv_full = conv_half(2, weights)
    away, near, read, cots = fence(away, near, read, cots)
    other = (away + swap_row(near, 1).astype(F32)).astype(BF16)
    other, lows, read = fence(other, lows, read)
    cross = swap_row(other, 2)
    read = gather_step(read, 2)
    mine, near, spans_near = conv_half(0, (conv_full,))
    near = fence(near, mine)[0]
    near = swap_row(near, 1)
    mine, near, cross = fence(mine, near, cross)
    read = gather_step(read, 3)
    hat_two, scale_two, low_two, hat_three, scale_three, pooled, last_full = kernel(
        functools.partial(stage_two, dims),
        [wide_f32, thin_f32, wide_bf16, wide_f32, thin_f32, quarter, square_of],
        [SM] + [VM] * 9,
        [pair_scratch],
        matmul,
        square + 24 * patches * width,
        where,
        mine,
        near,
        cross,
        x,
        norms,
        *lasts,
    )
    read = gather_step(read, 4, lambda v: v[: outs // 2], lambda v: v[outs // 2 :])
    pool_two, pool_one = swap_row(pooled, 2), swap_row(pooled, 1)
    pooled, pool_two, pool_one = fence(pooled, pool_two, pool_one)
    pools = [pooled, pool_one, pool_two, swap_row(pool_two, 1)]
    *shown, grad_low, mine, near, away = kernel(
        functools.partial(readout, slots),
        [quarter] * 4 + [wide_bf16, quarter_f32, near_quarter, quarter_f32],
        [SM] + [VM] * 9 + [HB] * (RING + 1),
        [pltpu.VMEM((RING, outs, width), BF16), DMA((RING + 1,))],
        2 * matmul,
        square + 12 * patches * width,
        where,
        *pools,
        *cots,
        norms,
        *flat_pieces(read[0]),
    )

    near = swap_row(near, 1)
    other = (away + near[1].astype(F32)).astype(BF16)
    other, grad_low, near = fence(other, grad_low, near)
    cross = swap_row(other, 2)
    half_read = shape(((outs + 16) // 2, width), BF16)
    *read_far, read_terms = kernel(
        readout_terms,
        [half_read, half_read, shape((RING, outs + 16, width), BF16)],
        [SM] + [VM] * 5,
        [pltpu.VMEM((RING, outs, width), F32)],
        matmul,
        2 * square,
        where,
        grad_low,
        *pools,
    )
    cross, read_far, read_terms, near = fence(cross, read_far, read_terms, near)
    read_a, read_b = scatter_step(*read_far, read_terms, None, None, 4)
    grad_three, grad_two, pool_sum, sums = kernel(
        functools.partial(stage_two_back, dims),
        [wide_bf16, wide_bf16, quarter_f32, shape((8, width), F32)],
        [SM] + [VM] * 9,
        [pair_scratch],
        matmul,
        square + 14 * patches * width,
        where,
        mine,
        near[0],
        cross,
        hat_three,
        scale_three,
        hat_two,
        scale_two,
        norms,
        last_full,
    )
    grad_three, grad_two, read_a, read_b = fence(grad_three, grad_two, read_a, read_b)
    grad_far, grad_next = swap_row(grad_two, 2), swap_row(grad_two, 1)
    read_a, read_b = scatter_step(*read_far, read_terms, read_a, read_b, 3)
    read_a, read_b = scatter_step(*read_far, read_terms, read_a, read_b, 2)
    here = kernel(
        conv_half_terms,
        shape((taps, group, width), F32),
        [SM] + [VM] * 3,
        [pltpu.VMEM((2 * patches, width), BF16)],
        9 * matmul // 2,
        18 * square,
        where,
        spans_near,
        grad_two,
        grad_next,
    )
    last_own, last_near, last_far = kernel(
        last_terms,
        [shape(block, F32), shape((2,) + block, BF16), shape(block, F32)],
        [SM, VM, VM],
        [pltpu.VMEM((RING, 4, own, width), F32)],
        matmul,
        3 * square,
        where,
        low_two,
        grad_three,
    )
    grad_two, grad_far, grad_next, last_near, last_far, read_a, read_b, here = fence(
        grad_two, grad_far, grad_next, last_near, last_far, read_a, read_b, here
    )
    grads = [grad_two, grad_next, grad_far, swap_row(grad_far, 1)]
    last_near = swap_row(last_near, 1)
    last_low = (last_far[:far] + last_near[1, :far].astype(F32)).astype(BF16)
    last_high = (last_far[far:] + last_near[1, far:].astype(F32)).astype(BF16)
    grads, last_near, last_low, last_high = fence(grads, last_near, last_low, last_high)
    last_low = swap_row(last_low, 2)
    read_a, read_b = scatter_step(*read_far, read_terms, read_a, read_b, 1)

    def weight_terms(first, number, next_to, parts):
        held = number + len(parts) // 4
        some = shape((held, own, width), BF16)
        return kernel(
            functools.partial(conv_terms, first, number, next_to),
            [some, some, shape((RING, held, own, width), BF16)],
            [SM] + [VM] * (4 + len(parts)),
            [pltpu.VMEM((2 * patches, width), BF16)],
            matmul * number,
            2 * square * number,
            where,
            here,
            spans_far,
            *grads[2:],
            *parts,
        )

    def add_to(terms, k, value):
        return (terms[k % RING].astype(F32) + value.astype(F32)).astype(BF16)

    one_far, one_side, one = weight_terms(0, 5, 5, ())
    one_far, one_side, one, grads, last_low, last_high, read_a, read_b = fence(
        one_far, one_side, one, grads, last_low, last_high, read_a, read_b
    )
    last_high = swap_row(last_high, 2)
    one_a, one_b = hop(one_far, True), hop(one_side, False)
    backs = kernel(
        functools.partial(conv_back, full),
        [piece] * 4,
        [SM] + [VM] * 5,
        [
            pltpu.VMEM((total, width), BF16),
            pltpu.VMEM((3, slots, pad_rows, group), F32),
            pltpu.VMEM((total, group), BF16),
        ],
        9 * matmul,
        9 * square + 12 * patches * width,
        where,
        *grads,
        conv_full,
    )
    one_a, one_b, backs, grads, last_high = fence(one_a, one_b, backs, grads, last_high)
    one_a, one_b = hop(add_to(one, 3, one_a), True), hop(add_to(one, -2, one_b), False)
    backs = exchange_row(backs)
    two_far, two_side, two = weight_terms(5, 4, 3, (last_own, last_near, last_low, last_high))
    one_a, one_b, two_far, two_side, two, backs = fence(one_a, one_b, two_far, two_side, two, backs)
    two_a, two_b = hop(two_side, True), hop(two_far, False)
    one_a, one_b = add_to(one, 2, one_a), add_to(one, -1, one_b)
    block = (RING, own + 8, width)
    grad_one, first_own, first_near, first_far = kernel(
        stage_one_back,
        [wide_bf16, shape(block, F32), shape((2,) + block, BF16), shape(block, F32)],
        [SM] + [VM] * 9,
        [pltpu.VMEM((patches, width), BF16), pltpu.VMEM((RING, 4, own, width), F32)],
        matmul,
        3 * square + 8 * patches * width,
        where,
        *backs,
        hat_one,
        scale_one,
        norms,
        x,
        sums,
    )
    one_a, one_b, two_a, two_b, grad_one, first_own, first_near, first_far, shown = fence(
        one_a, one_b, two_a, two_b, grad_one, first_own, first_near, first_far, shown
    )
    one_a, one_b = hop(one_a, True), hop(one_b, False)
    two_a, two_b = add_to(two, 2, two_a), add_to(two, -3, two_b)
    first_near = swap_row(first_near, 1)
    shown = exchange_row(shown)
    first_low = (first_far[:far] + first_near[1, :far].astype(F32)).astype(BF16)
    first_high = (first_far[far:] + first_near[1, far:].astype(F32)).astype(BF16)
    one_a, one_b_end, two_a, two_b, first_near, first_low, first_high, shown = fence(
        one_a, one_b, two_a, two_b, first_near, first_low, first_high, shown
    )
    two_a, two_b = hop(two_a, True), hop(two_b, False)
    one_a = add_to(one, 1, one_a)
    first_high = swap_row(first_high, 2)
    image_grad = kernel(
        functools.partial(image_back, dims),
        wide_bf16,
        [SM, VM, VM, VM],
        [pair_scratch],
        matmul,
        square + 8 * patches * width,
        where,
        grad_one,
        pool_sum,
        first_full,
    ).reshape(slots, band, cols, width)
    one_a, two_a, two_b, first_low, first_high, image_grad = fence(
        one_a, two_a, two_b, first_low, first_high, image_grad
    )
    one_a, two_b = hop(one_a, True), hop(add_to(two, -2, two_b), False)
    first_low = swap_row(first_low, 2)
    first_high = (first_own[far:] + first_near[0, far:].astype(F32) + first_high.astype(F32)).astype(BF16)
    two_a = add_to(two, 1, fence(two_a, first_high)[0])
    one_a, two_a, two_b, first_low, first_high, shown = fence(one_a, two_a, two_b, first_low, first_high, shown)
    first_a, first_b = hop(first_high[0], True), hop(first_high[1], False)
    two_a, two_b = hop(two_a, True), hop(add_to(two, -1, two_b), False)
    first_low = (first_own[:far] + first_near[0, :far].astype(F32) + first_low.astype(F32)).astype(BF16)
    readout_out = kernel(
        join_columns,
        shape((count, 4 * width), BF16),
        [SM] + [VM] * 4,
        [],
        0,
        16 * count * width,
        where,
        *shown,
    ).reshape(slots, band // 2, cols // 2, 4 * width)
    read_sum = scatter_end(read_terms, read_a, read_b)
    two_a, two_b, first_a, first_b, first_low, readout_out, read_sum = fence(
        two_a, two_b, first_a, first_b, first_low, readout_out, read_sum
    )
    first_a, first_b = hop(add_to(first_low, 3, first_a), True), hop(add_to(first_high[far - 2 :], 0, first_b), False)
    read_grad, bias_row = read_sum[:outs].T, read_sum[outs]
    bias_grad = lax.dynamic_slice_in_dim(bias_row, dp * outs, outs)
    first_a, first_b, read_grad = fence(first_a, first_b, read_grad)
    first_a, first_b = hop(add_to(first_low, 2, first_a), True), hop(add_to(first_high[far - 1 :], 0, first_b), False)
    two_sum = scatter_end(two, two_a, two_b)
    conv_grad = jnp.concatenate([scatter_end(one, one_a, one_b_end), two_sum[:4]], axis=0)
    conv_grad = conv_grad.reshape(3, 3, own, width)
    first_a, first_b, conv_grad = fence(first_a, first_b, conv_grad)
    first_a = hop(add_to(first_low, 1, first_a), True)
    tail = first_low[0].astype(F32) + first_a.astype(F32) + first_b.astype(F32)
    first_grad = tail[:own].reshape(own, 4, RING, own).transpose(0, 2, 1, 3).reshape(own, width)
    last_grad = two_sum[4]
    swapped = lax.dynamic_slice(tail, (own, (row * RING + dp) * own), (2, own))
    plain = lax.dynamic_slice(tail, (own + 2, (dp * 4 + row) * own), (4, own))
    norm_grad = jnp.concatenate([swapped, plain], axis=0)
    return (
        readout_out,
        image_grad,
        first_grad,
        conv_grad,
        last_grad,
        norm_grad,
        read_grad,
        bias_grad,
    )


def per_device(*arrays):
    if lax.axis_size("dp") == RING and lax.axis_size("row") == 4:
        return ringed(*arrays)
    return generic(*arrays)


def solution(mesh):
    return jax.shard_map(
        per_device,
        mesh=mesh,
        in_specs=(
            P("dp", "row", None, None),
            P(("dp", "row"), None),
            P(None, None, ("dp", "row"), None),
            P(("dp", "row"), None),
            P(None, ("dp", "row")),
            P(None, ("dp", "row")),
            P(("dp", "row")),
            P("dp", "row", None, None),
            P("dp"),
        ),
        out_specs=(
            P("dp", "row", None, None),
            P("dp", "row", None, None),
            P(("dp", "row"), None),
            P(None, None, ("dp", "row"), None),
            P(("dp", "row"), None),
            P(None, ("dp", "row")),
            P(None, ("dp", "row")),
            P(("dp", "row")),
        ),
        check_vma=False,
    )
```

```python
import functools

import jax
import jax.numpy as jnp
from jax import lax
from jax.experimental import pallas as pl
from jax.experimental.pallas import tpu as pltpu

from jax.sharding import PartitionSpec as P

eps = 1e-06
F32 = jnp.float32
BF16 = jnp.bfloat16
RING = 8


def ring_order(n):
    return list(range(0, n, 2)) + list(range(n - 1, 0, -2))


def ring_pairs(n):
    order = ring_order(n)
    right = [(order[i], order[(i + 1) % n]) for i in range(n)]
    left = [(b, a) for a, b in right]
    return right, left


def ring_index(n, step):
    me = lax.axis_index("dp")
    place = jnp.where(me % 2 == 0, me // 2, n - 1 - me // 2)
    place = (place + step) % n
    return jnp.where(place < n // 2, 2 * place, 2 * (n - 1 - place) + 1)


def gather_dp(x, n):
    return lax.all_gather(x, "dp", axis=0, tiled=False)


def scatter_dp(parts, n):
    return lax.psum_scatter(parts.astype(F32), "dp", scatter_dimension=0, tiled=False)


def swap_row(x, q):
    return lax.ppermute(x, "row", [(i, i ^ q) for i in range(4)])


def gather_row(x):
    two = swap_row(x, 2)
    one = swap_row(x, 1)
    return [x, one, two, swap_row(two, 1)]


def exchange_row(pieces):
    return [pieces[0]] + [swap_row(pieces[q], q) for q in (1, 2, 3)]


def scatter_row(pieces):
    near = swap_row(jnp.stack([pieces[1], pieces[3]]).astype(BF16), 1).astype(F32)
    mine = pieces[0].astype(F32) + near[0]
    other = (pieces[2].astype(F32) + near[1]).astype(BF16)
    return mine + swap_row(other, 2).astype(F32)


def pick(choices, index):
    value = choices[0]
    for i in range(1, len(choices)):
        value = jnp.where(index == i, choices[i], value)
    return value


def dot(left, right):
    return jnp.dot(left, right, preferred_element_type=F32)


def dot_t(left, right):
    return lax.dot_general(left, right, (((1,), (1,)), ((), ())), preferred_element_type=F32)


def t_dot(left, right):
    return lax.dot_general(left, right, (((0,), (0,)), ((), ())), preferred_element_type=F32)


def normalize(value):
    centred = value - jnp.mean(value, axis=-1, keepdims=True)
    scale = lax.rsqrt(jnp.mean(centred * centred, axis=-1, keepdims=True) + eps)
    return centred * scale, scale


def norm_backward(grad_out, normed, scale, gain):
    weighted = grad_out * gain
    return scale * (
        weighted
        - jnp.mean(weighted, axis=-1, keepdims=True)
        - normed * jnp.mean(weighted * normed, axis=-1, keepdims=True)
    )


def silu_slope(value):
    gate = jax.nn.sigmoid(value)
    return gate * (1.0 + value * (1.0 - gate))


def gelu_slope(value):
    return (
        0.5 * (1.0 + lax.erf(value * 0.7071067811865476))
        + value * jnp.exp(-0.5 * value * value) * 0.3989422804014327
    )


def columns(value):
    cols = value.shape[2]
    wide = jnp.pad(value, ((0, 0), (1, 1), (1, 1), (0, 0)))
    return jnp.concatenate([wide[:, :, v : v + cols] for v in range(3)], axis=3)


def generic(
    images,
    first_weight,
    conv_weight,
    last_weight,
    norm_rows,
    read_weight,
    read_bias,
    cotangent,
    live_count,
):
    n, ranks = lax.axis_size("dp"), lax.axis_size("row")
    row = lax.axis_index("row")
    slots, band, cols, width = images.shape
    patches = slots * band * cols
    high = ranks * band
    own = first_weight.shape[0]
    group = n * own
    outs = read_weight.shape[1]
    rows_at = [row ^ q for q in range(ranks)]

    first_mine = first_weight.reshape(own, n, ranks, own).transpose(0, 2, 1, 3).reshape(own, width)
    small = jnp.concatenate([norm_rows.reshape(-1), read_bias])
    small = jnp.pad(small, (0, 8 * width - small.shape[0])).reshape(8, width)
    first_ring = gather_dp(jnp.concatenate([first_mine, small], axis=0), n)
    first_parts = gather_row(first_ring)

    def interleave(parts):
        whole = jnp.zeros((n, ranks) + parts[0].shape[1:], parts[0].dtype)
        for q in range(ranks):
            whole = lax.dynamic_update_slice(whole, parts[q][:, None], (0, rows_at[q], 0, 0))
        return whole

    first_all = interleave(first_parts)
    first_full = first_all[:, :, :own].reshape(width, width)
    norms = first_all[:, :, own].reshape(n, ranks, width)[:, :, : 6 * own]
    norms = norms.reshape(n, ranks, 6, own).astype(F32)
    norm_vals = norms.transpose(2, 0, 1, 3).reshape(6, width)
    norm_swap = norms.transpose(2, 1, 0, 3).reshape(6, width)
    bias_mine = first_ring[:, own, 6 * own : 6 * own + outs].reshape(n * outs).astype(F32)

    conv_taps = [gather_dp(conv_weight[u].reshape(3 * own, width), n) for u in range(3)]
    conv_taps = [
        tap.reshape(n, 3, own, width).transpose(1, 0, 2, 3).reshape(3 * group, width) for tap in conv_taps
    ]
    last_full = interleave(gather_row(gather_dp(last_weight, n))).reshape(width, width)
    read_mine = gather_dp(read_weight.T, n).reshape(n * outs, width)

    cot = cotangent.reshape(-1, n, ranks, outs)
    cot = exchange_row([pick([cot[:, :, i] for i in range(ranks)], rows_at[q]) for q in range(ranks)])
    cot = jnp.concatenate(cot, axis=0).reshape(-1, n * outs)

    flat_in = images.reshape(patches, width)
    hat_one, scale_one = normalize(dot(flat_in, first_full))
    pre_one = hat_one * norm_swap[0] + norm_swap[1]
    low_one = jax.nn.silu(pre_one).astype(BF16)
    split = [low_one[:, i * group : (i + 1) * group] for i in range(ranks)]
    bands = exchange_row([pick(split, rows_at[q]) for q in range(ranks)])

    def stack_bands(pieces):
        whole = jnp.zeros((slots, ranks, band, cols, pieces[0].shape[-1]), pieces[0].dtype)
        for q in range(ranks):
            piece = pieces[q].reshape(slots, 1, band, cols, -1)
            whole = lax.dynamic_update_slice(whole, piece, (0, rows_at[q], 0, 0, 0))
        return whole.reshape(slots, high, cols, -1)

    def take_bands(value):
        value = value.reshape(slots, ranks, band * cols, -1)
        return [
            lax.dynamic_index_in_dim(value, rows_at[q], 1, keepdims=False).reshape(patches, -1)
            for q in range(ranks)
        ]

    wide_one = columns(stack_bands(bands))
    slabs = [wide_one[:, u : u + high].reshape(slots * high * cols, 3 * group) for u in range(3)]
    act_two = dot(slabs[0], conv_taps[0]) + dot(slabs[1], conv_taps[1]) + dot(slabs[2], conv_taps[2])
    hat_two, scale_two = normalize(scatter_row(take_bands(act_two)))
    pre_two = hat_two * norm_vals[2] + norm_vals[3]
    low_two = jax.nn.silu(pre_two).astype(BF16)
    hat_three, scale_three = normalize(dot(low_two, last_full))
    summed = flat_in.astype(F32) + (hat_three * norm_vals[4] + norm_vals[5])
    pooled = jnp.mean(summed.reshape(slots, band // 2, 2, cols // 2, 2, width), axis=(2, 4)).astype(BF16)
    pooled = pooled.reshape(-1, width)
    pools = jnp.concatenate(gather_row(pooled), axis=0)
    logits = dot_t(pools, read_mine) + bias_mine
    mask = (jnp.arange(slots, dtype=jnp.int32) < live_count[0]).astype(F32)
    mask = jnp.broadcast_to(mask[None, :, None], (ranks, slots, pooled.shape[0] // slots)).reshape(-1, 1)
    shown = (jax.nn.gelu(logits, approximate=False) * mask).astype(BF16)
    shown = exchange_row(jnp.split(shown, ranks, axis=0))
    readout = jnp.zeros((pooled.shape[0], n, ranks, outs), BF16)
    for q in range(ranks):
        readout = lax.dynamic_update_slice(
            readout, shown[q].reshape(-1, n, 1, outs), (0, 0, rows_at[q], 0)
        )
    readout_out = readout.reshape(slots, band // 2, cols // 2, n * ranks * outs)

    grad_low = (cot.astype(F32) * mask * gelu_slope(logits)).astype(BF16)
    read_terms = t_dot(grad_low, pools).reshape(n, outs, width)
    bias_terms = jnp.sum(grad_low.astype(F32), axis=0).reshape(n, 1, outs)
    bias_terms = jnp.pad(bias_terms, ((0, 0), (0, 7), (0, width - outs)))
    read_sum = scatter_dp(jnp.concatenate([read_terms, bias_terms], axis=1), n)
    read_grad, bias_grad = read_sum[:outs].T, read_sum[outs, :outs]
    grad_pool = scatter_row(jnp.split(dot(grad_low, read_mine), ranks, axis=0))
    grad_sum = (
        jnp.broadcast_to(
            grad_pool.reshape(slots, band // 2, 1, cols // 2, 1, width),
            (slots, band // 2, 2, cols // 2, 2, width),
        )
        * 0.25
    ).reshape(-1, width)
    gain_three = jnp.sum(grad_sum * hat_three, axis=0)
    shift_three = jnp.sum(grad_sum, axis=0)
    grad_three = norm_backward(grad_sum, hat_three, scale_three, norm_vals[4]).astype(BF16)
    grad_pre_two = dot_t(grad_three, last_full) * silu_slope(pre_two)
    gain_two = jnp.sum(grad_pre_two * hat_two, axis=0)
    shift_two = jnp.sum(grad_pre_two, axis=0)
    grad_two = norm_backward(grad_pre_two, hat_two, scale_two, norm_vals[2]).astype(BF16)
    grad_full = stack_bands(gather_row(grad_two))
    grad_flat = grad_full.reshape(-1, width)

    def row_sums(terms):
        terms = terms.reshape(n, ranks, -1, width)
        return scatter_row(
            [lax.dynamic_index_in_dim(terms, rows_at[q], 1, keepdims=False) for q in range(ranks)]
        )

    conv_grad = []
    for u in range(3):
        terms = t_dot(slabs[u], grad_flat).reshape(3, n, own, width).transpose(1, 0, 2, 3)
        conv_grad.append(scatter_dp(terms.reshape(n, 3 * own, width), n).reshape(3, own, width))
    conv_grad = jnp.stack(conv_grad)
    wide_grad = jnp.pad(grad_full, ((0, 0), (1, 1), (1, 1), (0, 0)))
    grad_mid = jnp.zeros((slots * high * cols, group), F32)
    for u in range(3):
        for v in range(3):
            slab = wide_grad[:, 2 - u : 2 - u + high, 2 - v : 2 - v + cols].reshape(-1, width)
            grad_mid = grad_mid + dot_t(slab, conv_taps[u][v * group : (v + 1) * group])
    pieces = exchange_row(take_bands(grad_mid.astype(BF16)))
    grad_low_one = jnp.concatenate(
        [pick([pieces[i ^ q] for i in range(ranks)], row) for q in range(ranks)], axis=1
    ).astype(F32)
    last_sum = scatter_dp(row_sums(t_dot(low_two, grad_three)), n)

    grad_pre_one = grad_low_one * silu_slope(pre_one)
    gain_one = jnp.sum(grad_pre_one * hat_one, axis=0)
    shift_one = jnp.sum(grad_pre_one, axis=0)
    grad_one = norm_backward(grad_pre_one, hat_one, scale_one, norm_swap[0]).astype(BF16)
    image_grad = (grad_sum + dot_t(grad_one, first_full)).astype(BF16)
    image_grad = image_grad.reshape(slots, band, cols, width)

    swapped = jnp.stack([gain_one, shift_one]).reshape(2, ranks, n, own).transpose(2, 1, 0, 3)
    plain = jnp.stack([gain_two, shift_two, gain_three, shift_three])
    plain = plain.reshape(4, n, ranks, own).transpose(1, 2, 0, 3)
    norm_terms = jnp.concatenate([swapped, plain], axis=2).reshape(n, ranks, 1, 6 * own)
    norm_terms = jnp.pad(norm_terms, ((0, 0), (0, 0), (0, 7), (0, width - 6 * own)))
    first_terms = t_dot(flat_in, grad_one).reshape(n, ranks, own, width)
    first_sum = scatter_dp(row_sums(jnp.concatenate([first_terms, norm_terms], axis=2)), n)
    norm_grad = first_sum[own, : 6 * own].reshape(6, own)
    first_grad = first_sum[:own].reshape(own, ranks, n, own).transpose(0, 2, 1, 3).reshape(own, width)
    return (
        readout_out,
        image_grad,
        first_grad,
        conv_grad,
        last_sum,
        norm_grad,
        read_grad,
        bias_grad,
    )


VM = pl.BlockSpec(memory_space=pltpu.VMEM)
SM = pl.BlockSpec(memory_space=pltpu.SMEM)
HB = pl.BlockSpec(memory_space=pltpu.HBM)


def shape(dims, dtype):
    return jax.ShapeDtypeStruct(dims, dtype)


def kernel(body, outs, ins, scratch, flops, moved, *arrays, specs=None, room=16):
    return pl.pallas_call(
        body,
        out_shape=outs,
        in_specs=ins,
        out_specs=jax.tree.map(lambda _: VM, outs) if specs is None else specs,
        scratch_shapes=scratch,
        cost_estimate=pl.CostEstimate(flops=flops // 64, bytes_accessed=moved // 64, transcendentals=0),
        compiler_params=pltpu.CompilerParams(vmem_limit_bytes=room << 20),
    )(*arrays)


def at_row(where, q):
    return where[0] ^ q


def start_all(copies):
    for copy in copies:
        copy.start()


def wait_all(copies):
    for copy in copies:
        copy.wait()


def copies_of(pairs, sems):
    return [pltpu.make_async_copy(a, b, sems.at[i]) for i, (a, b) in enumerate(pairs)]


def hop(x, turn, places=1):
    order = ring_order(RING)
    step = places if turn else -places
    return lax.ppermute(x, "dp", [(order[i], order[(i + step) % RING]) for i in range(RING)])


def gather_step(state, step, low=None, high=None):
    pieces, a, b = state
    pieces = list(pieces)
    if step < RING // 2:
        a, b = hop(a, True), hop(b, False)
        pieces[RING - step], pieces[step] = a, b
    else:
        pieces[step] = (hop(low(a), True), hop(high(b), False))
    return pieces, a, b


def gather_state(x):
    return [x] * RING, x, x


def scatter_step(low, high, terms, a, b, step):
    half = RING // 2
    if step == half:
        return hop(low, True), hop(high, False)
    right, left = terms[step].astype(F32), terms[RING - step].astype(F32)
    if step == half - 1:
        cut = low.shape[0]
        right = jnp.concatenate([right[:cut] + a.astype(F32), right[cut:]], axis=0)
        left = jnp.concatenate([left[:cut], left[cut:] + b.astype(F32)], axis=0)
    else:
        right, left = right + a.astype(F32), left + b.astype(F32)
    return hop(right.astype(BF16), True), hop(left.astype(BF16), False)


def scatter_end(terms, a, b):
    return terms[0].astype(F32) + a.astype(F32) + b.astype(F32)


def fence(*values):
    return lax.optimization_barrier(values)


def line_up(where, *refs):
    pieces, (first, last) = refs[: RING + 1], refs[RING + 1 :]
    rows = last.shape[1]
    for k in range(RING):
        if k == RING // 2:
            last[where[2 + k]] = pieces[k][...]
            first[where[2 + k]] = pieces[RING][...]
        else:
            last[where[2 + k]] = pieces[k][:rows]
            first[where[2 + k]] = pieces[k][rows:]


def fill(where, weight, parts):
    rows = weight.shape[2]
    for q, part in enumerate(parts):
        weight[:, at_row(where, q)] = part[:, :rows, :]


def center(value):
    mean = jnp.mean(value, axis=-1, keepdims=True)
    gap = value - mean
    scale = lax.rsqrt(jnp.mean(gap * gap, axis=-1, keepdims=True) + eps)
    return gap * scale, scale


def flat_pieces(pieces):
    half = RING // 2
    return [p[0] if k == half else p for k, p in enumerate(pieces)] + [pieces[half][1]]


def stage_one(where, x, f0, f1, f2, f3, hat, scale, s0, s1, s2, s3, norms, weight, low):
    firsts = (f0, f1, f2, f3)
    fill(where, weight, firsts)
    width, rows = x.shape[1], weight.shape[2]
    total = jnp.zeros((8, width), F32)
    bias = total
    for q, first in enumerate(firsts):
        for k in range(RING):
            block = first[k, rows:, :].astype(F32)
            total = total + block
            if q == 0:
                bias = bias + block
    line = lax.broadcasted_iota(jnp.int32, (8, width), 0)
    table = jnp.where(line == 6, bias, total)
    norms[...] = table
    act = dot(x[...], weight[...].reshape(width, width))
    normed, root = center(act)
    hat[...] = normed
    scale[...] = root
    pre = normed * norms[0:1, :] + norms[1:2, :]
    low[...] = (pre * jax.nn.sigmoid(pre)).astype(BF16)
    part = width // 4
    for q, out in enumerate((s0, s1, s2, s3)):
        out[...] = low[:, pl.ds(pl.multiple_of(at_row(where, q) * part, part), part)]


def conv_copies(where, pieces, weight, sems):
    far = RING // 2
    pairs = []
    for k in range(RING):
        if k == far:
            number = pieces[far].shape[0]
            pairs.append((pieces[far], weight.at[pl.ds(0, number), where[2 + k]]))
            pairs.append((pieces[RING], weight.at[pl.ds(number, pieces[RING].shape[0]), where[2 + k]]))
        else:
            pairs.append((pieces[k], weight.at[:, where[2 + k]]))
    return copies_of(pairs, sems)


def conv_forward(dims, first, where, s0, s1, s2, s3, *refs):
    slots, rows, cols = dims
    if first:
        own, near, spans, weight, pad, moved, wide, sems, done = refs[RING + 1 :]
        copies = conv_copies(where, refs[: RING + 1], weight, sems)
        start_all(copies)
    else:
        weight, own, near, spans, pad, moved, wide, done = refs
    group = s0.shape[1]
    patches = rows * cols
    band = patches // 4
    pad[...] = jnp.zeros_like(pad)
    for q, piece in enumerate((s0, s1, s2, s3)):
        for i in range(slots):
            at = pl.multiple_of(cols + 8 + at_row(where, q) * band, 8)
            pad[i, pl.ds(at, band), :] = piece[i * band : (i + 1) * band, :].astype(F32)
    for v in range(3):
        for i in range(slots):
            shifted = pad[i, 8 + v - 1 : 8 + v - 1 + patches + 2 * cols, :]
            if v != 1:
                col = lax.broadcasted_iota(jnp.int32, shifted.shape, 0) % cols
                shifted = jnp.where(col == (0 if v == 0 else cols - 1), 0.0, shifted)
            moved[i] = shifted

        @pl.loop(0, 2 * slots)
        def _(j):
            q, i = j // slots, j % slots
            here = pl.ds(pl.multiple_of(j * band, 16), band)
            for u in range(3):
                at = pl.multiple_of(at_row(where, first + q) * band + u * cols, 8)
                t = u * 3 + v
                wide[here, t * group : (t + 1) * group] = moved[i, pl.ds(at, band), :].astype(BF16)

    keep = pltpu.make_async_copy(wide, spans, done)
    keep.start()
    if first:
        wait_all(copies)
    width = own.shape[1]
    chunk = 256
    patches = slots * band

    @pl.loop(0, width // chunk)
    def _(j):
        lanes = pl.ds(pl.multiple_of(j * chunk, chunk), chunk)
        terms = dot(wide[...], weight[:, :, :, lanes].reshape(-1, chunk))
        own[:, lanes] = terms[:patches]
        near[:, lanes] = terms[patches:].astype(BF16)

    keep.wait()


def stage_two(dims, where, own, near, cross, x, norms, l0, l1, l2, l3, hat_two, scale_two, low, hat, scale, pooled, weight, pairs):
    slots, rows, cols = dims
    fill(where, weight, (l0, l1, l2, l3))
    width = x.shape[1]
    act = own[...] + near[...].astype(F32) + cross[...].astype(F32)
    normed, root = center(act)
    hat_two[...] = normed
    scale_two[...] = root
    pre = normed * norms[2:3, :] + norms[3:4, :]
    low[...] = (pre * jax.nn.sigmoid(pre)).astype(BF16)
    normed, root = center(dot(low[...], weight[...].reshape(width, width)))
    hat[...] = normed
    scale[...] = root
    y = x[...].astype(F32) + (normed * norms[4:5, :] + norms[5:6, :])
    y = jnp.sum(y.reshape(slots * rows // 2, 2, cols, width), axis=1).reshape(-1, width)
    count = pooled.shape[0]
    for g in range(pairs.shape[0]):
        lanes = slice(g * 128, (g + 1) * 128)
        pairs[g] = y[:, lanes]
        pooled[:, lanes] = (
            0.25 * (pairs[g, pl.ds(0, count, stride=2), :] + pairs[g, pl.ds(1, count, stride=2), :])
        ).astype(BF16)


def read_copies(where, pieces, weight, sems):
    half = RING // 2
    pairs = []
    for k in range(RING):
        if k == half:
            rows = pieces[half].shape[0]
            pairs.append((pieces[half], weight.at[where[2 + k], pl.ds(0, rows)]))
            pairs.append((pieces[RING], weight.at[where[2 + k], pl.ds(rows, rows)]))
        else:
            pairs.append((pieces[k], weight.at[where[2 + k]]))
    return copies_of(pairs, sems)


def readout(slots, where, p0, p1, p2, p3, c0, c1, c2, c3, norms, *refs):
    pieces = refs[: RING + 1]
    o0, o1, o2, o3, low, own, near, far, weight, sems = refs[RING + 1 :]
    copies = read_copies(where, pieces, weight, sems)
    start_all(copies)
    count, width = p0.shape
    table = jnp.concatenate([p[...] for p in (p0, p1, p2, p3)], axis=0)
    line = lax.broadcasted_iota(jnp.int32, (count, width), 0)
    mask = jnp.where(line // (count // slots) < where[1], 1.0, 0.0)
    wait_all(copies)
    whole = weight[...].reshape(-1, width)
    logits = dot_t(table, whole) + norms[6:7, :]
    for q, (cot, out) in enumerate(((c0, o0), (c1, o1), (c2, o2), (c3, o3))):
        z = logits[q * count : (q + 1) * count]
        phi = 0.5 * (1.0 + lax.erf(z * 0.7071067811865476))
        out[...] = (z * phi * mask).astype(BF16)
        slope = phi + z * jnp.exp(-0.5 * z * z) * 0.3989422804014327
        low[q * count : (q + 1) * count, :] = (cot[...].astype(F32) * mask * slope).astype(BF16)
    back = dot(low[...], whole)
    own[...] = back[:count]
    near[0] = back[count : 2 * count].astype(BF16)
    far[...] = back[2 * count : 3 * count]
    near[1] = back[3 * count :].astype(BF16)


def readout_terms(where, low, p0, p1, p2, p3, upper, lower, out, terms):
    width = p0.shape[1]
    table = jnp.concatenate([p[...] for p in (p0, p1, p2, p3)], axis=0)
    terms[...] = t_dot(low[...], table).reshape(terms.shape)
    bias = jnp.sum(low[...].astype(F32), axis=0, keepdims=True)
    rows = terms.shape[1]
    for k in range(RING):
        out[k, :rows, :] = terms[where[2 + k]].astype(BF16)
        out[k, rows:, :] = jnp.broadcast_to(bias, (out.shape[1] - rows, width)).astype(BF16)
    upper[...] = out[RING // 2, : upper.shape[0]]
    lower[...] = out[RING // 2, upper.shape[0] :]


def read_end(term, a, b, out, bias):
    total = term[...].astype(F32) + a[...].astype(F32) + b[...].astype(F32)
    rows = out.shape[1]
    out[...] = total[:rows].T
    bias[...] = total[rows : rows + 8]


def spread(pairs, grad, dims):
    slots, rows, cols = dims
    count, width = grad.shape
    for g in range(pairs.shape[0]):
        lanes = slice(g * 128, (g + 1) * 128)
        pairs[g, pl.ds(0, count, stride=2), :] = grad[:, lanes]
        pairs[g, pl.ds(1, count, stride=2), :] = grad[:, lanes]
    half = slots * rows // 2
    both = jnp.concatenate([pairs[g] for g in range(pairs.shape[0])], axis=1)
    both = jnp.broadcast_to(both.reshape(half, 1, cols, width), (half, 2, cols, width))
    return both.reshape(-1, width) * 0.25


def back_norm(grad, normed, root, gain):
    weighted = grad * gain
    return root * (
        weighted
        - jnp.mean(weighted, axis=-1, keepdims=True)
        - normed * jnp.mean(weighted * normed, axis=-1, keepdims=True)
    )


def total_rows(value):
    return jnp.sum(value, axis=0, keepdims=True)


def stage_two_back(dims, where, own, near, cross, hat, scale, hat_two, scale_two, norms, weight, grad_three, grad_two, pool_sum, sums, pairs):
    width = hat.shape[1]
    grad = own[...] + near[...].astype(F32) + cross[...].astype(F32)
    pool_sum[...] = grad
    gy = spread(pairs, grad, dims)
    sums[...] = jnp.zeros_like(sums)
    sums[4:5, :] = total_rows(gy * hat[...])
    sums[5:6, :] = total_rows(gy)
    grad_three[...] = back_norm(gy, hat[...], scale[...], norms[4:5, :]).astype(BF16)
    gs = dot_t(grad_three[...], weight[...].reshape(width, width))
    pre = hat_two[...] * norms[2:3, :] + norms[3:4, :]
    gn = gs * silu_slope(pre)
    sums[2:3, :] = total_rows(gn * hat_two[...])
    sums[3:4, :] = total_rows(gn)
    grad_two[...] = back_norm(gn, hat_two[...], scale_two[...], norms[2:3, :]).astype(BF16)


def last_terms(where, low, grad, own, near, far, terms):
    terms[...] = t_dot(low[...], grad[...]).reshape(terms.shape)
    for k in range(RING):
        own[k] = terms[where[2 + k], at_row(where, 0)]
        near[0, k] = terms[where[2 + k], at_row(where, 1)].astype(BF16)
        far[k] = terms[where[2 + k], at_row(where, 2)]
        near[1, k] = terms[where[2 + k], at_row(where, 3)].astype(BF16)


def stack_grad(dims, where, pieces, whole):
    slots, rows, cols = dims
    band = rows * cols // 4
    for q, piece in enumerate(pieces):
        for i in range(slots):
            at = pl.multiple_of(i * rows * cols + at_row(where, q) * band, 16)
            whole[pl.ds(at, band), :] = piece[i * band : (i + 1) * band, :]


def conv_half_terms(where, here, g0, g1, out, one):
    count = g0.shape[0]
    one[:count], one[count:] = g0[...], g1[...]
    group = out.shape[1]

    @pl.loop(0, out.shape[0])
    def _(t):
        lanes = pl.ds(pl.multiple_of(t * group, group), group)
        out[t] = t_dot(here[:, lanes], one[...])


def conv_terms(first, number, where, half, there, g2, g3, *refs):
    parts, outs, (two, line) = refs[: -RING - 2], refs[-RING - 2 : -2], refs[-2:]
    count = g2.shape[0]
    two[:count], two[count:] = g2[...], g3[...]
    rows, width = outs[0].shape[1:]
    group = RING * rows

    @pl.loop(0, number)
    def _(t):
        lanes = pl.ds(pl.multiple_of((first + t) * group, group), group)
        terms = half[first + t] + t_dot(there[:, lanes], two[...])
        line[...] = terms.astype(BF16).reshape(RING, rows, width)
        for k in range(RING):
            outs[k][t] = line[where[2 + k]]

    if parts:
        own, near, low, high = parts
        for k in range(RING):
            cross = low[k] if k < RING // 2 else high[k - RING // 2]
            outs[k][number] = (own[k] + near[0, k].astype(F32) + cross.astype(F32)).astype(BF16)


def conv_back(dims, where, g0, g1, g2, g3, weight, o0, o1, o2, o3, whole, held, low):
    slots, rows, cols = dims
    stack_grad(dims, where, (g0, g1, g2, g3), whole)
    patches = rows * cols
    band = patches // 4
    group = o0.shape[1]
    width = whole.shape[1]
    held[...] = jnp.zeros_like(held)
    @pl.loop(0, 3)
    def _(u):
        at = pl.ds(pl.multiple_of(8 + u * cols, 8), patches)
        for v in range(3):
            part = dot_t(whole[...], weight[u * 3 + v].reshape(group, width))
            for i in range(slots):
                held[v, i, at, :] += part[i * patches : (i + 1) * patches]

    col = lax.broadcasted_iota(jnp.int32, (patches, group), 0) % cols
    for i in range(slots):
        value = held[1, i, 8 + cols : 8 + cols + patches, :]
        value += jnp.where(col == cols - 1, 0.0, held[0, i, 9 + cols : 9 + cols + patches, :])
        value += jnp.where(col == 0, 0.0, held[2, i, 7 + cols : 7 + cols + patches, :])
        low[i * patches : (i + 1) * patches, :] = value.astype(BF16)
    for q, out in enumerate((o0, o1, o2, o3)):
        for i in range(slots):
            at = pl.multiple_of(i * patches + at_row(where, q) * band, 16)
            out[i * band : (i + 1) * band, :] = low[pl.ds(at, band), :]


def stage_one_back(where, b0, b1, b2, b3, hat, scale, norms, x, sums, grad_one, own, near, far, low, terms):
    width = hat.shape[1]
    part = width // 4
    for q, piece in enumerate((b0, b1, b2, b3)):
        low[:, pl.ds(pl.multiple_of(at_row(where, q) * part, part), part)] = piece[...]
    pre = hat[...] * norms[0:1, :] + norms[1:2, :]
    gn = low[...].astype(F32) * silu_slope(pre)
    line = lax.broadcasted_iota(jnp.int32, (8, width), 0)
    tail = jnp.where(line == 0, total_rows(gn * hat[...]), jnp.where(line == 1, total_rows(gn), sums[...]))
    grad_one[...] = back_norm(gn, hat[...], scale[...], norms[0:1, :]).astype(BF16)
    terms[...] = t_dot(x[...], grad_one[...]).reshape(terms.shape)
    rows = terms.shape[2]
    for k in range(RING):
        to = where[2 + (k + 3) % RING]
        own[k, :rows] = terms[to, at_row(where, 0)]
        near[0, k, :rows] = terms[to, at_row(where, 1)].astype(BF16)
        far[k, :rows] = terms[to, at_row(where, 2)]
        near[1, k, :rows] = terms[to, at_row(where, 3)].astype(BF16)
        own[k, rows:] = tail
        near[0, k, rows:] = tail.astype(BF16)
        far[k, rows:] = tail
        near[1, k, rows:] = tail.astype(BF16)


def image_back(dims, where, grad_one, pool_sum, weight, out, pairs):
    width = grad_one.shape[1]
    gy = spread(pairs, pool_sum[...], dims)
    out[...] = (gy + dot_t(grad_one[...], weight[...].reshape(width, width))).astype(BF16)


def split_columns(where, x, o0, o1, o2, o3):
    lanes = x.shape[1] // (4 * RING)
    for q, out in enumerate((o0, o1, o2, o3)):
        for g in range(RING):
            at = pl.multiple_of((g * 4 + at_row(where, q)) * lanes, lanes)
            out[:, g * lanes : (g + 1) * lanes] = x[:, pl.ds(at, lanes)]


def join_columns(where, i0, i1, i2, i3, out):
    lanes = out.shape[1] // (4 * RING)
    for q, piece in enumerate((i0, i1, i2, i3)):
        for g in range(RING):
            at = pl.multiple_of((g * 4 + at_row(where, q)) * lanes, lanes)
            out[:, pl.ds(at, lanes)] = piece[:, g * lanes : (g + 1) * lanes]


def ringed(
    images,
    first_weight,
    conv_weight,
    last_weight,
    norm_rows,
    read_weight,
    read_bias,
    cotangent,
    live_count,
):
    dp, row = lax.axis_index("dp"), lax.axis_index("row")
    slots, band, cols, width = images.shape
    dims = (slots, band, cols)
    full = (slots, 4 * band, cols)
    patches = slots * band * cols
    count = patches // 4
    own = first_weight.shape[0]
    group = RING * own
    outs = read_weight.shape[1]
    taps = 9
    DMA = pltpu.SemaphoreType.DMA
    index = jnp.arange(18, dtype=jnp.int32)
    place_of = lambda d: jnp.where(d % 2 == 0, d // 2, RING - 1 - d // 2)
    place = (place_of(dp) + index - 2) % RING
    ahead = jnp.where(place < RING // 2, 2 * place, 2 * (RING - 1 - place) + 1)
    steps = (place_of(index - 10) - place_of(dp)) % RING
    where = jnp.where(index == 0, row, jnp.where(index == 1, live_count[0], jnp.where(index < 10, ahead, steps)))
    where = where.astype(jnp.int32)

    first_mine = first_weight.reshape(own, RING, 4, own).transpose(0, 2, 1, 3).reshape(own, width)
    lane = jnp.arange(width, dtype=jnp.int32)[None, :]
    tiled = jnp.tile(norm_rows, (1, width // own))
    at = jnp.where(jnp.arange(6)[:, None] < 2, row * RING + dp, dp * 4 + row)
    small = jnp.where(lane // own == at, tiled, 0).astype(BF16)
    bias = jnp.where(lane // outs == dp, jnp.tile(read_bias, width // outs)[None, :], 0).astype(BF16)
    small = jnp.concatenate([small, bias, jnp.zeros((1, width), BF16)], axis=0)
    first_mine = jnp.concatenate([first_mine, small], axis=0)
    conv = conv_weight.reshape(taps, own, width)
    quarter = shape((count, width), BF16)
    wide_f32, thin_f32, wide_bf16 = (
        shape((patches, width), F32),
        shape((patches, 1), F32),
        shape((patches, width), BF16),
    )
    quarter_f32, near_quarter = shape((count, width), F32), shape((2, count, width), BF16)
    piece = shape((patches, group), BF16)
    block = (RING, own, width)
    matmul = 2 * patches * width * width
    square = 2 * width * width
    square_of = shape((RING, 4, own, width), BF16)
    total = 4 * patches
    pad_rows = full[1] * cols + 2 * cols + 16
    pair_scratch = pltpu.VMEM((width // 128, patches // 2, 128), F32)
    x = images.reshape(patches, width)

    far = RING // 2
    cut = own + 8
    low, high = lambda v: v[:own], lambda v: v[own:]
    more = gather_step(gather_state(conv), 1)
    ring = gather_step(gather_state(jnp.concatenate([last_weight, first_mine], axis=0)), 1)
    read = read_weight.T
    cots = cotangent.reshape(count, -1)
    places = ((row * RING + dp) * own, (dp * 4 + row) * own, dp * outs)
    more, ring, where, read, cots, x, places = fence(more, ring, where, read, cots, x, places)
    ring = gather_step(ring, 2)
    cots = kernel(split_columns, [quarter] * 4, [SM, VM], [], 0, 2 * count * 4 * width * 2, where, cots)
    ring, cots = fence(ring, cots)
    ring = gather_step(ring, 3)
    ring = fence(ring)[0]
    ring = gather_step(ring, 4, low, high)
    more, ring = fence(more, ring)
    ring = ring[0]
    firsts, lasts = kernel(
        line_up,
        [shape((RING, cut, width), BF16), shape((RING, own, width), BF16)],
        [SM] + [VM] * (RING + 1),
        [],
        0,
        4 * RING * (cut + own) * width,
        where,
        *flat_pieces(ring),
    )
    more = gather_step(more, 2)
    first_two, first_one = swap_row(firsts, 2), swap_row(firsts, 1)
    more, firsts, first_two, first_one, lasts = fence(more, firsts, first_two, first_one, lasts)
    more = gather_step(more, 3)
    firsts = [firsts, first_one, first_two, swap_row(first_two, 1)]
    last_two, last_one = swap_row(lasts, 2), swap_row(lasts, 1)
    hat_one, scale_one, *lows, norms, first_full = kernel(
        stage_one,
        [wide_f32, thin_f32] + [piece] * 4 + [shape((8, width), F32), square_of],
        [SM] + [VM] * 5,
        [pltpu.VMEM((patches, width), BF16)],
        matmul,
        square + 8 * patches * width,
        where,
        x,
        *firsts,
    )
    more, lows, lasts, last_two, last_one = fence(more, lows, lasts, last_two, last_one)
    taps_half = (taps + 1) // 2
    more = gather_step(more, 4, lambda v: v[:taps_half], lambda v: v[taps_half:])
    lows = exchange_row(lows)
    lasts = [lasts, last_one, last_two, swap_row(last_two, 1)]
    weights = flat_pieces(more[0])
    weights, lows, lasts, read, cots = fence(weights, lows, lasts, read, cots)

    conv_whole = (taps, RING, own, width)

    def conv_half(first, weights):
        return kernel(
            functools.partial(conv_forward, full, first),
            [wide_f32, wide_bf16, shape((2 * patches, taps * group), BF16)]
            + ([shape(conv_whole, BF16)] if first else []),
            [SM] + [VM] * 4 + ([HB] * (RING + 1) if first else [VM]),
            [
                pltpu.VMEM((slots, pad_rows, group), F32),
                pltpu.VMEM((slots, pad_rows - 16, group), F32),
                pltpu.VMEM((2 * patches, taps * group), BF16),
            ]
            + ([DMA((RING + 1,))] if first else [])
            + [DMA],
            9 * matmul // 2,
            9 * square + 6 * patches * width + 4 * patches * taps * group,
            where,
            *lows,
            *weights,
            specs=[VM, VM, HB] + ([VM] if first else []),
        )

    read = gather_step(gather_state(read), 1)
    cots = exchange_row(cots)
    away, near, spans_far, conv_full = conv_half(2, weights)
    away, near, read, cots = fence(away, near, read, cots)
    other = (away + swap_row(near, 1).astype(F32)).astype(BF16)
    other, lows, read = fence(other, lows, read)
    cross = swap_row(other, 2)
    read = gather_step(read, 2)
    mine, near, spans_near = conv_half(0, (conv_full,))
    near, read = fence(near, read)
    near = swap_row(near, 1)
    read = gather_step(read, 3)
    mine, near, cross, read = fence(mine, near, cross, read)
    read = gather_step(read, 4, lambda v: v[: outs // 2], lambda v: v[outs // 2 :])
    hat_two, scale_two, low_two, hat_three, scale_three, pooled, last_full = kernel(
        functools.partial(stage_two, dims),
        [wide_f32, thin_f32, wide_bf16, wide_f32, thin_f32, quarter, square_of],
        [SM] + [VM] * 9,
        [pair_scratch],
        matmul,
        square + 24 * patches * width,
        where,
        mine,
        near,
        cross,
        x,
        norms,
        *lasts,
    )
    pool_two, pool_one = swap_row(pooled, 2), swap_row(pooled, 1)
    pooled, pool_two, pool_one, read = fence(pooled, pool_two, pool_one, read)
    pools = [pooled, pool_one, pool_two, swap_row(pool_two, 1)]
    *shown, grad_low, mine, near, away = kernel(
        functools.partial(readout, slots),
        [quarter] * 4 + [wide_bf16, quarter_f32, near_quarter, quarter_f32],
        [SM] + [VM] * 9 + [HB] * (RING + 1),
        [pltpu.VMEM((RING, outs, width), BF16), DMA((RING + 1,))],
        2 * matmul,
        square + 12 * patches * width,
        where,
        *pools,
        *cots,
        norms,
        *flat_pieces(read[0]),
    )

    near = swap_row(near, 1)
    other = (away + near[1].astype(F32)).astype(BF16)
    other, grad_low, near = fence(other, grad_low, near)
    cross = swap_row(other, 2)
    half_read = shape(((outs + 16) // 2, width), BF16)
    *read_far, read_terms = kernel(
        readout_terms,
        [half_read, half_read, shape((RING, outs + 16, width), BF16)],
        [SM] + [VM] * 5,
        [pltpu.VMEM((RING, outs, width), F32)],
        matmul,
        2 * square,
        where,
        grad_low,
        *pools,
    )
    cross, read_far, read_terms, near = fence(cross, read_far, read_terms, near)
    read_a, read_b = scatter_step(*read_far, read_terms, None, None, 4)
    grad_three, grad_two, pool_sum, sums = kernel(
        functools.partial(stage_two_back, dims),
        [wide_bf16, wide_bf16, quarter_f32, shape((8, width), F32)],
        [SM] + [VM] * 9,
        [pair_scratch],
        matmul,
        square + 14 * patches * width,
        where,
        mine,
        near[0],
        cross,
        hat_three,
        scale_three,
        hat_two,
        scale_two,
        norms,
        last_full,
    )
    grad_three, grad_two, read_a, read_b = fence(grad_three, grad_two, read_a, read_b)
    grad_far, grad_next = swap_row(grad_two, 2), swap_row(grad_two, 1)
    read_a, read_b = scatter_step(*read_far, read_terms, read_a, read_b, 3)
    read_a, read_b = scatter_step(*read_far, read_terms, read_a, read_b, 2)
    here = kernel(
        conv_half_terms,
        shape((taps, group, width), F32),
        [SM] + [VM] * 3,
        [pltpu.VMEM((2 * patches, width), BF16)],
        9 * matmul // 2,
        18 * square,
        where,
        spans_near,
        grad_two,
        grad_next,
    )
    last_own, last_near, last_far = kernel(
        last_terms,
        [shape(block, F32), shape((2,) + block, BF16), shape(block, F32)],
        [SM, VM, VM],
        [pltpu.VMEM((RING, 4, own, width), F32)],
        matmul,
        3 * square,
        where,
        low_two,
        grad_three,
    )
    grad_two, grad_far, grad_next, last_near, last_far, read_a, read_b, here = fence(
        grad_two, grad_far, grad_next, last_near, last_far, read_a, read_b, here
    )
    grads = [grad_two, grad_next, grad_far, swap_row(grad_far, 1)]
    last_near = swap_row(last_near, 1)
    last_low = (last_far[:far] + last_near[1, :far].astype(F32)).astype(BF16)
    last_high = (last_far[far:] + last_near[1, far:].astype(F32)).astype(BF16)
    grads, last_near, last_low, last_high = fence(grads, last_near, last_low, last_high)
    last_low = swap_row(last_low, 2)
    read_a, read_b = scatter_step(*read_far, read_terms, read_a, read_b, 1)

    def weight_terms(first, number, parts):
        held = number + len(parts) // 4
        return kernel(
            functools.partial(conv_terms, first, number),
            [shape((held, own, width), BF16)] * RING,
            [SM] + [VM] * (4 + len(parts)),
            [pltpu.VMEM((2 * patches, width), BF16), pltpu.VMEM((RING, own, width), BF16)],
            matmul * number,
            2 * square * number,
            where,
            here,
            spans_far,
            *grads[2:],
            *parts,
        )

    def add_to(terms, k, value):
        return (terms[k % RING].astype(F32) + value.astype(F32)).astype(BF16)

    one = weight_terms(0, 5, ())
    one, grads, last_low, last_high, read_a, read_b = fence(
        one, grads, last_low, last_high, read_a, read_b
    )
    last_high = swap_row(last_high, 2)
    one_a, one_b = hop(one[far], True), hop(one[far + 1], False)
    backs = kernel(
        functools.partial(conv_back, full),
        [piece] * 4,
        [SM] + [VM] * 5,
        [
            pltpu.VMEM((total, width), BF16),
            pltpu.VMEM((3, slots, pad_rows, group), F32),
            pltpu.VMEM((total, group), BF16),
        ],
        9 * matmul,
        9 * square + 12 * patches * width,
        where,
        *grads,
        conv_full,
    )
    one_a, one_b, backs, grads, last_high = fence(one_a, one_b, backs, grads, last_high)
    one_a, one_b = hop(add_to(one, 3, one_a), True), hop(add_to(one, -2, one_b), False)
    backs = exchange_row(backs)
    two = weight_terms(5, 4, (last_own, last_near, last_low, last_high))
    one_a, one_b, two, backs = fence(one_a, one_b, two, backs)
    two_a, two_b = hop(two[far - 1], True), hop(two[far], False)
    one_a, one_b = add_to(one, 2, one_a), add_to(one, -1, one_b)
    block = (RING, own + 8, width)
    grad_one, first_own, first_near, first_far = kernel(
        stage_one_back,
        [wide_bf16, shape(block, F32), shape((2,) + block, BF16), shape(block, F32)],
        [SM] + [VM] * 9,
        [pltpu.VMEM((patches, width), BF16), pltpu.VMEM((RING, 4, own, width), F32)],
        matmul,
        3 * square + 8 * patches * width,
        where,
        *backs,
        hat_one,
        scale_one,
        norms,
        x,
        sums,
    )
    one_a, one_b, two_a, two_b, grad_one, first_own, first_near, first_far, shown = fence(
        one_a, one_b, two_a, two_b, grad_one, first_own, first_near, first_far, shown
    )
    one_a, one_b = hop(one_a, True), hop(one_b, False)
    two_a, two_b = add_to(two, 2, two_a), add_to(two, -3, two_b)
    first_near = swap_row(first_near, 1)
    shown = exchange_row(shown)
    first_low = (first_far[far:] + first_near[1, far:].astype(F32)).astype(BF16)
    first_high = (first_far[:far] + first_near[1, :far].astype(F32)).astype(BF16)
    one_a, one_b_end, two_a, two_b, first_near, first_low, first_high, shown = fence(
        one_a, one_b, two_a, two_b, first_near, first_low, first_high, shown
    )
    two_a, two_b = hop(two_a, True), hop(two_b, False)
    one_a = add_to(one, 1, one_a)
    first_high = swap_row(first_high, 2)
    image_grad = kernel(
        functools.partial(image_back, dims),
        wide_bf16,
        [SM, VM, VM, VM],
        [pair_scratch],
        matmul,
        square + 8 * patches * width,
        where,
        grad_one,
        pool_sum,
        first_full,
    ).reshape(slots, band, cols, width)
    one_a, two_a, two_b, first_low, first_high, image_grad = fence(
        one_a, two_a, two_b, first_low, first_high, image_grad
    )
    one_a, two_b = hop(one_a, True), hop(add_to(two, -2, two_b), False)
    first_high = (first_own[:far] + first_near[0, :far].astype(F32) + first_high.astype(F32)).astype(BF16)
    first_low = swap_row(first_low, 2)
    first_a, first_b, far_a = hop(first_high[0], True), hop(first_high[2], False), hop(first_high[1], True, 2)
    two_a = add_to(two, 1, two_a)
    read_grad, bias_rows = kernel(
        read_end,
        [shape((width, outs), F32), shape((8, width), F32)],
        [VM] * 3,
        [],
        0,
        10 * width * outs,
        read_terms[0],
        read_a,
        read_b,
    )
    one_a, two_a, two_b, first_low, first_high, first_a, first_b, far_a, shown, read_grad = fence(
        one_a, two_a, two_b, first_low, first_high, first_a, first_b, far_a, shown, read_grad
    )
    first_low = (first_own[far:] + first_near[0, far:].astype(F32) + first_low.astype(F32)).astype(BF16)
    first_a = (first_low[3].astype(F32) + first_a.astype(F32) + far_a.astype(F32)).astype(BF16)
    first_a, first_b = hop(first_a, True), hop(add_to(first_high, 3, first_b), False)
    two_a, two_b = hop(two_a, True), hop(add_to(two, -1, two_b), False)
    readout_out = kernel(
        join_columns,
        shape((count, 4 * width), BF16),
        [SM] + [VM] * 4,
        [],
        0,
        16 * count * width,
        where,
        *shown,
    ).reshape(slots, band // 2, cols // 2, 4 * width)
    one_sum = scatter_end(one, one_a, one_b_end)
    two_a, two_b, first_a, first_b, first_low, readout_out, one_sum = fence(
        two_a, two_b, first_a, first_b, first_low, readout_out, one_sum
    )
    first_a, first_b = hop(add_to(first_low, 2, first_a), True), hop(add_to(first_low, 0, first_b), False)
    bias_grad = lax.dynamic_slice(bias_rows, (0, places[2]), (1, outs), allow_negative_indices=False)[0]
    two_sum = scatter_end(two, two_a, two_b)
    conv_grad = jnp.concatenate([one_sum, two_sum[:4]], axis=0)
    conv_grad = conv_grad.reshape(3, 3, own, width)
    tail = first_low[1].astype(F32) + first_a.astype(F32) + first_b.astype(F32)
    first_grad = tail[:own].reshape(own, 4, RING, own).transpose(0, 2, 1, 3).reshape(own, width)
    last_grad = two_sum[4]
    swapped = lax.dynamic_slice(tail, (own, places[0]), (2, own), allow_negative_indices=False)
    plain = lax.dynamic_slice(tail, (own + 2, places[1]), (4, own), allow_negative_indices=False)
    norm_grad = jnp.concatenate([swapped, plain], axis=0)
    return (
        readout_out,
        image_grad,
        first_grad,
        conv_grad,
        last_grad,
        norm_grad,
        read_grad,
        bias_grad,
    )


def per_device(*arrays):
    if lax.axis_size("dp") == RING and lax.axis_size("row") == 4:
        return ringed(*arrays)
    return generic(*arrays)


def solution(mesh):
    return jax.shard_map(
        per_device,
        mesh=mesh,
        in_specs=(
            P("dp", "row", None, None),
            P(("dp", "row"), None),
            P(None, None, ("dp", "row"), None),
            P(("dp", "row"), None),
            P(None, ("dp", "row")),
            P(None, ("dp", "row")),
            P(("dp", "row")),
            P("dp", "row", None, None),
            P("dp"),
        ),
        out_specs=(
            P("dp", "row", None, None),
            P("dp", "row", None, None),
            P(("dp", "row"), None),
            P(None, None, ("dp", "row"), None),
            P(("dp", "row"), None),
            P(None, ("dp", "row")),
            P(None, ("dp", "row")),
            P(("dp", "row")),
        ),
        check_vma=False,
    )
```

```python
import functools

import jax
import jax.numpy as jnp
from jax import lax
from jax.experimental import pallas as pl
from jax.experimental.pallas import tpu as pltpu

from jax.sharding import PartitionSpec as P

eps = 1e-06
F32 = jnp.float32
BF16 = jnp.bfloat16
RING = 8


def ring_order(n):
    return list(range(0, n, 2)) + list(range(n - 1, 0, -2))


def ring_pairs(n):
    order = ring_order(n)
    right = [(order[i], order[(i + 1) % n]) for i in range(n)]
    left = [(b, a) for a, b in right]
    return right, left


def ring_index(n, step):
    me = lax.axis_index("dp")
    place = jnp.where(me % 2 == 0, me // 2, n - 1 - me // 2)
    place = (place + step) % n
    return jnp.where(place < n // 2, 2 * place, 2 * (n - 1 - place) + 1)


def gather_dp(x, n):
    return lax.all_gather(x, "dp", axis=0, tiled=False)


def scatter_dp(parts, n):
    return lax.psum_scatter(parts.astype(F32), "dp", scatter_dimension=0, tiled=False)


def swap_row(x, q):
    return lax.ppermute(x, "row", [(i, i ^ q) for i in range(4)])


def gather_row(x):
    two = swap_row(x, 2)
    one = swap_row(x, 1)
    return [x, one, two, swap_row(two, 1)]


def exchange_row(pieces):
    return [pieces[0]] + [swap_row(pieces[q], q) for q in (1, 2, 3)]


def scatter_row(pieces):
    near = swap_row(jnp.stack([pieces[1], pieces[3]]).astype(BF16), 1).astype(F32)
    mine = pieces[0].astype(F32) + near[0]
    other = (pieces[2].astype(F32) + near[1]).astype(BF16)
    return mine + swap_row(other, 2).astype(F32)


def pick(choices, index):
    value = choices[0]
    for i in range(1, len(choices)):
        value = jnp.where(index == i, choices[i], value)
    return value


def dot(left, right):
    return jnp.dot(left, right, preferred_element_type=F32)


def dot_t(left, right):
    return lax.dot_general(left, right, (((1,), (1,)), ((), ())), preferred_element_type=F32)


def t_dot(left, right):
    return lax.dot_general(left, right, (((0,), (0,)), ((), ())), preferred_element_type=F32)


def normalize(value):
    centred = value - jnp.mean(value, axis=-1, keepdims=True)
    scale = lax.rsqrt(jnp.mean(centred * centred, axis=-1, keepdims=True) + eps)
    return centred * scale, scale


def norm_backward(grad_out, normed, scale, gain):
    weighted = grad_out * gain
    return scale * (
        weighted
        - jnp.mean(weighted, axis=-1, keepdims=True)
        - normed * jnp.mean(weighted * normed, axis=-1, keepdims=True)
    )


def silu_slope(value):
    gate = jax.nn.sigmoid(value)
    return gate * (1.0 + value * (1.0 - gate))


def gelu_slope(value):
    return (
        0.5 * (1.0 + lax.erf(value * 0.7071067811865476))
        + value * jnp.exp(-0.5 * value * value) * 0.3989422804014327
    )


def columns(value):
    cols = value.shape[2]
    wide = jnp.pad(value, ((0, 0), (1, 1), (1, 1), (0, 0)))
    return jnp.concatenate([wide[:, :, v : v + cols] for v in range(3)], axis=3)


def generic(
    images,
    first_weight,
    conv_weight,
    last_weight,
    norm_rows,
    read_weight,
    read_bias,
    cotangent,
    live_count,
):
    n, ranks = lax.axis_size("dp"), lax.axis_size("row")
    row = lax.axis_index("row")
    slots, band, cols, width = images.shape
    patches = slots * band * cols
    high = ranks * band
    own = first_weight.shape[0]
    group = n * own
    outs = read_weight.shape[1]
    rows_at = [row ^ q for q in range(ranks)]

    first_mine = first_weight.reshape(own, n, ranks, own).transpose(0, 2, 1, 3).reshape(own, width)
    small = jnp.concatenate([norm_rows.reshape(-1), read_bias])
    small = jnp.pad(small, (0, 8 * width - small.shape[0])).reshape(8, width)
    first_ring = gather_dp(jnp.concatenate([first_mine, small], axis=0), n)
    first_parts = gather_row(first_ring)

    def interleave(parts):
        whole = jnp.zeros((n, ranks) + parts[0].shape[1:], parts[0].dtype)
        for q in range(ranks):
            whole = lax.dynamic_update_slice(whole, parts[q][:, None], (0, rows_at[q], 0, 0))
        return whole

    first_all = interleave(first_parts)
    first_full = first_all[:, :, :own].reshape(width, width)
    norms = first_all[:, :, own].reshape(n, ranks, width)[:, :, : 6 * own]
    norms = norms.reshape(n, ranks, 6, own).astype(F32)
    norm_vals = norms.transpose(2, 0, 1, 3).reshape(6, width)
    norm_swap = norms.transpose(2, 1, 0, 3).reshape(6, width)
    bias_mine = first_ring[:, own, 6 * own : 6 * own + outs].reshape(n * outs).astype(F32)

    conv_taps = [gather_dp(conv_weight[u].reshape(3 * own, width), n) for u in range(3)]
    conv_taps = [
        tap.reshape(n, 3, own, width).transpose(1, 0, 2, 3).reshape(3 * group, width) for tap in conv_taps
    ]
    last_full = interleave(gather_row(gather_dp(last_weight, n))).reshape(width, width)
    read_mine = gather_dp(read_weight.T, n).reshape(n * outs, width)

    cot = cotangent.reshape(-1, n, ranks, outs)
    cot = exchange_row([pick([cot[:, :, i] for i in range(ranks)], rows_at[q]) for q in range(ranks)])
    cot = jnp.concatenate(cot, axis=0).reshape(-1, n * outs)

    flat_in = images.reshape(patches, width)
    hat_one, scale_one = normalize(dot(flat_in, first_full))
    pre_one = hat_one * norm_swap[0] + norm_swap[1]
    low_one = jax.nn.silu(pre_one).astype(BF16)
    split = [low_one[:, i * group : (i + 1) * group] for i in range(ranks)]
    bands = exchange_row([pick(split, rows_at[q]) for q in range(ranks)])

    def stack_bands(pieces):
        whole = jnp.zeros((slots, ranks, band, cols, pieces[0].shape[-1]), pieces[0].dtype)
        for q in range(ranks):
            piece = pieces[q].reshape(slots, 1, band, cols, -1)
            whole = lax.dynamic_update_slice(whole, piece, (0, rows_at[q], 0, 0, 0))
        return whole.reshape(slots, high, cols, -1)

    def take_bands(value):
        value = value.reshape(slots, ranks, band * cols, -1)
        return [
            lax.dynamic_index_in_dim(value, rows_at[q], 1, keepdims=False).reshape(patches, -1)
            for q in range(ranks)
        ]

    wide_one = columns(stack_bands(bands))
    slabs = [wide_one[:, u : u + high].reshape(slots * high * cols, 3 * group) for u in range(3)]
    act_two = dot(slabs[0], conv_taps[0]) + dot(slabs[1], conv_taps[1]) + dot(slabs[2], conv_taps[2])
    hat_two, scale_two = normalize(scatter_row(take_bands(act_two)))
    pre_two = hat_two * norm_vals[2] + norm_vals[3]
    low_two = jax.nn.silu(pre_two).astype(BF16)
    hat_three, scale_three = normalize(dot(low_two, last_full))
    summed = flat_in.astype(F32) + (hat_three * norm_vals[4] + norm_vals[5])
    pooled = jnp.mean(summed.reshape(slots, band // 2, 2, cols // 2, 2, width), axis=(2, 4)).astype(BF16)
    pooled = pooled.reshape(-1, width)
    pools = jnp.concatenate(gather_row(pooled), axis=0)
    logits = dot_t(pools, read_mine) + bias_mine
    mask = (jnp.arange(slots, dtype=jnp.int32) < live_count[0]).astype(F32)
    mask = jnp.broadcast_to(mask[None, :, None], (ranks, slots, pooled.shape[0] // slots)).reshape(-1, 1)
    shown = (jax.nn.gelu(logits, approximate=False) * mask).astype(BF16)
    shown = exchange_row(jnp.split(shown, ranks, axis=0))
    readout = jnp.zeros((pooled.shape[0], n, ranks, outs), BF16)
    for q in range(ranks):
        readout = lax.dynamic_update_slice(
            readout, shown[q].reshape(-1, n, 1, outs), (0, 0, rows_at[q], 0)
        )
    readout_out = readout.reshape(slots, band // 2, cols // 2, n * ranks * outs)

    grad_low = (cot.astype(F32) * mask * gelu_slope(logits)).astype(BF16)
    read_terms = t_dot(grad_low, pools).reshape(n, outs, width)
    bias_terms = jnp.sum(grad_low.astype(F32), axis=0).reshape(n, 1, outs)
    bias_terms = jnp.pad(bias_terms, ((0, 0), (0, 7), (0, width - outs)))
    read_sum = scatter_dp(jnp.concatenate([read_terms, bias_terms], axis=1), n)
    read_grad, bias_grad = read_sum[:outs].T, read_sum[outs, :outs]
    grad_pool = scatter_row(jnp.split(dot(grad_low, read_mine), ranks, axis=0))
    grad_sum = (
        jnp.broadcast_to(
            grad_pool.reshape(slots, band // 2, 1, cols // 2, 1, width),
            (slots, band // 2, 2, cols // 2, 2, width),
        )
        * 0.25
    ).reshape(-1, width)
    gain_three = jnp.sum(grad_sum * hat_three, axis=0)
    shift_three = jnp.sum(grad_sum, axis=0)
    grad_three = norm_backward(grad_sum, hat_three, scale_three, norm_vals[4]).astype(BF16)
    grad_pre_two = dot_t(grad_three, last_full) * silu_slope(pre_two)
    gain_two = jnp.sum(grad_pre_two * hat_two, axis=0)
    shift_two = jnp.sum(grad_pre_two, axis=0)
    grad_two = norm_backward(grad_pre_two, hat_two, scale_two, norm_vals[2]).astype(BF16)
    grad_full = stack_bands(gather_row(grad_two))
    grad_flat = grad_full.reshape(-1, width)

    def row_sums(terms):
        terms = terms.reshape(n, ranks, -1, width)
        return scatter_row(
            [lax.dynamic_index_in_dim(terms, rows_at[q], 1, keepdims=False) for q in range(ranks)]
        )

    conv_grad = []
    for u in range(3):
        terms = t_dot(slabs[u], grad_flat).reshape(3, n, own, width).transpose(1, 0, 2, 3)
        conv_grad.append(scatter_dp(terms.reshape(n, 3 * own, width), n).reshape(3, own, width))
    conv_grad = jnp.stack(conv_grad)
    wide_grad = jnp.pad(grad_full, ((0, 0), (1, 1), (1, 1), (0, 0)))
    grad_mid = jnp.zeros((slots * high * cols, group), F32)
    for u in range(3):
        for v in range(3):
            slab = wide_grad[:, 2 - u : 2 - u + high, 2 - v : 2 - v + cols].reshape(-1, width)
            grad_mid = grad_mid + dot_t(slab, conv_taps[u][v * group : (v + 1) * group])
    pieces = exchange_row(take_bands(grad_mid.astype(BF16)))
    grad_low_one = jnp.concatenate(
        [pick([pieces[i ^ q] for i in range(ranks)], row) for q in range(ranks)], axis=1
    ).astype(F32)
    last_sum = scatter_dp(row_sums(t_dot(low_two, grad_three)), n)

    grad_pre_one = grad_low_one * silu_slope(pre_one)
    gain_one = jnp.sum(grad_pre_one * hat_one, axis=0)
    shift_one = jnp.sum(grad_pre_one, axis=0)
    grad_one = norm_backward(grad_pre_one, hat_one, scale_one, norm_swap[0]).astype(BF16)
    image_grad = (grad_sum + dot_t(grad_one, first_full)).astype(BF16)
    image_grad = image_grad.reshape(slots, band, cols, width)

    swapped = jnp.stack([gain_one, shift_one]).reshape(2, ranks, n, own).transpose(2, 1, 0, 3)
    plain = jnp.stack([gain_two, shift_two, gain_three, shift_three])
    plain = plain.reshape(4, n, ranks, own).transpose(1, 2, 0, 3)
    norm_terms = jnp.concatenate([swapped, plain], axis=2).reshape(n, ranks, 1, 6 * own)
    norm_terms = jnp.pad(norm_terms, ((0, 0), (0, 0), (0, 7), (0, width - 6 * own)))
    first_terms = t_dot(flat_in, grad_one).reshape(n, ranks, own, width)
    first_sum = scatter_dp(row_sums(jnp.concatenate([first_terms, norm_terms], axis=2)), n)
    norm_grad = first_sum[own, : 6 * own].reshape(6, own)
    first_grad = first_sum[:own].reshape(own, ranks, n, own).transpose(0, 2, 1, 3).reshape(own, width)
    return (
        readout_out,
        image_grad,
        first_grad,
        conv_grad,
        last_sum,
        norm_grad,
        read_grad,
        bias_grad,
    )


VM = pl.BlockSpec(memory_space=pltpu.VMEM)
SM = pl.BlockSpec(memory_space=pltpu.SMEM)
HB = pl.BlockSpec(memory_space=pltpu.HBM)


def shape(dims, dtype):
    return jax.ShapeDtypeStruct(dims, dtype)


def kernel(body, outs, ins, scratch, flops, moved, *arrays, specs=None, room=16):
    return pl.pallas_call(
        body,
        out_shape=outs,
        in_specs=ins,
        out_specs=jax.tree.map(lambda _: VM, outs) if specs is None else specs,
        scratch_shapes=scratch,
        cost_estimate=pl.CostEstimate(flops=flops // 64, bytes_accessed=moved // 64, transcendentals=0),
        compiler_params=pltpu.CompilerParams(vmem_limit_bytes=room << 20),
    )(*arrays)


def at_row(where, q):
    return where[0] ^ q


def start_all(copies):
    for copy in copies:
        copy.start()


def wait_all(copies):
    for copy in copies:
        copy.wait()


def copies_of(pairs, sems):
    return [pltpu.make_async_copy(a, b, sems.at[i]) for i, (a, b) in enumerate(pairs)]


def hop(x, turn, places=1):
    order = ring_order(RING)
    step = places if turn else -places
    return lax.ppermute(x, "dp", [(order[i], order[(i + step) % RING]) for i in range(RING)])


def gather_step(state, step, low=None, high=None):
    pieces, a, b = state
    pieces = list(pieces)
    if step < RING // 2:
        a, b = hop(a, True), hop(b, False)
        pieces[RING - step], pieces[step] = a, b
    else:
        pieces[step] = (hop(low(a), True), hop(high(b), False))
    return pieces, a, b


def gather_state(x):
    return [x] * RING, x, x


def scatter_step(low, high, terms, a, b, step):
    half = RING // 2
    if step == half:
        return hop(low, True), hop(high, False)
    right, left = terms[step].astype(F32), terms[RING - step].astype(F32)
    if step == half - 1:
        cut = low.shape[0]
        right = jnp.concatenate([right[:cut] + a.astype(F32), right[cut:]], axis=0)
        left = jnp.concatenate([left[:cut], left[cut:] + b.astype(F32)], axis=0)
    else:
        right, left = right + a.astype(F32), left + b.astype(F32)
    return hop(right.astype(BF16), True), hop(left.astype(BF16), False)


def scatter_end(terms, a, b):
    return terms[0].astype(F32) + a.astype(F32) + b.astype(F32)


def fence(*values):
    return lax.optimization_barrier(values)


def line_up(where, *refs):
    pieces, (first, last) = refs[: RING + 1], refs[RING + 1 :]
    rows = last.shape[1]
    for k in range(RING):
        if k == RING // 2:
            last[where[2 + k]] = pieces[k][...]
            first[where[2 + k]] = pieces[RING][...]
        else:
            last[where[2 + k]] = pieces[k][:rows]
            first[where[2 + k]] = pieces[k][rows:]


def fill(where, weight, parts):
    rows = weight.shape[2]
    for q, part in enumerate(parts):
        weight[:, at_row(where, q)] = part[:, :rows, :]


def center(value):
    mean = jnp.mean(value, axis=-1, keepdims=True)
    gap = value - mean
    scale = lax.rsqrt(jnp.mean(gap * gap, axis=-1, keepdims=True) + eps)
    return gap * scale, scale


def flat_pieces(pieces):
    half = RING // 2
    return [p[0] if k == half else p for k, p in enumerate(pieces)] + [pieces[half][1]]


def stage_one(where, x, f0, f1, f2, f3, hat, scale, s0, s1, s2, s3, norms, weight, low):
    firsts = (f0, f1, f2, f3)
    fill(where, weight, firsts)
    width, rows = x.shape[1], weight.shape[2]
    total = jnp.zeros((8, width), F32)
    bias = total
    for q, first in enumerate(firsts):
        for k in range(RING):
            block = first[k, rows:, :].astype(F32)
            total = total + block
            if q == 0:
                bias = bias + block
    line = lax.broadcasted_iota(jnp.int32, (8, width), 0)
    table = jnp.where(line == 6, bias, total)
    norms[...] = table
    act = dot(x[...], weight[...].reshape(width, width))
    normed, root = center(act)
    hat[...] = normed
    scale[...] = root
    pre = normed * norms[0:1, :] + norms[1:2, :]
    low[...] = (pre * jax.nn.sigmoid(pre)).astype(BF16)
    part = width // 4
    for q, out in enumerate((s0, s1, s2, s3)):
        out[...] = low[:, pl.ds(pl.multiple_of(at_row(where, q) * part, part), part)]


def conv_copies(where, pieces, weight, sems):
    far = RING // 2
    pairs = []
    for k in range(RING):
        if k == far:
            number = pieces[far].shape[0]
            pairs.append((pieces[far], weight.at[pl.ds(0, number), where[2 + k]]))
            pairs.append((pieces[RING], weight.at[pl.ds(number, pieces[RING].shape[0]), where[2 + k]]))
        else:
            pairs.append((pieces[k], weight.at[:, where[2 + k]]))
    return copies_of(pairs, sems)


def conv_forward(dims, first, where, s0, s1, s2, s3, *refs):
    slots, rows, cols = dims
    if first:
        own, near, spans, weight, pad, moved, wide, sems, done = refs[RING + 1 :]
        copies = conv_copies(where, refs[: RING + 1], weight, sems)
        start_all(copies)
    else:
        weight, own, near, spans, pad, moved, wide, done = refs
    group = s0.shape[1]
    patches = rows * cols
    band = patches // 4
    pad[...] = jnp.zeros_like(pad)
    for q, piece in enumerate((s0, s1, s2, s3)):
        for i in range(slots):
            at = pl.multiple_of(cols + 8 + at_row(where, q) * band, 8)
            pad[i, pl.ds(at, band), :] = piece[i * band : (i + 1) * band, :].astype(F32)
    for v in range(3):
        for i in range(slots):
            shifted = pad[i, 8 + v - 1 : 8 + v - 1 + patches + 2 * cols, :]
            if v != 1:
                col = lax.broadcasted_iota(jnp.int32, shifted.shape, 0) % cols
                shifted = jnp.where(col == (0 if v == 0 else cols - 1), 0.0, shifted)
            moved[i] = shifted

        @pl.loop(0, 2 * slots)
        def _(j):
            q, i = j // slots, j % slots
            here = pl.ds(pl.multiple_of(j * band, 16), band)
            for u in range(3):
                at = pl.multiple_of(at_row(where, first + q) * band + u * cols, 8)
                t = u * 3 + v
                wide[here, t * group : (t + 1) * group] = moved[i, pl.ds(at, band), :].astype(BF16)

    keep = pltpu.make_async_copy(wide, spans, done)
    keep.start()
    if first:
        wait_all(copies)
    width = own.shape[1]
    chunk = 256
    patches = slots * band

    @pl.loop(0, width // chunk)
    def _(j):
        lanes = pl.ds(pl.multiple_of(j * chunk, chunk), chunk)
        terms = dot(wide[...], weight[:, :, :, lanes].reshape(-1, chunk))
        own[:, lanes] = terms[:patches]
        near[:, lanes] = terms[patches:].astype(BF16)

    keep.wait()


def stage_two(dims, where, own, near, cross, x, norms, l0, l1, l2, l3, hat_two, scale_two, low, hat, scale, pooled, weight, pairs):
    slots, rows, cols = dims
    fill(where, weight, (l0, l1, l2, l3))
    width = x.shape[1]
    act = own[...] + near[...].astype(F32) + cross[...].astype(F32)
    normed, root = center(act)
    hat_two[...] = normed
    scale_two[...] = root
    pre = normed * norms[2:3, :] + norms[3:4, :]
    low[...] = (pre * jax.nn.sigmoid(pre)).astype(BF16)
    normed, root = center(dot(low[...], weight[...].reshape(width, width)))
    hat[...] = normed
    scale[...] = root
    y = x[...].astype(F32) + (normed * norms[4:5, :] + norms[5:6, :])
    y = jnp.sum(y.reshape(slots * rows // 2, 2, cols, width), axis=1).reshape(-1, width)
    count = pooled.shape[0]
    for g in range(pairs.shape[0]):
        lanes = slice(g * 128, (g + 1) * 128)
        pairs[g] = y[:, lanes]
        pooled[:, lanes] = (
            0.25 * (pairs[g, pl.ds(0, count, stride=2), :] + pairs[g, pl.ds(1, count, stride=2), :])
        ).astype(BF16)


def read_copies(where, pieces, weight, sems):
    half = RING // 2
    pairs = []
    for k in range(RING):
        if k == half:
            rows = pieces[half].shape[0]
            pairs.append((pieces[half], weight.at[where[2 + k], pl.ds(0, rows)]))
            pairs.append((pieces[RING], weight.at[where[2 + k], pl.ds(rows, rows)]))
        else:
            pairs.append((pieces[k], weight.at[where[2 + k]]))
    return copies_of(pairs, sems)


def readout(slots, where, p0, p1, p2, p3, c0, c1, c2, c3, norms, *refs):
    pieces = refs[: RING + 1]
    o0, o1, o2, o3, low, own, near, far, weight, sems = refs[RING + 1 :]
    copies = read_copies(where, pieces, weight, sems)
    start_all(copies)
    count, width = p0.shape
    table = jnp.concatenate([p[...] for p in (p0, p1, p2, p3)], axis=0)
    line = lax.broadcasted_iota(jnp.int32, (count, width), 0)
    mask = jnp.where(line // (count // slots) < where[1], 1.0, 0.0)
    wait_all(copies)
    whole = weight[...].reshape(-1, width)
    logits = dot_t(table, whole) + norms[6:7, :]
    for q, (cot, out) in enumerate(((c0, o0), (c1, o1), (c2, o2), (c3, o3))):
        z = logits[q * count : (q + 1) * count]
        phi = 0.5 * (1.0 + lax.erf(z * 0.7071067811865476))
        out[...] = (z * phi * mask).astype(BF16)
        slope = phi + z * jnp.exp(-0.5 * z * z) * 0.3989422804014327
        low[q * count : (q + 1) * count, :] = (cot[...].astype(F32) * mask * slope).astype(BF16)
    back = dot(low[...], whole)
    own[...] = back[:count]
    near[0] = back[count : 2 * count].astype(BF16)
    far[...] = back[2 * count : 3 * count]
    near[1] = back[3 * count :].astype(BF16)


def readout_terms(where, low, p0, p1, p2, p3, upper, lower, out, terms):
    width = p0.shape[1]
    table = jnp.concatenate([p[...] for p in (p0, p1, p2, p3)], axis=0)
    terms[...] = t_dot(low[...], table).reshape(terms.shape)
    bias = jnp.sum(low[...].astype(F32), axis=0, keepdims=True)
    rows = terms.shape[1]
    for k in range(RING):
        out[k, :rows, :] = terms[where[2 + k]].astype(BF16)
        out[k, rows:, :] = jnp.broadcast_to(bias, (out.shape[1] - rows, width)).astype(BF16)
    upper[...] = out[RING // 2, : upper.shape[0]]
    lower[...] = out[RING // 2, upper.shape[0] :]


def read_end(term, a, b, out, bias):
    total = term[...].astype(F32) + a[...].astype(F32) + b[...].astype(F32)
    rows = out.shape[1]
    out[...] = total[:rows].T
    bias[...] = total[rows : rows + 8]


def conv_end(one, one_a, one_b, two, two_a, two_b, conv, last):
    taps = one.shape[0]
    conv[:taps] = one[...].astype(F32) + one_a[...].astype(F32) + one_b[...].astype(F32)
    total = two[...].astype(F32) + two_a[...].astype(F32) + two_b[...].astype(F32)
    conv[taps:] = total[:-1]
    last[...] = total[-1]


def first_end(where, term, a, b, grad, norm):
    total = term[...].astype(F32) + a[...].astype(F32) + b[...].astype(F32)
    rows, width = grad.shape
    for g in range(RING):
        for r in range(4):
            to, at = (g * 4 + r) * rows, (r * RING + g) * rows
            grad[:, to : to + rows] = total[:rows, at : at + rows]
    block = total[rows:]
    swapped, plain = [pltpu.roll(block, lax.rem(width - where[i], width), 1)[:, :rows] for i in (18, 19)]
    line = lax.broadcasted_iota(jnp.int32, swapped.shape, 0)
    norm[...] = jnp.where(line < 2, swapped, plain)


def spread(pairs, grad, dims):
    slots, rows, cols = dims
    count, width = grad.shape
    for g in range(pairs.shape[0]):
        lanes = slice(g * 128, (g + 1) * 128)
        pairs[g, pl.ds(0, count, stride=2), :] = grad[:, lanes]
        pairs[g, pl.ds(1, count, stride=2), :] = grad[:, lanes]
    half = slots * rows // 2
    both = jnp.concatenate([pairs[g] for g in range(pairs.shape[0])], axis=1)
    both = jnp.broadcast_to(both.reshape(half, 1, cols, width), (half, 2, cols, width))
    return both.reshape(-1, width) * 0.25


def back_norm(grad, normed, root, gain):
    weighted = grad * gain
    return root * (
        weighted
        - jnp.mean(weighted, axis=-1, keepdims=True)
        - normed * jnp.mean(weighted * normed, axis=-1, keepdims=True)
    )


def total_rows(value):
    return jnp.sum(value, axis=0, keepdims=True)


def stage_two_back(dims, where, own, near, cross, hat, scale, hat_two, scale_two, norms, weight, grad_three, grad_two, pool_sum, sums, pairs):
    width = hat.shape[1]
    grad = own[...] + near[...].astype(F32) + cross[...].astype(F32)
    pool_sum[...] = grad
    gy = spread(pairs, grad, dims)
    sums[...] = jnp.zeros_like(sums)
    sums[4:5, :] = total_rows(gy * hat[...])
    sums[5:6, :] = total_rows(gy)
    grad_three[...] = back_norm(gy, hat[...], scale[...], norms[4:5, :]).astype(BF16)
    gs = dot_t(grad_three[...], weight[...].reshape(width, width))
    pre = hat_two[...] * norms[2:3, :] + norms[3:4, :]
    gn = gs * silu_slope(pre)
    sums[2:3, :] = total_rows(gn * hat_two[...])
    sums[3:4, :] = total_rows(gn)
    grad_two[...] = back_norm(gn, hat_two[...], scale_two[...], norms[2:3, :]).astype(BF16)


def last_terms(where, low, grad, own, near, far, terms):
    terms[...] = t_dot(low[...], grad[...]).reshape(terms.shape)
    for k in range(RING):
        own[k] = terms[where[2 + k], at_row(where, 0)]
        near[0, k] = terms[where[2 + k], at_row(where, 1)].astype(BF16)
        far[k] = terms[where[2 + k], at_row(where, 2)]
        near[1, k] = terms[where[2 + k], at_row(where, 3)].astype(BF16)


def stack_grad(dims, where, pieces, whole):
    slots, rows, cols = dims
    band = rows * cols // 4
    for q, piece in enumerate(pieces):
        for i in range(slots):
            at = pl.multiple_of(i * rows * cols + at_row(where, q) * band, 16)
            whole[pl.ds(at, band), :] = piece[i * band : (i + 1) * band, :]


def conv_half_terms(where, here, g0, g1, out, one):
    count = g0.shape[0]
    one[:count], one[count:] = g0[...], g1[...]
    group = out.shape[1]

    @pl.loop(0, out.shape[0])
    def _(t):
        lanes = pl.ds(pl.multiple_of(t * group, group), group)
        out[t] = t_dot(here[:, lanes], one[...])


def conv_terms(first, number, where, half, there, g2, g3, *refs):
    parts, outs, (two, line) = refs[: -RING - 2], refs[-RING - 2 : -2], refs[-2:]
    count = g2.shape[0]
    two[:count], two[count:] = g2[...], g3[...]
    rows, width = outs[0].shape[1:]
    group = RING * rows

    @pl.loop(0, number)
    def _(t):
        lanes = pl.ds(pl.multiple_of((first + t) * group, group), group)
        terms = half[first + t] + t_dot(there[:, lanes], two[...])
        line[...] = terms.astype(BF16).reshape(RING, rows, width)
        for k in range(RING):
            outs[k][t] = line[where[2 + k]]

    if parts:
        own, near, low, high = parts
        for k in range(RING):
            cross = low[k] if k < RING // 2 else high[k - RING // 2]
            outs[k][number] = (own[k] + near[0, k].astype(F32) + cross.astype(F32)).astype(BF16)


def conv_back(dims, where, g0, g1, g2, g3, weight, o0, o1, o2, o3, whole, held, low):
    slots, rows, cols = dims
    stack_grad(dims, where, (g0, g1, g2, g3), whole)
    patches = rows * cols
    band = patches // 4
    group = o0.shape[1]
    width = whole.shape[1]
    held[...] = jnp.zeros_like(held)
    @pl.loop(0, 3)
    def _(u):
        at = pl.ds(pl.multiple_of(8 + u * cols, 8), patches)
        for v in range(3):
            part = dot_t(whole[...], weight[u * 3 + v].reshape(group, width))
            for i in range(slots):
                held[v, i, at, :] += part[i * patches : (i + 1) * patches]

    col = lax.broadcasted_iota(jnp.int32, (patches, group), 0) % cols
    for i in range(slots):
        value = held[1, i, 8 + cols : 8 + cols + patches, :]
        value += jnp.where(col == cols - 1, 0.0, held[0, i, 9 + cols : 9 + cols + patches, :])
        value += jnp.where(col == 0, 0.0, held[2, i, 7 + cols : 7 + cols + patches, :])
        low[i * patches : (i + 1) * patches, :] = value.astype(BF16)
    for q, out in enumerate((o0, o1, o2, o3)):
        for i in range(slots):
            at = pl.multiple_of(i * patches + at_row(where, q) * band, 16)
            out[i * band : (i + 1) * band, :] = low[pl.ds(at, band), :]


def stage_one_back(where, b0, b1, b2, b3, hat, scale, norms, x, sums, grad_one, own, near, far, low, terms):
    width = hat.shape[1]
    part = width // 4
    for q, piece in enumerate((b0, b1, b2, b3)):
        low[:, pl.ds(pl.multiple_of(at_row(where, q) * part, part), part)] = piece[...]
    pre = hat[...] * norms[0:1, :] + norms[1:2, :]
    gn = low[...].astype(F32) * silu_slope(pre)
    line = lax.broadcasted_iota(jnp.int32, (8, width), 0)
    tail = jnp.where(line == 0, total_rows(gn * hat[...]), jnp.where(line == 1, total_rows(gn), sums[...]))
    grad_one[...] = back_norm(gn, hat[...], scale[...], norms[0:1, :]).astype(BF16)
    terms[...] = t_dot(x[...], grad_one[...]).reshape(terms.shape)
    rows = terms.shape[2]
    for k in range(RING):
        to = where[2 + (k + 3) % RING]
        own[k, :rows] = terms[to, at_row(where, 0)]
        near[0, k, :rows] = terms[to, at_row(where, 1)].astype(BF16)
        far[k, :rows] = terms[to, at_row(where, 2)]
        near[1, k, :rows] = terms[to, at_row(where, 3)].astype(BF16)
        own[k, rows:] = tail
        near[0, k, rows:] = tail.astype(BF16)
        far[k, rows:] = tail
        near[1, k, rows:] = tail.astype(BF16)


def image_back(dims, where, grad_one, pool_sum, weight, out, pairs):
    width = grad_one.shape[1]
    gy = spread(pairs, pool_sum[...], dims)
    out[...] = (gy + dot_t(grad_one[...], weight[...].reshape(width, width))).astype(BF16)


def split_columns(where, x, o0, o1, o2, o3):
    lanes = x.shape[1] // (4 * RING)
    for q, out in enumerate((o0, o1, o2, o3)):
        for g in range(RING):
            at = pl.multiple_of((g * 4 + at_row(where, q)) * lanes, lanes)
            out[:, g * lanes : (g + 1) * lanes] = x[:, pl.ds(at, lanes)]


def join_columns(where, i0, i1, i2, i3, out):
    lanes = out.shape[1] // (4 * RING)
    for q, piece in enumerate((i0, i1, i2, i3)):
        for g in range(RING):
            at = pl.multiple_of((g * 4 + at_row(where, q)) * lanes, lanes)
            out[:, pl.ds(at, lanes)] = piece[:, g * lanes : (g + 1) * lanes]


def ringed(
    images,
    first_weight,
    conv_weight,
    last_weight,
    norm_rows,
    read_weight,
    read_bias,
    cotangent,
    live_count,
):
    dp, row = lax.axis_index("dp"), lax.axis_index("row")
    slots, band, cols, width = images.shape
    dims = (slots, band, cols)
    full = (slots, 4 * band, cols)
    patches = slots * band * cols
    count = patches // 4
    own = first_weight.shape[0]
    group = RING * own
    outs = read_weight.shape[1]
    taps = 9
    DMA = pltpu.SemaphoreType.DMA
    index = jnp.arange(20, dtype=jnp.int32)
    place_of = lambda d: jnp.where(d % 2 == 0, d // 2, RING - 1 - d // 2)
    place = (place_of(dp) + index - 2) % RING
    ahead = jnp.where(place < RING // 2, 2 * place, 2 * (RING - 1 - place) + 1)
    steps = (place_of(index - 10) - place_of(dp)) % RING
    where = jnp.where(index == 0, row, jnp.where(index == 1, live_count[0], jnp.where(index < 10, ahead, steps)))
    where = jnp.where(index == 18, (row * RING + dp) * own, jnp.where(index == 19, (dp * 4 + row) * own, where))
    where = where.astype(jnp.int32)

    first_mine = first_weight.reshape(own, RING, 4, own).transpose(0, 2, 1, 3).reshape(own, width)
    lane = jnp.arange(width, dtype=jnp.int32)[None, :]
    tiled = jnp.tile(norm_rows, (1, width // own))
    at = jnp.where(jnp.arange(6)[:, None] < 2, row * RING + dp, dp * 4 + row)
    small = jnp.where(lane // own == at, tiled, 0).astype(BF16)
    bias = jnp.where(lane // outs == dp, jnp.tile(read_bias, width // outs)[None, :], 0).astype(BF16)
    small = jnp.concatenate([small, bias, jnp.zeros((1, width), BF16)], axis=0)
    first_mine = jnp.concatenate([first_mine, small], axis=0)
    conv = conv_weight.reshape(taps, own, width)
    quarter = shape((count, width), BF16)
    wide_f32, thin_f32, wide_bf16 = (
        shape((patches, width), F32),
        shape((patches, 1), F32),
        shape((patches, width), BF16),
    )
    quarter_f32, near_quarter = shape((count, width), F32), shape((2, count, width), BF16)
    piece = shape((patches, group), BF16)
    block = (RING, own, width)
    matmul = 2 * patches * width * width
    square = 2 * width * width
    square_of = shape((RING, 4, own, width), BF16)
    total = 4 * patches
    pad_rows = full[1] * cols + 2 * cols + 16
    pair_scratch = pltpu.VMEM((width // 128, patches // 2, 128), F32)
    x = images.reshape(patches, width)

    far = RING // 2
    cut = own + 8
    low, high = lambda v: v[:own], lambda v: v[own:]
    more = gather_step(gather_state(conv), 1)
    ring = gather_step(gather_state(jnp.concatenate([last_weight, first_mine], axis=0)), 1)
    read = read_weight.T
    cots = cotangent.reshape(count, -1)
    bias_place = dp * outs
    more, ring, where, read, cots, x, bias_place = fence(more, ring, where, read, cots, x, bias_place)
    ring = gather_step(ring, 2)
    cots = kernel(split_columns, [quarter] * 4, [SM, VM], [], 0, 2 * count * 4 * width * 2, where, cots)
    ring, cots = fence(ring, cots)
    ring = gather_step(ring, 3)
    ring = fence(ring)[0]
    ring = gather_step(ring, 4, low, high)
    more, ring = fence(more, ring)
    ring = ring[0]
    firsts, lasts = kernel(
        line_up,
        [shape((RING, cut, width), BF16), shape((RING, own, width), BF16)],
        [SM] + [VM] * (RING + 1),
        [],
        0,
        4 * RING * (cut + own) * width,
        where,
        *flat_pieces(ring),
    )
    more = gather_step(more, 2)
    first_two, first_one = swap_row(firsts, 2), swap_row(firsts, 1)
    more, firsts, first_two, first_one, lasts = fence(more, firsts, first_two, first_one, lasts)
    more = gather_step(more, 3)
    firsts = [firsts, first_one, first_two, swap_row(first_two, 1)]
    last_two, last_one = swap_row(lasts, 2), swap_row(lasts, 1)
    hat_one, scale_one, *lows, norms, first_full = kernel(
        stage_one,
        [wide_f32, thin_f32] + [piece] * 4 + [shape((8, width), F32), square_of],
        [SM] + [VM] * 5,
        [pltpu.VMEM((patches, width), BF16)],
        matmul,
        square + 8 * patches * width,
        where,
        x,
        *firsts,
    )
    more, lows, lasts, last_two, last_one = fence(more, lows, lasts, last_two, last_one)
    taps_half = (taps + 1) // 2
    more = gather_step(more, 4, lambda v: v[:taps_half], lambda v: v[taps_half:])
    lows = exchange_row(lows)
    lasts = [lasts, last_one, last_two, swap_row(last_two, 1)]
    weights = flat_pieces(more[0])
    weights, lows, lasts, read, cots = fence(weights, lows, lasts, read, cots)

    conv_whole = (taps, RING, own, width)

    def conv_half(first, weights):
        return kernel(
            functools.partial(conv_forward, full, first),
            [wide_f32, wide_bf16, shape((2 * patches, taps * group), BF16)]
            + ([shape(conv_whole, BF16)] if first else []),
            [SM] + [VM] * 4 + ([HB] * (RING + 1) if first else [VM]),
            [
                pltpu.VMEM((slots, pad_rows, group), F32),
                pltpu.VMEM((slots, pad_rows - 16, group), F32),
                pltpu.VMEM((2 * patches, taps * group), BF16),
            ]
            + ([DMA((RING + 1,))] if first else [])
            + [DMA],
            9 * matmul // 2,
            9 * square + 6 * patches * width + 4 * patches * taps * group,
            where,
            *lows,
            *weights,
            specs=[VM, VM, HB] + ([VM] if first else []),
        )

    read = gather_step(gather_state(read), 1)
    cots = exchange_row(cots)
    away, near, spans_far, conv_full = conv_half(2, weights)
    away, near, read, cots = fence(away, near, read, cots)
    other = (away + swap_row(near, 1).astype(F32)).astype(BF16)
    other, lows, read = fence(other, lows, read)
    cross = swap_row(other, 2)
    read = gather_step(read, 2)
    mine, near, spans_near = conv_half(0, (conv_full,))
    near, read = fence(near, read)
    near = swap_row(near, 1)
    read = gather_step(read, 3)
    mine, near, cross, read = fence(mine, near, cross, read)
    read = gather_step(read, 4, lambda v: v[: outs // 2], lambda v: v[outs // 2 :])
    hat_two, scale_two, low_two, hat_three, scale_three, pooled, last_full = kernel(
        functools.partial(stage_two, dims),
        [wide_f32, thin_f32, wide_bf16, wide_f32, thin_f32, quarter, square_of],
        [SM] + [VM] * 9,
        [pair_scratch],
        matmul,
        square + 24 * patches * width,
        where,
        mine,
        near,
        cross,
        x,
        norms,
        *lasts,
    )
    pool_two, pool_one = swap_row(pooled, 2), swap_row(pooled, 1)
    pooled, pool_two, pool_one, read = fence(pooled, pool_two, pool_one, read)
    pools = [pooled, pool_one, pool_two, swap_row(pool_two, 1)]
    *shown, grad_low, mine, near, away = kernel(
        functools.partial(readout, slots),
        [quarter] * 4 + [wide_bf16, quarter_f32, near_quarter, quarter_f32],
        [SM] + [VM] * 9 + [HB] * (RING + 1),
        [pltpu.VMEM((RING, outs, width), BF16), DMA((RING + 1,))],
        2 * matmul,
        square + 12 * patches * width,
        where,
        *pools,
        *cots,
        norms,
        *flat_pieces(read[0]),
    )

    near = swap_row(near, 1)
    other = (away + near[1].astype(F32)).astype(BF16)
    other, grad_low, near = fence(other, grad_low, near)
    cross = swap_row(other, 2)
    half_read = shape(((outs + 16) // 2, width), BF16)
    *read_far, read_terms = kernel(
        readout_terms,
        [half_read, half_read, shape((RING, outs + 16, width), BF16)],
        [SM] + [VM] * 5,
        [pltpu.VMEM((RING, outs, width), F32)],
        matmul,
        2 * square,
        where,
        grad_low,
        *pools,
    )
    cross, read_far, read_terms, near = fence(cross, read_far, read_terms, near)
    read_a, read_b = scatter_step(*read_far, read_terms, None, None, 4)
    grad_three, grad_two, pool_sum, sums = kernel(
        functools.partial(stage_two_back, dims),
        [wide_bf16, wide_bf16, quarter_f32, shape((8, width), F32)],
        [SM] + [VM] * 9,
        [pair_scratch],
        matmul,
        square + 14 * patches * width,
        where,
        mine,
        near[0],
        cross,
        hat_three,
        scale_three,
        hat_two,
        scale_two,
        norms,
        last_full,
    )
    grad_three, grad_two, read_a, read_b = fence(grad_three, grad_two, read_a, read_b)
    grad_far, grad_next = swap_row(grad_two, 2), swap_row(grad_two, 1)
    read_a, read_b = scatter_step(*read_far, read_terms, read_a, read_b, 3)
    read_a, read_b = scatter_step(*read_far, read_terms, read_a, read_b, 2)
    here = kernel(
        conv_half_terms,
        shape((taps, group, width), F32),
        [SM] + [VM] * 3,
        [pltpu.VMEM((2 * patches, width), BF16)],
        9 * matmul // 2,
        18 * square,
        where,
        spans_near,
        grad_two,
        grad_next,
    )
    last_own, last_near, last_far = kernel(
        last_terms,
        [shape(block, F32), shape((2,) + block, BF16), shape(block, F32)],
        [SM, VM, VM],
        [pltpu.VMEM((RING, 4, own, width), F32)],
        matmul,
        3 * square,
        where,
        low_two,
        grad_three,
    )
    grad_two, grad_far, grad_next, last_near, last_far, read_a, read_b, here = fence(
        grad_two, grad_far, grad_next, last_near, last_far, read_a, read_b, here
    )
    grads = [grad_two, grad_next, grad_far, swap_row(grad_far, 1)]
    last_near = swap_row(last_near, 1)
    last_low = (last_far[:far] + last_near[1, :far].astype(F32)).astype(BF16)
    last_high = (last_far[far:] + last_near[1, far:].astype(F32)).astype(BF16)
    grads, last_near, last_low, last_high = fence(grads, last_near, last_low, last_high)
    last_low = swap_row(last_low, 2)
    read_a, read_b = scatter_step(*read_far, read_terms, read_a, read_b, 1)

    def weight_terms(first, number, parts):
        held = number + len(parts) // 4
        return kernel(
            functools.partial(conv_terms, first, number),
            [shape((held, own, width), BF16)] * RING,
            [SM] + [VM] * (4 + len(parts)),
            [pltpu.VMEM((2 * patches, width), BF16), pltpu.VMEM((RING, own, width), BF16)],
            matmul * number,
            2 * square * number,
            where,
            here,
            spans_far,
            *grads[2:],
            *parts,
        )

    def add_to(terms, k, value):
        return (terms[k % RING].astype(F32) + value.astype(F32)).astype(BF16)

    one = weight_terms(0, 5, ())
    one, grads, last_low, last_high, read_a, read_b = fence(
        one, grads, last_low, last_high, read_a, read_b
    )
    last_high = swap_row(last_high, 2)
    one_a, one_b = hop(one[far], True), hop(one[far + 1], False)
    backs = kernel(
        functools.partial(conv_back, full),
        [piece] * 4,
        [SM] + [VM] * 5,
        [
            pltpu.VMEM((total, width), BF16),
            pltpu.VMEM((3, slots, pad_rows, group), F32),
            pltpu.VMEM((total, group), BF16),
        ],
        9 * matmul,
        9 * square + 12 * patches * width,
        where,
        *grads,
        conv_full,
    )
    one_a, one_b, backs, grads, last_high = fence(one_a, one_b, backs, grads, last_high)
    one_a, one_b = hop(add_to(one, 3, one_a), True), hop(add_to(one, -2, one_b), False)
    backs = exchange_row(backs)
    two = weight_terms(5, 4, (last_own, last_near, last_low, last_high))
    one_a, one_b, two, backs = fence(one_a, one_b, two, backs)
    two_a, two_b = hop(two[far - 1], True), hop(two[far], False)
    one_a, one_b = add_to(one, 2, one_a), add_to(one, -1, one_b)
    block = (RING, own + 8, width)
    grad_one, first_own, first_near, first_far = kernel(
        stage_one_back,
        [wide_bf16, shape(block, F32), shape((2,) + block, BF16), shape(block, F32)],
        [SM] + [VM] * 9,
        [pltpu.VMEM((patches, width), BF16), pltpu.VMEM((RING, 4, own, width), F32)],
        matmul,
        3 * square + 8 * patches * width,
        where,
        *backs,
        hat_one,
        scale_one,
        norms,
        x,
        sums,
    )
    one_a, one_b, two_a, two_b, grad_one, first_own, first_near, first_far, shown = fence(
        one_a, one_b, two_a, two_b, grad_one, first_own, first_near, first_far, shown
    )
    one_a, one_b = hop(one_a, True), hop(one_b, False)
    two_a, two_b = add_to(two, 2, two_a), add_to(two, -3, two_b)
    first_near = swap_row(first_near, 1)
    shown = exchange_row(shown)
    first_low = (first_far[far:] + first_near[1, far:].astype(F32)).astype(BF16)
    first_high = (first_far[:far] + first_near[1, :far].astype(F32)).astype(BF16)
    one_a, one_b_end, two_a, two_b, first_near, first_low, first_high, shown = fence(
        one_a, one_b, two_a, two_b, first_near, first_low, first_high, shown
    )
    two_a, two_b = hop(two_a, True), hop(two_b, False)
    one_a = add_to(one, 1, one_a)
    first_high = swap_row(first_high, 2)
    image_grad = kernel(
        functools.partial(image_back, dims),
        wide_bf16,
        [SM, VM, VM, VM],
        [pair_scratch],
        matmul,
        square + 8 * patches * width,
        where,
        grad_one,
        pool_sum,
        first_full,
    ).reshape(slots, band, cols, width)
    one_a, two_a, two_b, first_low, first_high, image_grad = fence(
        one_a, two_a, two_b, first_low, first_high, image_grad
    )
    one_a, two_b = hop(one_a, True), hop(add_to(two, -2, two_b), False)
    first_high = (first_own[:far] + first_near[0, :far].astype(F32) + first_high.astype(F32)).astype(BF16)
    first_low = swap_row(first_low, 2)
    first_a, first_b, far_a = hop(first_high[0], True), hop(first_high[2], False), hop(first_high[1], True, 2)
    two_a = add_to(two, 1, two_a)
    read_grad, bias_rows = kernel(
        read_end,
        [shape((width, outs), F32), shape((8, width), F32)],
        [VM] * 3,
        [],
        0,
        10 * width * outs,
        read_terms[0],
        read_a,
        read_b,
    )
    one_a, two_a, two_b, first_low, first_high, first_a, first_b, far_a, shown, read_grad = fence(
        one_a, two_a, two_b, first_low, first_high, first_a, first_b, far_a, shown, read_grad
    )
    first_low = (first_own[far:] + first_near[0, far:].astype(F32) + first_low.astype(F32)).astype(BF16)
    first_a = (first_low[3].astype(F32) + first_a.astype(F32) + far_a.astype(F32)).astype(BF16)
    first_a, first_b = hop(first_a, True), hop(add_to(first_high, 3, first_b), False)
    two_a, two_b = hop(two_a, True), hop(add_to(two, -1, two_b), False)
    readout_out = kernel(
        join_columns,
        shape((count, 4 * width), BF16),
        [SM] + [VM] * 4,
        [],
        0,
        16 * count * width,
        where,
        *shown,
    ).reshape(slots, band // 2, cols // 2, 4 * width)
    two_a, two_b, first_a, first_b, first_low, readout_out = fence(
        two_a, two_b, first_a, first_b, first_low, readout_out
    )
    first_a, first_b = hop(add_to(first_low, 2, first_a), True), hop(add_to(first_low, 0, first_b), False)
    bias_grad = lax.dynamic_slice(bias_rows, (0, bias_place), (1, outs), allow_negative_indices=False)[0]
    conv_grad, last_grad = kernel(
        conv_end,
        [shape((taps, own, width), F32), shape((own, width), F32)],
        [VM] * 6,
        [],
        0,
        10 * (taps + 1) * own * width,
        one[0],
        one_a,
        one_b_end,
        two[0],
        two_a,
        two_b,
    )
    conv_grad = conv_grad.reshape(3, 3, own, width)
    first_grad, norm_grad = kernel(
        first_end,
        [shape((own, width), F32), shape((8, own), F32)],
        [SM] + [VM] * 3,
        [],
        0,
        10 * own * width,
        where,
        first_low[1],
        first_a,
        first_b,
    )
    norm_grad = norm_grad[:6]
    return (
        readout_out,
        image_grad,
        first_grad,
        conv_grad,
        last_grad,
        norm_grad,
        read_grad,
        bias_grad,
    )


def per_device(*arrays):
    if lax.axis_size("dp") == RING and lax.axis_size("row") == 4:
        return ringed(*arrays)
    return generic(*arrays)


def solution(mesh):
    return jax.shard_map(
        per_device,
        mesh=mesh,
        in_specs=(
            P("dp", "row", None, None),
            P(("dp", "row"), None),
            P(None, None, ("dp", "row"), None),
            P(("dp", "row"), None),
            P(None, ("dp", "row")),
            P(None, ("dp", "row")),
            P(("dp", "row")),
            P("dp", "row", None, None),
            P("dp"),
        ),
        out_specs=(
            P("dp", "row", None, None),
            P("dp", "row", None, None),
            P(("dp", "row"), None),
            P(None, None, ("dp", "row"), None),
            P(("dp", "row"), None),
            P(None, ("dp", "row")),
            P(None, ("dp", "row")),
            P(("dp", "row")),
        ),
        check_vma=False,
    )
```

```python
import functools

import jax
import jax.numpy as jnp
from jax import lax
from jax.experimental import pallas as pl
from jax.experimental.pallas import tpu as pltpu

from jax.sharding import PartitionSpec as P

eps = 1e-06
F32 = jnp.float32
BF16 = jnp.bfloat16
RING = 8


def ring_order(n):
    return list(range(0, n, 2)) + list(range(n - 1, 0, -2))


def ring_pairs(n):
    order = ring_order(n)
    right = [(order[i], order[(i + 1) % n]) for i in range(n)]
    left = [(b, a) for a, b in right]
    return right, left


def ring_index(n, step):
    me = lax.axis_index("dp")
    place = jnp.where(me % 2 == 0, me // 2, n - 1 - me // 2)
    place = (place + step) % n
    return jnp.where(place < n // 2, 2 * place, 2 * (n - 1 - place) + 1)


def gather_dp(x, n):
    return lax.all_gather(x, "dp", axis=0, tiled=False)


def scatter_dp(parts, n):
    return lax.psum_scatter(parts.astype(F32), "dp", scatter_dimension=0, tiled=False)


def swap_row(x, q):
    return lax.ppermute(x, "row", [(i, i ^ q) for i in range(4)])


def gather_row(x):
    two = swap_row(x, 2)
    one = swap_row(x, 1)
    return [x, one, two, swap_row(two, 1)]


def exchange_row(pieces):
    return [pieces[0]] + [swap_row(pieces[q], q) for q in (1, 2, 3)]


def scatter_row(pieces):
    near = swap_row(jnp.stack([pieces[1], pieces[3]]).astype(BF16), 1).astype(F32)
    mine = pieces[0].astype(F32) + near[0]
    other = (pieces[2].astype(F32) + near[1]).astype(BF16)
    return mine + swap_row(other, 2).astype(F32)


def pick(choices, index):
    value = choices[0]
    for i in range(1, len(choices)):
        value = jnp.where(index == i, choices[i], value)
    return value


def dot(left, right):
    return jnp.dot(left, right, preferred_element_type=F32)


def dot_t(left, right):
    return lax.dot_general(left, right, (((1,), (1,)), ((), ())), preferred_element_type=F32)


def t_dot(left, right):
    return lax.dot_general(left, right, (((0,), (0,)), ((), ())), preferred_element_type=F32)


def normalize(value):
    centred = value - jnp.mean(value, axis=-1, keepdims=True)
    scale = lax.rsqrt(jnp.mean(centred * centred, axis=-1, keepdims=True) + eps)
    return centred * scale, scale


def norm_backward(grad_out, normed, scale, gain):
    weighted = grad_out * gain
    return scale * (
        weighted
        - jnp.mean(weighted, axis=-1, keepdims=True)
        - normed * jnp.mean(weighted * normed, axis=-1, keepdims=True)
    )


def silu_slope(value):
    gate = jax.nn.sigmoid(value)
    return gate * (1.0 + value * (1.0 - gate))


def gelu_slope(value):
    return (
        0.5 * (1.0 + lax.erf(value * 0.7071067811865476))
        + value * jnp.exp(-0.5 * value * value) * 0.3989422804014327
    )


def columns(value):
    cols = value.shape[2]
    wide = jnp.pad(value, ((0, 0), (1, 1), (1, 1), (0, 0)))
    return jnp.concatenate([wide[:, :, v : v + cols] for v in range(3)], axis=3)


def generic(
    images,
    first_weight,
    conv_weight,
    last_weight,
    norm_rows,
    read_weight,
    read_bias,
    cotangent,
    live_count,
):
    n, ranks = lax.axis_size("dp"), lax.axis_size("row")
    row = lax.axis_index("row")
    slots, band, cols, width = images.shape
    patches = slots * band * cols
    high = ranks * band
    own = first_weight.shape[0]
    group = n * own
    outs = read_weight.shape[1]
    rows_at = [row ^ q for q in range(ranks)]

    first_mine = first_weight.reshape(own, n, ranks, own).transpose(0, 2, 1, 3).reshape(own, width)
    small = jnp.concatenate([norm_rows.reshape(-1), read_bias])
    small = jnp.pad(small, (0, 8 * width - small.shape[0])).reshape(8, width)
    first_ring = gather_dp(jnp.concatenate([first_mine, small], axis=0), n)
    first_parts = gather_row(first_ring)

    def interleave(parts):
        whole = jnp.zeros((n, ranks) + parts[0].shape[1:], parts[0].dtype)
        for q in range(ranks):
            whole = lax.dynamic_update_slice(whole, parts[q][:, None], (0, rows_at[q], 0, 0))
        return whole

    first_all = interleave(first_parts)
    first_full = first_all[:, :, :own].reshape(width, width)
    norms = first_all[:, :, own].reshape(n, ranks, width)[:, :, : 6 * own]
    norms = norms.reshape(n, ranks, 6, own).astype(F32)
    norm_vals = norms.transpose(2, 0, 1, 3).reshape(6, width)
    norm_swap = norms.transpose(2, 1, 0, 3).reshape(6, width)
    bias_mine = first_ring[:, own, 6 * own : 6 * own + outs].reshape(n * outs).astype(F32)

    conv_taps = [gather_dp(conv_weight[u].reshape(3 * own, width), n) for u in range(3)]
    conv_taps = [
        tap.reshape(n, 3, own, width).transpose(1, 0, 2, 3).reshape(3 * group, width) for tap in conv_taps
    ]
    last_full = interleave(gather_row(gather_dp(last_weight, n))).reshape(width, width)
    read_mine = gather_dp(read_weight.T, n).reshape(n * outs, width)

    cot = cotangent.reshape(-1, n, ranks, outs)
    cot = exchange_row([pick([cot[:, :, i] for i in range(ranks)], rows_at[q]) for q in range(ranks)])
    cot = jnp.concatenate(cot, axis=0).reshape(-1, n * outs)

    flat_in = images.reshape(patches, width)
    hat_one, scale_one = normalize(dot(flat_in, first_full))
    pre_one = hat_one * norm_swap[0] + norm_swap[1]
    low_one = jax.nn.silu(pre_one).astype(BF16)
    split = [low_one[:, i * group : (i + 1) * group] for i in range(ranks)]
    bands = exchange_row([pick(split, rows_at[q]) for q in range(ranks)])

    def stack_bands(pieces):
        whole = jnp.zeros((slots, ranks, band, cols, pieces[0].shape[-1]), pieces[0].dtype)
        for q in range(ranks):
            piece = pieces[q].reshape(slots, 1, band, cols, -1)
            whole = lax.dynamic_update_slice(whole, piece, (0, rows_at[q], 0, 0, 0))
        return whole.reshape(slots, high, cols, -1)

    def take_bands(value):
        value = value.reshape(slots, ranks, band * cols, -1)
        return [
            lax.dynamic_index_in_dim(value, rows_at[q], 1, keepdims=False).reshape(patches, -1)
            for q in range(ranks)
        ]

    wide_one = columns(stack_bands(bands))
    slabs = [wide_one[:, u : u + high].reshape(slots * high * cols, 3 * group) for u in range(3)]
    act_two = dot(slabs[0], conv_taps[0]) + dot(slabs[1], conv_taps[1]) + dot(slabs[2], conv_taps[2])
    hat_two, scale_two = normalize(scatter_row(take_bands(act_two)))
    pre_two = hat_two * norm_vals[2] + norm_vals[3]
    low_two = jax.nn.silu(pre_two).astype(BF16)
    hat_three, scale_three = normalize(dot(low_two, last_full))
    summed = flat_in.astype(F32) + (hat_three * norm_vals[4] + norm_vals[5])
    pooled = jnp.mean(summed.reshape(slots, band // 2, 2, cols // 2, 2, width), axis=(2, 4)).astype(BF16)
    pooled = pooled.reshape(-1, width)
    pools = jnp.concatenate(gather_row(pooled), axis=0)
    logits = dot_t(pools, read_mine) + bias_mine
    mask = (jnp.arange(slots, dtype=jnp.int32) < live_count[0]).astype(F32)
    mask = jnp.broadcast_to(mask[None, :, None], (ranks, slots, pooled.shape[0] // slots)).reshape(-1, 1)
    shown = (jax.nn.gelu(logits, approximate=False) * mask).astype(BF16)
    shown = exchange_row(jnp.split(shown, ranks, axis=0))
    readout = jnp.zeros((pooled.shape[0], n, ranks, outs), BF16)
    for q in range(ranks):
        readout = lax.dynamic_update_slice(
            readout, shown[q].reshape(-1, n, 1, outs), (0, 0, rows_at[q], 0)
        )
    readout_out = readout.reshape(slots, band // 2, cols // 2, n * ranks * outs)

    grad_low = (cot.astype(F32) * mask * gelu_slope(logits)).astype(BF16)
    read_terms = t_dot(grad_low, pools).reshape(n, outs, width)
    bias_terms = jnp.sum(grad_low.astype(F32), axis=0).reshape(n, 1, outs)
    bias_terms = jnp.pad(bias_terms, ((0, 0), (0, 7), (0, width - outs)))
    read_sum = scatter_dp(jnp.concatenate([read_terms, bias_terms], axis=1), n)
    read_grad, bias_grad = read_sum[:outs].T, read_sum[outs, :outs]
    grad_pool = scatter_row(jnp.split(dot(grad_low, read_mine), ranks, axis=0))
    grad_sum = (
        jnp.broadcast_to(
            grad_pool.reshape(slots, band // 2, 1, cols // 2, 1, width),
            (slots, band // 2, 2, cols // 2, 2, width),
        )
        * 0.25
    ).reshape(-1, width)
    gain_three = jnp.sum(grad_sum * hat_three, axis=0)
    shift_three = jnp.sum(grad_sum, axis=0)
    grad_three = norm_backward(grad_sum, hat_three, scale_three, norm_vals[4]).astype(BF16)
    grad_pre_two = dot_t(grad_three, last_full) * silu_slope(pre_two)
    gain_two = jnp.sum(grad_pre_two * hat_two, axis=0)
    shift_two = jnp.sum(grad_pre_two, axis=0)
    grad_two = norm_backward(grad_pre_two, hat_two, scale_two, norm_vals[2]).astype(BF16)
    grad_full = stack_bands(gather_row(grad_two))
    grad_flat = grad_full.reshape(-1, width)

    def row_sums(terms):
        terms = terms.reshape(n, ranks, -1, width)
        return scatter_row(
            [lax.dynamic_index_in_dim(terms, rows_at[q], 1, keepdims=False) for q in range(ranks)]
        )

    conv_grad = []
    for u in range(3):
        terms = t_dot(slabs[u], grad_flat).reshape(3, n, own, width).transpose(1, 0, 2, 3)
        conv_grad.append(scatter_dp(terms.reshape(n, 3 * own, width), n).reshape(3, own, width))
    conv_grad = jnp.stack(conv_grad)
    wide_grad = jnp.pad(grad_full, ((0, 0), (1, 1), (1, 1), (0, 0)))
    grad_mid = jnp.zeros((slots * high * cols, group), F32)
    for u in range(3):
        for v in range(3):
            slab = wide_grad[:, 2 - u : 2 - u + high, 2 - v : 2 - v + cols].reshape(-1, width)
            grad_mid = grad_mid + dot_t(slab, conv_taps[u][v * group : (v + 1) * group])
    pieces = exchange_row(take_bands(grad_mid.astype(BF16)))
    grad_low_one = jnp.concatenate(
        [pick([pieces[i ^ q] for i in range(ranks)], row) for q in range(ranks)], axis=1
    ).astype(F32)
    last_sum = scatter_dp(row_sums(t_dot(low_two, grad_three)), n)

    grad_pre_one = grad_low_one * silu_slope(pre_one)
    gain_one = jnp.sum(grad_pre_one * hat_one, axis=0)
    shift_one = jnp.sum(grad_pre_one, axis=0)
    grad_one = norm_backward(grad_pre_one, hat_one, scale_one, norm_swap[0]).astype(BF16)
    image_grad = (grad_sum + dot_t(grad_one, first_full)).astype(BF16)
    image_grad = image_grad.reshape(slots, band, cols, width)

    swapped = jnp.stack([gain_one, shift_one]).reshape(2, ranks, n, own).transpose(2, 1, 0, 3)
    plain = jnp.stack([gain_two, shift_two, gain_three, shift_three])
    plain = plain.reshape(4, n, ranks, own).transpose(1, 2, 0, 3)
    norm_terms = jnp.concatenate([swapped, plain], axis=2).reshape(n, ranks, 1, 6 * own)
    norm_terms = jnp.pad(norm_terms, ((0, 0), (0, 0), (0, 7), (0, width - 6 * own)))
    first_terms = t_dot(flat_in, grad_one).reshape(n, ranks, own, width)
    first_sum = scatter_dp(row_sums(jnp.concatenate([first_terms, norm_terms], axis=2)), n)
    norm_grad = first_sum[own, : 6 * own].reshape(6, own)
    first_grad = first_sum[:own].reshape(own, ranks, n, own).transpose(0, 2, 1, 3).reshape(own, width)
    return (
        readout_out,
        image_grad,
        first_grad,
        conv_grad,
        last_sum,
        norm_grad,
        read_grad,
        bias_grad,
    )


VM = pl.BlockSpec(memory_space=pltpu.VMEM)
SM = pl.BlockSpec(memory_space=pltpu.SMEM)
HB = pl.BlockSpec(memory_space=pltpu.HBM)


def shape(dims, dtype):
    return jax.ShapeDtypeStruct(dims, dtype)


def kernel(body, outs, ins, scratch, flops, moved, *arrays, specs=None, room=16):
    return pl.pallas_call(
        body,
        out_shape=outs,
        in_specs=ins,
        out_specs=jax.tree.map(lambda _: VM, outs) if specs is None else specs,
        scratch_shapes=scratch,
        cost_estimate=pl.CostEstimate(flops=flops // 64, bytes_accessed=moved // 64, transcendentals=0),
        compiler_params=pltpu.CompilerParams(vmem_limit_bytes=room << 20),
    )(*arrays)


def at_row(where, q):
    return where[0] ^ q


def start_all(copies):
    for copy in copies:
        copy.start()


def wait_all(copies):
    for copy in copies:
        copy.wait()


def copies_of(pairs, sems):
    return [pltpu.make_async_copy(a, b, sems.at[i]) for i, (a, b) in enumerate(pairs)]


def hop(x, turn, places=1):
    order = ring_order(RING)
    step = places if turn else -places
    return lax.ppermute(x, "dp", [(order[i], order[(i + step) % RING]) for i in range(RING)])


def gather_step(state, step, low=None, high=None):
    pieces, a, b = state
    pieces = list(pieces)
    if step < RING // 2:
        a, b = hop(a, True), hop(b, False)
        pieces[RING - step], pieces[step] = a, b
    else:
        pieces[step] = (hop(low(a), True), hop(high(b), False))
    return pieces, a, b


def gather_state(x):
    return [x] * RING, x, x


def scatter_step(low, high, terms, a, b, step):
    half = RING // 2
    if step == half:
        return hop(low, True), hop(high, False)
    right, left = terms[step].astype(F32), terms[RING - step].astype(F32)
    if step == half - 1:
        cut = low.shape[0]
        right = jnp.concatenate([right[:cut] + a.astype(F32), right[cut:]], axis=0)
        left = jnp.concatenate([left[:cut], left[cut:] + b.astype(F32)], axis=0)
    else:
        right, left = right + a.astype(F32), left + b.astype(F32)
    return hop(right.astype(BF16), True), hop(left.astype(BF16), False)


def scatter_end(terms, a, b):
    return terms[0].astype(F32) + a.astype(F32) + b.astype(F32)


def fence(*values):
    return lax.optimization_barrier(values)


def line_up(where, *refs):
    pieces, (first, last) = refs[: RING + 1], refs[RING + 1 :]
    rows = last.shape[1]
    for k in range(RING):
        if k == RING // 2:
            last[where[2 + k]] = pieces[k][...]
            first[where[2 + k]] = pieces[RING][...]
        else:
            last[where[2 + k]] = pieces[k][:rows]
            first[where[2 + k]] = pieces[k][rows:]


def fill(where, weight, parts):
    rows = weight.shape[2]
    for q, part in enumerate(parts):
        weight[:, at_row(where, q)] = part[:, :rows, :]


def center(value):
    mean = jnp.mean(value, axis=-1, keepdims=True)
    gap = value - mean
    scale = lax.rsqrt(jnp.mean(gap * gap, axis=-1, keepdims=True) + eps)
    return gap * scale, scale


def flat_pieces(pieces):
    half = RING // 2
    return [p[0] if k == half else p for k, p in enumerate(pieces)] + [pieces[half][1]]


def stage_one(where, x, f0, f1, f2, f3, hat, scale, s0, s1, s2, s3, norms, weight, low):
    firsts = (f0, f1, f2, f3)
    fill(where, weight, firsts)
    width, rows = x.shape[1], weight.shape[2]
    total = jnp.zeros((8, width), F32)
    bias = total
    for q, first in enumerate(firsts):
        for k in range(RING):
            block = first[k, rows:, :].astype(F32)
            total = total + block
            if q == 0:
                bias = bias + block
    line = lax.broadcasted_iota(jnp.int32, (8, width), 0)
    table = jnp.where(line == 6, bias, total)
    norms[...] = table
    act = dot(x[...], weight[...].reshape(width, width))
    normed, root = center(act)
    hat[...] = normed
    scale[...] = root
    pre = normed * norms[0:1, :] + norms[1:2, :]
    low[...] = (pre * jax.nn.sigmoid(pre)).astype(BF16)
    part = width // 4
    for q, out in enumerate((s0, s1, s2, s3)):
        out[...] = low[:, pl.ds(pl.multiple_of(at_row(where, q) * part, part), part)]


def conv_copies(where, pieces, weight, sems):
    far = RING // 2
    pairs = []
    for k in range(RING):
        if k == far:
            number = pieces[far].shape[0]
            pairs.append((pieces[far], weight.at[pl.ds(0, number), where[2 + k]]))
            pairs.append((pieces[RING], weight.at[pl.ds(number, pieces[RING].shape[0]), where[2 + k]]))
        else:
            pairs.append((pieces[k], weight.at[:, where[2 + k]]))
    return copies_of(pairs, sems)


def conv_forward(dims, first, where, s0, s1, s2, s3, *refs):
    slots, rows, cols = dims
    if first:
        own, near, spans, weight, pad, moved, wide, sems, done = refs[RING + 1 :]
        copies = conv_copies(where, refs[: RING + 1], weight, sems)
        start_all(copies)
    else:
        weight, own, near, spans, pad, moved, wide, done = refs
    group = s0.shape[1]
    patches = rows * cols
    band = patches // 4
    pad[...] = jnp.zeros_like(pad)
    for q, piece in enumerate((s0, s1, s2, s3)):
        for i in range(slots):
            at = pl.multiple_of(cols + 8 + at_row(where, q) * band, 8)
            pad[i, pl.ds(at, band), :] = piece[i * band : (i + 1) * band, :].astype(F32)
    for v in range(3):
        for i in range(slots):
            shifted = pad[i, 8 + v - 1 : 8 + v - 1 + patches + 2 * cols, :]
            if v != 1:
                col = lax.broadcasted_iota(jnp.int32, shifted.shape, 0) % cols
                shifted = jnp.where(col == (0 if v == 0 else cols - 1), 0.0, shifted)
            moved[i] = shifted

        @pl.loop(0, 2 * slots)
        def _(j):
            q, i = j // slots, j % slots
            here = pl.ds(pl.multiple_of(j * band, 16), band)
            for u in range(3):
                at = pl.multiple_of(at_row(where, first + q) * band + u * cols, 8)
                t = u * 3 + v
                wide[here, t * group : (t + 1) * group] = moved[i, pl.ds(at, band), :].astype(BF16)

    keep = pltpu.make_async_copy(wide, spans, done)
    keep.start()
    if first:
        wait_all(copies)
    width = own.shape[1]
    chunk = 256
    patches = slots * band

    @pl.loop(0, width // chunk)
    def _(j):
        lanes = pl.ds(pl.multiple_of(j * chunk, chunk), chunk)
        terms = dot(wide[...], weight[:, :, :, lanes].reshape(-1, chunk))
        own[:, lanes] = terms[:patches]
        near[:, lanes] = terms[patches:].astype(BF16)

    keep.wait()


def stage_two(dims, where, own, near, cross, x, norms, l0, l1, l2, l3, hat_two, scale_two, low, hat, scale, pooled, weight, pairs):
    slots, rows, cols = dims
    fill(where, weight, (l0, l1, l2, l3))
    width = x.shape[1]
    act = own[...] + near[...].astype(F32) + cross[...].astype(F32)
    normed, root = center(act)
    hat_two[...] = normed
    scale_two[...] = root
    pre = normed * norms[2:3, :] + norms[3:4, :]
    low[...] = (pre * jax.nn.sigmoid(pre)).astype(BF16)
    normed, root = center(dot(low[...], weight[...].reshape(width, width)))
    hat[...] = normed
    scale[...] = root
    y = x[...].astype(F32) + (normed * norms[4:5, :] + norms[5:6, :])
    y = jnp.sum(y.reshape(slots * rows // 2, 2, cols, width), axis=1).reshape(-1, width)
    count = pooled.shape[0]
    for g in range(pairs.shape[0]):
        lanes = slice(g * 128, (g + 1) * 128)
        pairs[g] = y[:, lanes]
        pooled[:, lanes] = (
            0.25 * (pairs[g, pl.ds(0, count, stride=2), :] + pairs[g, pl.ds(1, count, stride=2), :])
        ).astype(BF16)


def read_copies(where, pieces, weight, sems):
    half = RING // 2
    pairs = []
    for k in range(RING):
        if k == half:
            rows = pieces[half].shape[0]
            pairs.append((pieces[half], weight.at[where[2 + k], pl.ds(0, rows)]))
            pairs.append((pieces[RING], weight.at[where[2 + k], pl.ds(rows, rows)]))
        else:
            pairs.append((pieces[k], weight.at[where[2 + k]]))
    return copies_of(pairs, sems)


def readout(slots, where, p0, p1, p2, p3, c0, c1, c2, c3, norms, *refs):
    pieces = refs[: RING + 1]
    o0, o1, o2, o3, low, own, near, far, weight, sems = refs[RING + 1 :]
    copies = read_copies(where, pieces, weight, sems)
    start_all(copies)
    count, width = p0.shape
    table = jnp.concatenate([p[...] for p in (p0, p1, p2, p3)], axis=0)
    line = lax.broadcasted_iota(jnp.int32, (count, width), 0)
    mask = jnp.where(line // (count // slots) < where[1], 1.0, 0.0)
    wait_all(copies)
    whole = weight[...].reshape(-1, width)
    logits = dot_t(table, whole) + norms[6:7, :]
    for q, (cot, out) in enumerate(((c0, o0), (c1, o1), (c2, o2), (c3, o3))):
        z = logits[q * count : (q + 1) * count]
        phi = 0.5 * (1.0 + lax.erf(z * 0.7071067811865476))
        out[...] = (z * phi * mask).astype(BF16)
        slope = phi + z * jnp.exp(-0.5 * z * z) * 0.3989422804014327
        low[q * count : (q + 1) * count, :] = (cot[...].astype(F32) * mask * slope).astype(BF16)
    back = dot(low[...], whole)
    own[...] = back[:count]
    near[0] = back[count : 2 * count].astype(BF16)
    far[...] = back[2 * count : 3 * count]
    near[1] = back[3 * count :].astype(BF16)


def readout_terms(where, low, p0, p1, p2, p3, upper, lower, out, terms):
    width = p0.shape[1]
    table = jnp.concatenate([p[...] for p in (p0, p1, p2, p3)], axis=0)
    terms[...] = t_dot(low[...], table).reshape(terms.shape)
    bias = jnp.sum(low[...].astype(F32), axis=0, keepdims=True)
    rows = terms.shape[1]
    for k in range(RING):
        out[k, :rows, :] = terms[where[2 + k]].astype(BF16)
        out[k, rows:, :] = jnp.broadcast_to(bias, (out.shape[1] - rows, width)).astype(BF16)
    upper[...] = out[RING // 2, : upper.shape[0]]
    lower[...] = out[RING // 2, upper.shape[0] :]


def read_end(term, a, b, out, bias):
    total = term[...].astype(F32) + a[...].astype(F32) + b[...].astype(F32)
    rows = out.shape[1]
    out[...] = total[:rows].T
    bias[...] = total[rows : rows + 8]


def conv_end(one, one_a, one_b, two, two_a, two_b, conv, last):
    taps = one.shape[0]
    conv[:taps] = one[...].astype(F32) + one_a[...].astype(F32) + one_b[...].astype(F32)
    total = two[...].astype(F32) + two_a[...].astype(F32) + two_b[...].astype(F32)
    conv[taps:] = total[:-1]
    last[...] = total[-1]


def first_end(where, term, a, b, grad, norm):
    total = term[...].astype(F32) + a[...].astype(F32) + b[...].astype(F32)
    rows, width = grad.shape
    for g in range(RING):
        for r in range(4):
            to, at = (g * 4 + r) * rows, (r * RING + g) * rows
            grad[:, to : to + rows] = total[:rows, at : at + rows]
    block = total[rows:]
    swapped, plain = [pltpu.roll(block, lax.rem(width - where[i], width), 1)[:, :rows] for i in (18, 19)]
    line = lax.broadcasted_iota(jnp.int32, swapped.shape, 0)
    norm[...] = jnp.where(line < 2, swapped, plain)


def spread(pairs, grad, dims):
    slots, rows, cols = dims
    count, width = grad.shape
    for g in range(pairs.shape[0]):
        lanes = slice(g * 128, (g + 1) * 128)
        pairs[g, pl.ds(0, count, stride=2), :] = grad[:, lanes]
        pairs[g, pl.ds(1, count, stride=2), :] = grad[:, lanes]
    half = slots * rows // 2
    both = jnp.concatenate([pairs[g] for g in range(pairs.shape[0])], axis=1)
    both = jnp.broadcast_to(both.reshape(half, 1, cols, width), (half, 2, cols, width))
    return both.reshape(-1, width) * 0.25


def back_norm(grad, normed, root, gain):
    weighted = grad * gain
    return root * (
        weighted
        - jnp.mean(weighted, axis=-1, keepdims=True)
        - normed * jnp.mean(weighted * normed, axis=-1, keepdims=True)
    )


def total_rows(value):
    return jnp.sum(value, axis=0, keepdims=True)


def stage_two_back(dims, where, own, near, cross, hat, scale, hat_two, scale_two, norms, weight, grad_three, grad_two, pool_sum, sums, pairs):
    width = hat.shape[1]
    grad = own[...] + near[...].astype(F32) + cross[...].astype(F32)
    pool_sum[...] = grad
    gy = spread(pairs, grad, dims)
    sums[...] = jnp.zeros_like(sums)
    sums[4:5, :] = total_rows(gy * hat[...])
    sums[5:6, :] = total_rows(gy)
    grad_three[...] = back_norm(gy, hat[...], scale[...], norms[4:5, :]).astype(BF16)
    gs = dot_t(grad_three[...], weight[...].reshape(width, width))
    pre = hat_two[...] * norms[2:3, :] + norms[3:4, :]
    gn = gs * silu_slope(pre)
    sums[2:3, :] = total_rows(gn * hat_two[...])
    sums[3:4, :] = total_rows(gn)
    grad_two[...] = back_norm(gn, hat_two[...], scale_two[...], norms[2:3, :]).astype(BF16)


def last_terms(where, low, grad, own, near, far, terms):
    terms[...] = t_dot(low[...], grad[...]).reshape(terms.shape)
    for k in range(RING):
        own[k] = terms[where[2 + k], at_row(where, 0)]
        near[0, k] = terms[where[2 + k], at_row(where, 1)].astype(BF16)
        far[k] = terms[where[2 + k], at_row(where, 2)]
        near[1, k] = terms[where[2 + k], at_row(where, 3)].astype(BF16)


def stack_grad(dims, where, pieces, whole):
    slots, rows, cols = dims
    band = rows * cols // 4
    for q, piece in enumerate(pieces):
        for i in range(slots):
            at = pl.multiple_of(i * rows * cols + at_row(where, q) * band, 16)
            whole[pl.ds(at, band), :] = piece[i * band : (i + 1) * band, :]


def conv_half_terms(where, here, g0, g1, out, one):
    count = g0.shape[0]
    one[:count], one[count:] = g0[...], g1[...]
    group = out.shape[1]

    @pl.loop(0, out.shape[0])
    def _(t):
        lanes = pl.ds(pl.multiple_of(t * group, group), group)
        out[t] = t_dot(here[:, lanes], one[...])


def conv_terms(first, number, where, half, there, g2, g3, *refs):
    parts, outs, (two, line) = refs[: -RING - 2], refs[-RING - 2 : -2], refs[-2:]
    count = g2.shape[0]
    two[:count], two[count:] = g2[...], g3[...]
    rows, width = outs[0].shape[1:]
    group = RING * rows

    @pl.loop(0, number)
    def _(t):
        lanes = pl.ds(pl.multiple_of((first + t) * group, group), group)
        terms = half[first + t] + t_dot(there[:, lanes], two[...])
        line[...] = terms.astype(BF16).reshape(RING, rows, width)
        for k in range(RING):
            outs[k][t] = line[where[2 + k]]

    if parts:
        own, near, low, high = parts
        for k in range(RING):
            cross = low[k] if k < RING // 2 else high[k - RING // 2]
            outs[k][number] = (own[k] + near[0, k].astype(F32) + cross.astype(F32)).astype(BF16)


def conv_back(dims, where, g0, g1, g2, g3, weight, o0, o1, o2, o3, whole, held, low):
    slots, rows, cols = dims
    stack_grad(dims, where, (g0, g1, g2, g3), whole)
    patches = rows * cols
    band = patches // 4
    group = o0.shape[1]
    width = whole.shape[1]
    held[...] = jnp.zeros_like(held)
    for u in range(3):
        for v in range(3):
            part = dot_t(whole[...], weight[u * 3 + v].reshape(group, width))
            for i in range(slots):
                held[v, i, 8 + u * cols : 8 + u * cols + patches, :] += part[i * patches : (i + 1) * patches]
    col = lax.broadcasted_iota(jnp.int32, (patches, group), 0) % cols
    for i in range(slots):
        value = held[1, i, 8 + cols : 8 + cols + patches, :]
        value += jnp.where(col == cols - 1, 0.0, held[0, i, 9 + cols : 9 + cols + patches, :])
        value += jnp.where(col == 0, 0.0, held[2, i, 7 + cols : 7 + cols + patches, :])
        low[i * patches : (i + 1) * patches, :] = value.astype(BF16)
    for q, out in enumerate((o0, o1, o2, o3)):
        for i in range(slots):
            at = pl.multiple_of(i * patches + at_row(where, q) * band, 16)
            out[i * band : (i + 1) * band, :] = low[pl.ds(at, band), :]


def stage_one_back(where, b0, b1, b2, b3, hat, scale, norms, x, sums, grad_one, own, near, far, low, terms):
    width = hat.shape[1]
    part = width // 4
    for q, piece in enumerate((b0, b1, b2, b3)):
        low[:, pl.ds(pl.multiple_of(at_row(where, q) * part, part), part)] = piece[...]
    pre = hat[...] * norms[0:1, :] + norms[1:2, :]
    gn = low[...].astype(F32) * silu_slope(pre)
    line = lax.broadcasted_iota(jnp.int32, (8, width), 0)
    tail = jnp.where(line == 0, total_rows(gn * hat[...]), jnp.where(line == 1, total_rows(gn), sums[...]))
    grad_one[...] = back_norm(gn, hat[...], scale[...], norms[0:1, :]).astype(BF16)
    terms[...] = t_dot(x[...], grad_one[...]).reshape(terms.shape)
    rows = terms.shape[2]
    for k in range(RING):
        to = where[2 + (k + 3) % RING]
        own[k, :rows] = terms[to, at_row(where, 0)]
        near[0, k, :rows] = terms[to, at_row(where, 1)].astype(BF16)
        far[k, :rows] = terms[to, at_row(where, 2)]
        near[1, k, :rows] = terms[to, at_row(where, 3)].astype(BF16)
        own[k, rows:] = tail
        near[0, k, rows:] = tail.astype(BF16)
        far[k, rows:] = tail
        near[1, k, rows:] = tail.astype(BF16)


def image_back(dims, where, grad_one, pool_sum, weight, out, pairs):
    width = grad_one.shape[1]
    gy = spread(pairs, pool_sum[...], dims)
    out[...] = (gy + dot_t(grad_one[...], weight[...].reshape(width, width))).astype(BF16)


def split_columns(where, x, o0, o1, o2, o3):
    lanes = x.shape[1] // (4 * RING)
    for q, out in enumerate((o0, o1, o2, o3)):
        for g in range(RING):
            at = pl.multiple_of((g * 4 + at_row(where, q)) * lanes, lanes)
            out[:, g * lanes : (g + 1) * lanes] = x[:, pl.ds(at, lanes)]


def join_columns(where, i0, i1, i2, i3, out):
    lanes = out.shape[1] // (4 * RING)
    for q, piece in enumerate((i0, i1, i2, i3)):
        for g in range(RING):
            at = pl.multiple_of((g * 4 + at_row(where, q)) * lanes, lanes)
            out[:, pl.ds(at, lanes)] = piece[:, g * lanes : (g + 1) * lanes]


def ringed(
    images,
    first_weight,
    conv_weight,
    last_weight,
    norm_rows,
    read_weight,
    read_bias,
    cotangent,
    live_count,
):
    dp, row = lax.axis_index("dp"), lax.axis_index("row")
    slots, band, cols, width = images.shape
    dims = (slots, band, cols)
    full = (slots, 4 * band, cols)
    patches = slots * band * cols
    count = patches // 4
    own = first_weight.shape[0]
    group = RING * own
    outs = read_weight.shape[1]
    taps = 9
    DMA = pltpu.SemaphoreType.DMA
    index = jnp.arange(20, dtype=jnp.int32)
    place_of = lambda d: jnp.where(d % 2 == 0, d // 2, RING - 1 - d // 2)
    place = (place_of(dp) + index - 2) % RING
    ahead = jnp.where(place < RING // 2, 2 * place, 2 * (RING - 1 - place) + 1)
    steps = (place_of(index - 10) - place_of(dp)) % RING
    where = jnp.where(index == 0, row, jnp.where(index == 1, live_count[0], jnp.where(index < 10, ahead, steps)))
    where = jnp.where(index == 18, (row * RING + dp) * own, jnp.where(index == 19, (dp * 4 + row) * own, where))
    where = where.astype(jnp.int32)

    first_mine = first_weight.reshape(own, RING, 4, own).transpose(0, 2, 1, 3).reshape(own, width)
    lane = jnp.arange(width, dtype=jnp.int32)[None, :]
    tiled = jnp.tile(norm_rows, (1, width // own))
    at = jnp.where(jnp.arange(6)[:, None] < 2, row * RING + dp, dp * 4 + row)
    small = jnp.where(lane // own == at, tiled, 0).astype(BF16)
    bias = jnp.where(lane // outs == dp, jnp.tile(read_bias, width // outs)[None, :], 0).astype(BF16)
    small = jnp.concatenate([small, bias, jnp.zeros((1, width), BF16)], axis=0)
    first_mine = jnp.concatenate([first_mine, small], axis=0)
    conv = conv_weight.reshape(taps, own, width)
    quarter = shape((count, width), BF16)
    wide_f32, thin_f32, wide_bf16 = (
        shape((patches, width), F32),
        shape((patches, 1), F32),
        shape((patches, width), BF16),
    )
    quarter_f32, near_quarter = shape((count, width), F32), shape((2, count, width), BF16)
    piece = shape((patches, group), BF16)
    block = (RING, own, width)
    matmul = 2 * patches * width * width
    square = 2 * width * width
    square_of = shape((RING, 4, own, width), BF16)
    total = 4 * patches
    pad_rows = full[1] * cols + 2 * cols + 16
    pair_scratch = pltpu.VMEM((width // 128, patches // 2, 128), F32)
    x = images.reshape(patches, width)

    far = RING // 2
    cut = own + 8
    low, high = lambda v: v[:own], lambda v: v[own:]
    more = gather_step(gather_state(conv), 1)
    ring = gather_step(gather_state(jnp.concatenate([last_weight, first_mine], axis=0)), 1)
    read = read_weight.T
    cots = cotangent.reshape(count, -1)
    bias_place = dp * outs
    more, ring, where, read, cots, x, bias_place = fence(more, ring, where, read, cots, x, bias_place)
    ring = gather_step(ring, 2)
    cots = kernel(split_columns, [quarter] * 4, [SM, VM], [], 0, 2 * count * 4 * width * 2, where, cots)
    ring, cots = fence(ring, cots)
    ring = gather_step(ring, 3)
    ring = fence(ring)[0]
    ring = gather_step(ring, 4, low, high)
    more, ring = fence(more, ring)
    ring = ring[0]
    firsts, lasts = kernel(
        line_up,
        [shape((RING, cut, width), BF16), shape((RING, own, width), BF16)],
        [SM] + [VM] * (RING + 1),
        [],
        0,
        4 * RING * (cut + own) * width,
        where,
        *flat_pieces(ring),
    )
    more = gather_step(more, 2)
    first_two, first_one = swap_row(firsts, 2), swap_row(firsts, 1)
    more, firsts, first_two, first_one, lasts = fence(more, firsts, first_two, first_one, lasts)
    more = gather_step(more, 3)
    firsts = [firsts, first_one, first_two, swap_row(first_two, 1)]
    last_two, last_one = swap_row(lasts, 2), swap_row(lasts, 1)
    hat_one, scale_one, *lows, norms, first_full = kernel(
        stage_one,
        [wide_f32, thin_f32] + [piece] * 4 + [shape((8, width), F32), square_of],
        [SM] + [VM] * 5,
        [pltpu.VMEM((patches, width), BF16)],
        matmul,
        square + 8 * patches * width,
        where,
        x,
        *firsts,
    )
    more, lows, lasts, last_two, last_one = fence(more, lows, lasts, last_two, last_one)
    taps_half = (taps + 1) // 2
    more = gather_step(more, 4, lambda v: v[:taps_half], lambda v: v[taps_half:])
    lows = exchange_row(lows)
    lasts = [lasts, last_one, last_two, swap_row(last_two, 1)]
    weights = flat_pieces(more[0])
    weights, lows, lasts, read, cots = fence(weights, lows, lasts, read, cots)

    conv_whole = (taps, RING, own, width)

    def conv_half(first, weights):
        return kernel(
            functools.partial(conv_forward, full, first),
            [wide_f32, wide_bf16, shape((2 * patches, taps * group), BF16)]
            + ([shape(conv_whole, BF16)] if first else []),
            [SM] + [VM] * 4 + ([HB] * (RING + 1) if first else [VM]),
            [
                pltpu.VMEM((slots, pad_rows, group), F32),
                pltpu.VMEM((slots, pad_rows - 16, group), F32),
                pltpu.VMEM((2 * patches, taps * group), BF16),
            ]
            + ([DMA((RING + 1,))] if first else [])
            + [DMA],
            9 * matmul // 2,
            9 * square + 6 * patches * width + 4 * patches * taps * group,
            where,
            *lows,
            *weights,
            specs=[VM, VM, HB] + ([VM] if first else []),
        )

    read = gather_step(gather_state(read), 1)
    cots = exchange_row(cots)
    away, near, spans_far, conv_full = conv_half(2, weights)
    away, near, read, cots = fence(away, near, read, cots)
    other = (away + swap_row(near, 1).astype(F32)).astype(BF16)
    other, lows, read = fence(other, lows, read)
    cross = swap_row(other, 2)
    read = gather_step(read, 2)
    mine, near, spans_near = conv_half(0, (conv_full,))
    near, read = fence(near, read)
    near = swap_row(near, 1)
    read = gather_step(read, 3)
    mine, near, cross, read = fence(mine, near, cross, read)
    read = gather_step(read, 4, lambda v: v[: outs // 2], lambda v: v[outs // 2 :])
    hat_two, scale_two, low_two, hat_three, scale_three, pooled, last_full = kernel(
        functools.partial(stage_two, dims),
        [wide_f32, thin_f32, wide_bf16, wide_f32, thin_f32, quarter, square_of],
        [SM] + [VM] * 9,
        [pair_scratch],
        matmul,
        square + 24 * patches * width,
        where,
        mine,
        near,
        cross,
        x,
        norms,
        *lasts,
    )
    pool_two, pool_one = swap_row(pooled, 2), swap_row(pooled, 1)
    pooled, pool_two, pool_one, read = fence(pooled, pool_two, pool_one, read)
    pools = [pooled, pool_one, pool_two, swap_row(pool_two, 1)]
    *shown, grad_low, mine, near, away = kernel(
        functools.partial(readout, slots),
        [quarter] * 4 + [wide_bf16, quarter_f32, near_quarter, quarter_f32],
        [SM] + [VM] * 9 + [HB] * (RING + 1),
        [pltpu.VMEM((RING, outs, width), BF16), DMA((RING + 1,))],
        2 * matmul,
        square + 12 * patches * width,
        where,
        *pools,
        *cots,
        norms,
        *flat_pieces(read[0]),
    )

    near = swap_row(near, 1)
    other = (away + near[1].astype(F32)).astype(BF16)
    other, grad_low, near = fence(other, grad_low, near)
    cross = swap_row(other, 2)
    half_read = shape(((outs + 16) // 2, width), BF16)
    *read_far, read_terms = kernel(
        readout_terms,
        [half_read, half_read, shape((RING, outs + 16, width), BF16)],
        [SM] + [VM] * 5,
        [pltpu.VMEM((RING, outs, width), F32)],
        matmul,
        2 * square,
        where,
        grad_low,
        *pools,
    )
    cross, read_far, read_terms, near = fence(cross, read_far, read_terms, near)
    read_a, read_b = scatter_step(*read_far, read_terms, None, None, 4)
    grad_three, grad_two, pool_sum, sums = kernel(
        functools.partial(stage_two_back, dims),
        [wide_bf16, wide_bf16, quarter_f32, shape((8, width), F32)],
        [SM] + [VM] * 9,
        [pair_scratch],
        matmul,
        square + 14 * patches * width,
        where,
        mine,
        near[0],
        cross,
        hat_three,
        scale_three,
        hat_two,
        scale_two,
        norms,
        last_full,
    )
    grad_three, grad_two, read_a, read_b = fence(grad_three, grad_two, read_a, read_b)
    grad_far, grad_next = swap_row(grad_two, 2), swap_row(grad_two, 1)
    read_a, read_b = scatter_step(*read_far, read_terms, read_a, read_b, 3)
    read_a, read_b = scatter_step(*read_far, read_terms, read_a, read_b, 2)
    here = kernel(
        conv_half_terms,
        shape((taps, group, width), F32),
        [SM] + [VM] * 3,
        [pltpu.VMEM((2 * patches, width), BF16)],
        9 * matmul // 2,
        18 * square,
        where,
        spans_near,
        grad_two,
        grad_next,
    )
    last_own, last_near, last_far = kernel(
        last_terms,
        [shape(block, F32), shape((2,) + block, BF16), shape(block, F32)],
        [SM, VM, VM],
        [pltpu.VMEM((RING, 4, own, width), F32)],
        matmul,
        3 * square,
        where,
        low_two,
        grad_three,
    )
    grad_two, grad_far, grad_next, last_near, last_far, read_a, read_b, here = fence(
        grad_two, grad_far, grad_next, last_near, last_far, read_a, read_b, here
    )
    grads = [grad_two, grad_next, grad_far, swap_row(grad_far, 1)]
    last_near = swap_row(last_near, 1)
    last_low = (last_far[:far] + last_near[1, :far].astype(F32)).astype(BF16)
    last_high = (last_far[far:] + last_near[1, far:].astype(F32)).astype(BF16)
    grads, last_near, last_low, last_high = fence(grads, last_near, last_low, last_high)
    last_low = swap_row(last_low, 2)
    read_a, read_b = scatter_step(*read_far, read_terms, read_a, read_b, 1)

    def weight_terms(first, number, parts):
        held = number + len(parts) // 4
        return kernel(
            functools.partial(conv_terms, first, number),
            [shape((held, own, width), BF16)] * RING,
            [SM] + [VM] * (4 + len(parts)),
            [pltpu.VMEM((2 * patches, width), BF16), pltpu.VMEM((RING, own, width), BF16)],
            matmul * number,
            2 * square * number,
            where,
            here,
            spans_far,
            *grads[2:],
            *parts,
        )

    def add_to(terms, k, value):
        return (terms[k % RING].astype(F32) + value.astype(F32)).astype(BF16)

    one = weight_terms(0, 5, ())
    one, grads, last_low, last_high, read_a, read_b = fence(
        one, grads, last_low, last_high, read_a, read_b
    )
    last_high = swap_row(last_high, 2)
    one_a, one_b = hop(one[far], True), hop(one[far + 1], False)
    backs = kernel(
        functools.partial(conv_back, full),
        [piece] * 4,
        [SM] + [VM] * 5,
        [
            pltpu.VMEM((total, width), BF16),
            pltpu.VMEM((3, slots, pad_rows, group), F32),
            pltpu.VMEM((total, group), BF16),
        ],
        9 * matmul,
        9 * square + 12 * patches * width,
        where,
        *grads,
        conv_full,
    )
    one_a, one_b, backs, grads, last_high = fence(one_a, one_b, backs, grads, last_high)
    one_a, one_b = hop(add_to(one, 3, one_a), True), hop(add_to(one, -2, one_b), False)
    backs = exchange_row(backs)
    two = weight_terms(5, 4, (last_own, last_near, last_low, last_high))
    one_a, one_b, two, backs = fence(one_a, one_b, two, backs)
    two_a, two_b = hop(two[far - 1], True), hop(two[far], False)
    one_a, one_b = add_to(one, 2, one_a), add_to(one, -1, one_b)
    block = (RING, own + 8, width)
    grad_one, first_own, first_near, first_far = kernel(
        stage_one_back,
        [wide_bf16, shape(block, F32), shape((2,) + block, BF16), shape(block, F32)],
        [SM] + [VM] * 9,
        [pltpu.VMEM((patches, width), BF16), pltpu.VMEM((RING, 4, own, width), F32)],
        matmul,
        3 * square + 8 * patches * width,
        where,
        *backs,
        hat_one,
        scale_one,
        norms,
        x,
        sums,
    )
    one_a, one_b, two_a, two_b, grad_one, first_own, first_near, first_far, shown = fence(
        one_a, one_b, two_a, two_b, grad_one, first_own, first_near, first_far, shown
    )
    one_a, one_b = hop(one_a, True), hop(one_b, False)
    two_a, two_b = add_to(two, 2, two_a), add_to(two, -3, two_b)
    first_near = swap_row(first_near, 1)
    shown = exchange_row(shown)
    first_low = (first_far[far:] + first_near[1, far:].astype(F32)).astype(BF16)
    first_high = (first_far[:far] + first_near[1, :far].astype(F32)).astype(BF16)
    one_a, one_b_end, two_a, two_b, first_near, first_low, first_high, shown = fence(
        one_a, one_b, two_a, two_b, first_near, first_low, first_high, shown
    )
    two_a, two_b = hop(two_a, True), hop(two_b, False)
    one_a = add_to(one, 1, one_a)
    first_high = swap_row(first_high, 2)
    image_grad = kernel(
        functools.partial(image_back, dims),
        wide_bf16,
        [SM, VM, VM, VM],
        [pair_scratch],
        matmul,
        square + 8 * patches * width,
        where,
        grad_one,
        pool_sum,
        first_full,
    ).reshape(slots, band, cols, width)
    one_a, two_a, two_b, first_low, first_high, image_grad = fence(
        one_a, two_a, two_b, first_low, first_high, image_grad
    )
    one_a, two_b = hop(one_a, True), hop(add_to(two, -2, two_b), False)
    first_high = (first_own[:far] + first_near[0, :far].astype(F32) + first_high.astype(F32)).astype(BF16)
    first_low = swap_row(first_low, 2)
    first_a, first_b, far_a = hop(first_high[0], True), hop(first_high[2], False), hop(first_high[1], True, 2)
    two_a = add_to(two, 1, two_a)
    read_grad, bias_rows = kernel(
        read_end,
        [shape((width, outs), F32), shape((8, width), F32)],
        [VM] * 3,
        [],
        0,
        10 * width * outs,
        read_terms[0],
        read_a,
        read_b,
    )
    one_a, two_a, two_b, first_low, first_high, first_a, first_b, far_a, shown, read_grad = fence(
        one_a, two_a, two_b, first_low, first_high, first_a, first_b, far_a, shown, read_grad
    )
    first_low = (first_own[far:] + first_near[0, far:].astype(F32) + first_low.astype(F32)).astype(BF16)
    first_a = (first_low[3].astype(F32) + first_a.astype(F32) + far_a.astype(F32)).astype(BF16)
    first_a, first_b = hop(first_a, True), hop(add_to(first_high, 3, first_b), False)
    two_a, two_b = hop(two_a, True), hop(add_to(two, -1, two_b), False)
    readout_out = kernel(
        join_columns,
        shape((count, 4 * width), BF16),
        [SM] + [VM] * 4,
        [],
        0,
        16 * count * width,
        where,
        *shown,
    ).reshape(slots, band // 2, cols // 2, 4 * width)
    two_a, two_b, first_a, first_b, first_low, readout_out = fence(
        two_a, two_b, first_a, first_b, first_low, readout_out
    )
    first_a, first_b = hop(add_to(first_low, 2, first_a), True), hop(add_to(first_low, 0, first_b), False)
    bias_grad = lax.dynamic_slice(bias_rows, (0, bias_place), (1, outs), allow_negative_indices=False)[0]
    conv_grad, last_grad = kernel(
        conv_end,
        [shape((taps, own, width), F32), shape((own, width), F32)],
        [VM] * 6,
        [],
        0,
        10 * (taps + 1) * own * width,
        one[0],
        one_a,
        one_b_end,
        two[0],
        two_a,
        two_b,
    )
    conv_grad = conv_grad.reshape(3, 3, own, width)
    first_grad, norm_grad = kernel(
        first_end,
        [shape((own, width), F32), shape((8, own), F32)],
        [SM] + [VM] * 3,
        [],
        0,
        10 * own * width,
        where,
        first_low[1],
        first_a,
        first_b,
    )
    norm_grad = norm_grad[:6]
    return (
        readout_out,
        image_grad,
        first_grad,
        conv_grad,
        last_grad,
        norm_grad,
        read_grad,
        bias_grad,
    )


def per_device(*arrays):
    if lax.axis_size("dp") == RING and lax.axis_size("row") == 4:
        return ringed(*arrays)
    return generic(*arrays)


def solution(mesh):
    return jax.shard_map(
        per_device,
        mesh=mesh,
        in_specs=(
            P("dp", "row", None, None),
            P(("dp", "row"), None),
            P(None, None, ("dp", "row"), None),
            P(("dp", "row"), None),
            P(None, ("dp", "row")),
            P(None, ("dp", "row")),
            P(("dp", "row")),
            P("dp", "row", None, None),
            P("dp"),
        ),
        out_specs=(
            P("dp", "row", None, None),
            P("dp", "row", None, None),
            P(("dp", "row"), None),
            P(None, None, ("dp", "row"), None),
            P(("dp", "row"), None),
            P(None, ("dp", "row")),
            P(None, ("dp", "row")),
            P(("dp", "row")),
        ),
        check_vma=False,
    )
```
